32 devices in a mesh: grp: 1, ev: 32 (over z, y, x, core).
Axes of the slice: x: 2, y: 2, z: 4, core: 2. Of those that a mesh axis runs over, the one named last changes fastest.
Arguments:
- windows: bfloat16 [256, 3, 64, 1024], P(('grp', 'ev')), may hold values from -400 to 400, as said below
- rotation: bfloat16 [256, 3, 64], P(('grp', 'ev')), may hold values from -3 to 3
- source_inverse: bfloat16 [256, 1024], P(('grp', 'ev')), may hold values from -3.4 to 3.4
- send_rows: int32 [1024, 64], P(('grp', 'ev')), may hold values from 0 to 511, as said below
- tile_station: int32 [2048], P(('grp', 'ev')), may hold values from 0 to 63, as said below
- tile_count: int32 [2048], P(('grp', 'ev')), may hold values from 16 to 128
- pair_rows: int32 [2, 262144], P(None, ('grp', 'ev')), may hold values from 0 to 2047, as said below
Outputs:
- correlation: float32 [262144, 255], P(('grp', 'ev'))
The draws below stay inside these ranges and needn't reach their ends.
Inputs may be any that keep to these rules, and one draw needn't show every extreme that they name: Each event's windows carry a scale of their own, and each station's another. `send_rows`: row j of the block of device o names the rows of device o sent to device j, each as local event times 64 plus station, with the station of the tile whose residue matches the receiving slot (o * 64 + k) mod 64. `tile_station`: tile t of a device is fed by received slots r with r mod 64 = t mod 64, all at the tile's station. `pair_rows`: entries count the rows a device receives by sending device then slot; both members of a slot lie at its tile's station.
All inputs are finite; a program needn't handle non-finite values.
Results may differ from the reference program's by a relative error of at most 0.007.
Values may be sent and summed in bfloat16 or wider, within the bound.
No kernel may reach another device: no remote copies, remote signals or barrier semaphores. Data moves between devices by JAX's collectives and lax.ppermute only.
A program may use at most 64 MiB of HBM per device.

```python
import math
from functools import partial
import jax
import jax.numpy as jnp
from jax import lax

NS = 1024
LAGS = 255
STA = 64
TILE_PAIRS = 128
EV_DEV = 8
TILES_DEV = 64
SLOTS_DEV = 2048
PEERS = 32
EVENTS = 256
TILES = 2048
PAIRS_DEV = 8192
PAIRS = 262144
CAP = 64


def route_tables(key):
    base_key = jax.random.fold_in(key, 501)
    capacity = SLOTS_DEV // PEERS
    stations = jax.random.randint(jax.random.fold_in(base_key, 1), (PEERS, TILES_DEV), 0, STA)
    stations = stations.at[0, 0].set(STA - 1)
    stations = stations.at[1, 0].set(0)
    source = jnp.arange(PEERS, dtype=jnp.int32)[:, None, None]
    slot_index = jnp.arange(capacity, dtype=jnp.int32)[None, None, :]
    column = (source * capacity + slot_index) % TILES_DEV
    target = jnp.arange(PEERS, dtype=jnp.int32)[None, :, None]
    station_ids = stations[target, column]
    event_ids = jax.random.randint(jax.random.fold_in(base_key, 2), (PEERS, PEERS, capacity), 0, EV_DEV)
    event_ids = event_ids.at[0, 0, 0].set(EV_DEV - 1)
    event_ids = event_ids.at[0, 1, 0].set(0)
    send_table = (event_ids * STA + station_ids).reshape(PEERS * PEERS, capacity).astype(jnp.int32)
    picked = jax.random.randint(jax.random.fold_in(base_key, 3), (2, PEERS, TILES_DEV, TILE_PAIRS), 0, SLOTS_DEV // TILES_DEV)
    tile_ids = jnp.arange(TILES_DEV, dtype=jnp.int32)[None, None, :, None]
    pair_slots = tile_ids + TILES_DEV * picked
    pair_slots = pair_slots.at[0, :, 0, 0].set(0)
    pair_slots = pair_slots.at[1, :, TILES_DEV - 1, 0].set(SLOTS_DEV - 1)
    return (stations.reshape(TILES).astype(jnp.int32), send_table, pair_slots.reshape(2, PAIRS).astype(jnp.int32))


def draw_send_rows(key, part):
    return route_tables(key)[1]


def draw_tile_station(key, part):
    return route_tables(key)[0]


def draw_pair_rows(key, part):
    return route_tables(key)[2]


def draw_windows(key, part):
    base_key = jax.random.fold_in(key, 11)
    gauss_part = jnp.clip(jax.random.normal(jax.random.fold_in(base_key, 1), (EVENTS, 3, STA, NS), jnp.float32), -5.0, 5.0)
    position = jnp.arange(EVENTS, dtype=jnp.float32) / max(EVENTS - 1, 1)
    station_gain = jnp.exp(jax.random.uniform(jax.random.fold_in(base_key, 2), (STA,), jnp.float32, 0.0, 1.1))
    growth = jnp.sqrt(1.0 + 2.0 * position)
    spread = jnp.exp(jax.random.uniform(jax.random.fold_in(base_key, 3), (EVENTS,), jnp.float32, 0.0, 1.15))
    amplitude = (growth * spread)[:, None, None, None] * station_gain[None, None, :, None]
    return (gauss_part * amplitude).astype(jnp.bfloat16)


def draw_source_inverse(key, part):
    base_key = jax.random.fold_in(key, 23)
    magnitude = jnp.exp(jax.random.uniform(jax.random.fold_in(base_key, 1), (EVENTS, NS // 2), jnp.float32, -0.7, 0.7))
    angles = jax.random.uniform(jax.random.fold_in(base_key, 2), (EVENTS, NS // 2), jnp.float32, -math.pi, math.pi)
    return jnp.concatenate([magnitude * jnp.cos(angles), magnitude * jnp.sin(angles)], axis=1).astype(jnp.bfloat16)


def set_ends(values, stream_key, least, largest):
    longest = values.shape.index(max(values.shape))
    spots = []
    for shift in (0, 1):
        where = [jax.random.randint(jax.random.fold_in(stream_key, axis), (), 0, length) for axis, length in enumerate(values.shape)]
        where[longest] = (where[longest] + shift) % values.shape[longest]
        spots.append(tuple(where))
    return values.at[spots[0]].set(least).at[spots[1]].set(largest)


def levels(stream_key, shape, cuts, least, top_value):
    level = 1.0
    for dim, shards_of in cuts:
        steps = jax.random.uniform(jax.random.fold_in(jax.random.fold_in(stream_key, 6), dim), (shards_of,), jnp.float32, least / len(cuts), top_value / len(cuts))
        level = level * jnp.repeat(jnp.exp(steps), shape[dim] // shards_of).reshape((-1,) + (1,) * (len(shape) - 1 - dim))
    return level


def bell_draw(own_key, extent, deviation, bound, split=(), held_as=jnp.bfloat16):
    loudness = levels(own_key, extent, split, -0.22, 0.18) if split else 1.0
    drawn = jax.random.normal(own_key, extent, jnp.float32) * deviation * loudness
    return jnp.minimum(jnp.maximum(drawn, -bound), bound).astype(held_as)


def setup_inputs(seed: int = 0, part: int = 0) -> dict:
    arg_keys = jax.random.split(jax.random.key(seed), 8)
    part_keys = jax.random.split(jax.random.fold_in(arg_keys[7], part), 8)
    windows = draw_windows(jax.random.fold_in(jax.random.fold_in(arg_keys[7], part), 71), part)
    rotation = bell_draw(part_keys[1], (EVENTS, 3, STA), 0.6, 3.0, ((0, 32),))
    source_inverse = draw_source_inverse(jax.random.fold_in(jax.random.fold_in(arg_keys[7], part), 71), part)
    send_rows = draw_send_rows(jax.random.fold_in(jax.random.fold_in(arg_keys[7], part), 71), part)
    tile_station = draw_tile_station(jax.random.fold_in(jax.random.fold_in(arg_keys[7], part), 71), part)
    tile_count = set_ends(jax.random.randint(part_keys[5], (TILES,), TILE_PAIRS // 8, TILE_PAIRS + 1), jax.random.fold_in(part_keys[5], 1), TILE_PAIRS // 8, TILE_PAIRS).astype(jnp.int32)
    pair_rows = draw_pair_rows(jax.random.fold_in(jax.random.fold_in(arg_keys[7], part), 71), part)
    return {"windows": windows, "rotation": rotation, "source_inverse": source_inverse, "send_rows": send_rows, "tile_station": tile_station, "tile_count": tile_count, "pair_rows": pair_rows}


epsilon = 1e-06

def spectral_table(length):
    half_len = length // 2
    samples = jnp.arange(length, dtype=jnp.int32)[:, None]
    frequency = jnp.arange(half_len, dtype=jnp.int32)[None, :]
    angles = (samples * frequency % length).astype(jnp.float32) * (2.0 * math.pi / length)
    factor = 1.0 / math.sqrt(length)
    return jnp.concatenate([jnp.cos(angles) * factor, -jnp.sin(angles) * factor], axis=1).astype(jnp.bfloat16)

def lag_table(length, lag_count):
    half_len = length // 2
    frequency = jnp.arange(half_len, dtype=jnp.int32)[:, None]
    shifts = jnp.arange(lag_count, dtype=jnp.int32)[None, :] - lag_count // 2
    angles = (frequency * shifts % length).astype(jnp.float32) * (2.0 * math.pi / length)
    factor = 1.0 / math.sqrt(half_len)
    return jnp.concatenate([jnp.cos(angles) * factor, -jnp.sin(angles) * factor], axis=0).astype(jnp.bfloat16)

def event_spectra(windows, rotation, source_inverse, dft_table):
    half_len = dft_table.shape[1] // 2
    transverse = lax.optimization_barrier(jnp.sum(rotation.astype(jnp.float32)[..., None] * windows.astype(jnp.float32), axis=1)).astype(jnp.bfloat16)
    events, stations, length = transverse.shape
    spectrum = jnp.dot(transverse.reshape(events * stations, length), dft_table, preferred_element_type=jnp.float32)
    spectrum = spectrum.reshape(events, stations, length)
    filter_gain = source_inverse.astype(jnp.float32)[:, None, :]
    real_in, imag_in = (spectrum[..., :half_len], spectrum[..., half_len:])
    real_gain, imag_gain = (filter_gain[..., :half_len], filter_gain[..., half_len:])
    return jnp.concatenate([real_in * real_gain - imag_in * imag_gain, real_in * imag_gain + imag_in * real_gain], axis=-1)

def correlate_group(spectra, lag_tab, tile_pairs, pieces):
    first_rows, second_rows, weights, counts = pieces
    half_len = spectra.shape[1] // 2
    first_spec = spectra[first_rows].astype(jnp.float32)
    second_spec = spectra[second_rows].astype(jnp.float32)
    first_re, first_im = (first_spec[:, :half_len], first_spec[:, half_len:])
    second_re, second_im = (second_spec[:, :half_len], second_spec[:, half_len:])
    row_weight = jnp.repeat(weights, tile_pairs, axis=0)
    cross_spec = jnp.concatenate([(first_re * second_re + first_im * second_im) * row_weight, (first_im * second_re - first_re * second_im) * row_weight], axis=1).astype(jnp.bfloat16)
    lagged = jnp.dot(cross_spec, lag_tab, preferred_element_type=jnp.float32)
    live_rows = jnp.arange(lagged.shape[0], dtype=jnp.int32) % tile_pairs < jnp.repeat(counts, tile_pairs)
    return jnp.where(live_rows[:, None], lagged, jnp.zeros_like(lagged))

def reference(windows, rotation, source_inverse, send_rows, tile_station, tile_count, pair_rows):
    events, components, stations, length = windows.shape
    half_len = length // 2
    dft_table = spectral_table(length)

    def per_owner(pieces):
        deconvolved = event_spectra(pieces[0], pieces[1], pieces[2], dft_table)
        power_part = lax.optimization_barrier(jnp.sum(deconvolved[..., :half_len] ** 2 + deconvolved[..., half_len:] ** 2, axis=0))
        return (deconvolved.astype(jnp.bfloat16), power_part)
    shaped = (windows.reshape(PEERS, EV_DEV, components, stations, length), rotation.reshape(PEERS, EV_DEV, components, stations), source_inverse.reshape(PEERS, EV_DEV, length))
    spectra, powers = lax.map(per_owner, shaped)
    power_sum = lax.optimization_barrier(jnp.sum(powers, axis=0))
    weight = 1.0 / (power_sum / events + epsilon)
    spectra = spectra.reshape(events * stations, length)
    pair_total = pair_rows.shape[1]
    device = jnp.arange(pair_total, dtype=jnp.int32) // PAIRS_DEV
    source = pair_rows // CAP
    slot_index = pair_rows % CAP
    local_row = send_rows[source * PEERS + device[None, :], slot_index]
    row_ids = (source * (EV_DEV * stations) + local_row).astype(jnp.int32)
    onehot = (tile_station[:, None] == jnp.arange(stations, dtype=jnp.int32)[None, :]).astype(jnp.float32)
    tile_weight = jnp.dot(onehot, weight, precision=lax.Precision.HIGHEST)
    groups = tile_station.shape[0] // 4
    group_rows = 4 * TILE_PAIRS
    correlate = partial(correlate_group, spectra, lag_table(length, LAGS), TILE_PAIRS)
    result = lax.map(correlate, (row_ids[0].reshape(groups, group_rows), row_ids[1].reshape(groups, group_rows), tile_weight.reshape(groups, 4, half_len), tile_count.reshape(groups, 4)))
    return result.reshape(pair_total, LAGS)
```

```python
from functools import partial
import math

import jax
import jax.numpy as jnp
import numpy as np
from jax import lax
from jax.experimental import pallas as pl
from jax.experimental.pallas import tpu as pltpu
from jax.sharding import PartitionSpec as P

LAGS = 255
SUB = 8
LANES = 128
CHUNKS = 4

epsilon = 1e-06
F32 = jnp.float32
BF16 = jnp.bfloat16


def spectral_table(length):
    half_len = length // 2
    samples = np.arange(length)[:, None]
    frequency = np.arange(half_len)[None, :]
    angles = (samples * frequency % length) * (2.0 * math.pi / length)
    factor = 1.0 / math.sqrt(length)
    table = np.concatenate([np.cos(angles) * factor, -np.sin(angles) * factor], axis=1)
    return jnp.asarray(table.astype(np.float32)).astype(BF16)


def lag_table(length, lag_count, width):
    half_len = length // 2
    frequency = np.arange(half_len)[:, None]
    shifts = np.arange(lag_count)[None, :] - lag_count // 2
    angles = (frequency * shifts % length) * (2.0 * math.pi / length)
    factor = 1.0 / math.sqrt(half_len)
    table = np.concatenate([np.cos(angles) * factor, -np.sin(angles) * factor], axis=0)
    table = np.pad(table, ((0, 0), (0, width - lag_count)))
    return jnp.asarray(table.astype(np.float32)).astype(BF16)


def column(values):
    return jnp.transpose(jnp.broadcast_to(values, (LANES, LANES)))


def one_hot(values, width):
    down = column(values)
    lane = lax.broadcasted_iota(jnp.int32, (LANES, LANES), 1)
    parts = [
        jnp.where(down == lane + LANES * j, 1.0, 0.0).astype(BF16) for j in range(width // LANES)
    ]
    return jnp.concatenate(parts, axis=1)


def front_kernel(steps, win_ref, rot_ref, inv_ref, table_ref, index_ref, *refs):
    *send_refs, power_ref, rows_ref = refs
    step = pl.program_id(0)
    events, comps, stations, length = win_ref.shape
    half_len = length // 2
    blocks = []
    for e in range(events):
        rot = jnp.transpose(rot_ref[e].astype(F32))
        total = rot[:, 0:1] * win_ref[e, 0].astype(F32)
        for c in range(1, comps):
            total += rot[:, c : c + 1] * win_ref[e, c].astype(F32)
        blocks.append(total.astype(BF16))
    transverse = jnp.concatenate(blocks, axis=0)
    spectrum = jnp.dot(transverse, table_ref[...], preferred_element_type=F32)
    power = jnp.zeros((stations, half_len), F32)
    for e in range(events):
        re_in = spectrum[e * stations : (e + 1) * stations, :half_len]
        im_in = spectrum[e * stations : (e + 1) * stations, half_len:]
        gain = inv_ref[0, e : e + 1, :].astype(F32)
        re_g, im_g = gain[:, :half_len], gain[:, half_len:]
        re = re_in * re_g - im_in * im_g
        im = re_in * im_g + im_in * re_g
        power += re * re + im * im
        base = pl.multiple_of((step * events + e) * stations, stations)
        rows_ref[pl.ds(base, stations), :half_len] = re.astype(BF16)
        rows_ref[pl.ds(base, stations), half_len:] = im.astype(BF16)

    @pl.when(step == 0)
    def _():
        power_ref[...] = power

    @pl.when(step > 0)
    def _():
        power_ref[...] += power

    @pl.when(step == steps - 1)
    def _():
        rows = rows_ref[...]
        line = 0
        for ref in send_refs:
            for j in range(ref.shape[0] // LANES):
                pick = one_hot(index_ref[line : line + 1, :], rows.shape[0])
                picked = jnp.dot(pick, rows, preferred_element_type=F32)
                ref[j * LANES : (j + 1) * LANES, :] = picked.astype(BF16)
                line += 1


def front(windows, rotation, source_inverse, index, table, chunks):
    ev_dev, comps, stations, length = windows.shape
    steps = 2 if ev_dev % 2 == 0 else 1
    events = ev_dev // steps
    lines = index.shape[0]
    rows_c = lines * LANES // chunks
    whole = lambda *shape: pl.BlockSpec(shape, lambda i: (0,) * len(shape))
    return pl.pallas_call(
        partial(front_kernel, steps),
        grid=(steps,),
        in_specs=[
            pl.BlockSpec((events, comps, stations, length), lambda i: (i, 0, 0, 0)),
            pl.BlockSpec((events, comps, stations), lambda i: (i, 0, 0)),
            pl.BlockSpec((1, events, length), lambda i: (i, 0, 0)),
            whole(length, length),
            whole(lines, LANES),
        ],
        out_specs=[whole(rows_c, length)] * chunks + [whole(stations, length // 2)],
        out_shape=[jax.ShapeDtypeStruct((rows_c, length), BF16)] * chunks
        + [jax.ShapeDtypeStruct((stations, length // 2), F32)],
        scratch_shapes=[pltpu.VMEM((ev_dev * stations, length), BF16)],
        compiler_params=pltpu.CompilerParams(vmem_limit_bytes=48 << 20),
        name="front",
    )(windows, rotation, source_inverse.reshape(steps, events, length), table, index)


def pair_kernel(geo, first, station_ref, count_ref, pair_ref, got_ref, weight_ref, lag_ref, *refs):
    out_ref = refs[-1]
    owners, cap, joint = geo
    group = pl.program_id(0) + first
    length = got_ref.shape[-1]
    half_len = length // 2
    rows = got_ref[...].reshape(owners * SUB, length)
    width = owners * SUB
    for j in range(joint):
        for i in range(SUB):
            tile = j * cap + group * SUB + i
            picks = []
            for m in range(2):
                r = pair_ref[m, j, i : i + 1, :]
                place = lax.div(r, cap) * SUB + lax.rem(r, SUB)
                picks.append(one_hot(place, width))
            members = jnp.dot(jnp.concatenate(picks, axis=0), rows, preferred_element_type=F32)
            a, b = members[:LANES], members[LANES:]
            re_a, im_a = a[:, :half_len], a[:, half_len:]
            re_b, im_b = b[:, :half_len], b[:, half_len:]
            scale = weight_ref[pl.ds(station_ref[tile], 1), :]
            cross = jnp.concatenate(
                [
                    ((re_a * re_b + im_a * im_b) * scale).astype(BF16),
                    ((im_a * re_b - re_a * im_b) * scale).astype(BF16),
                ],
                axis=1,
            )
            lagged = jnp.dot(cross, lag_ref[...], preferred_element_type=F32)
            slot = lax.broadcasted_iota(jnp.int32, lagged.shape, 0)
            lagged = jnp.where(slot < count_ref[tile], lagged, 0.0)
            out_ref[j, i * LANES : (i + 1) * LANES, :] = lagged[:, :LAGS]


def correlate(chunk, chunks, geo, stations_of, counts, pairs, received, weight, lag_tab, previous):
    owners, cap, joint = geo
    groups = cap // SUB
    steps = groups // chunks
    first = chunk * steps
    length = received.shape[-1]
    stations = weight.shape[0]
    in_specs = [
        pl.BlockSpec((2, joint, SUB, LANES), lambda i, *_: (0, 0, i + first, 0)),
        pl.BlockSpec((owners, SUB, length), lambda i, *_: (0, i, 0)),
        pl.BlockSpec((stations, length // 2), lambda i, *_: (0, 0)),
        pl.BlockSpec(lag_tab.shape, lambda i, *_: (0, 0)),
    ]
    args = [pairs, received, weight, lag_tab]
    aliases = {}
    if previous is not None:
        in_specs.append(pl.BlockSpec(memory_space=pl.ANY))
        args.append(previous)
        aliases = {6: 0}
    return pl.pallas_call(
        partial(pair_kernel, geo, first),
        grid_spec=pltpu.PrefetchScalarGridSpec(
            num_scalar_prefetch=2,
            grid=(steps,),
            in_specs=in_specs,
            out_specs=pl.BlockSpec((joint, SUB * LANES, LAGS), lambda i, *_: (0, i + first, 0)),
        ),
        out_shape=jax.ShapeDtypeStruct((joint, cap * LANES, LAGS), F32),
        input_output_aliases=aliases,
        compiler_params=pltpu.CompilerParams(vmem_limit_bytes=48 << 20),
        name="pairs",
    )(stations_of, counts, *args)


def power_total(power, owners):
    stations, half_len = power.shape
    share = stations // owners
    parts = power.reshape(owners, share, half_len)
    mine = lax.all_to_all(parts, "ev", split_axis=0, concat_axis=0, tiled=True)
    mine = jnp.sum(mine, axis=0)
    every = jnp.broadcast_to(mine[None], (owners, share, half_len))
    every = lax.all_to_all(every, "ev", split_axis=0, concat_axis=0, tiled=True)
    return every.reshape(stations, half_len)


def shards(windows, rotation, source_inverse, send_rows, tile_station, tile_count, pair_rows):
    ev_dev, comps, stations, length = windows.shape
    owners = lax.axis_size("ev")
    cap = send_rows.shape[1]
    tiles_dev = tile_station.shape[0]
    joint = tiles_dev // cap
    geo = (owners, cap, joint)
    chunks = CHUNKS
    index = send_rows.reshape(owners, chunks, cap // chunks).swapaxes(0, 1).reshape(-1, LANES)
    *sends, power = front(
        windows, rotation, source_inverse, index, spectral_table(length), chunks
    )
    power_sum = power_total(power, owners)
    weight = 1.0 / (power_sum / (ev_dev * owners) + epsilon)
    pairs = pair_rows.reshape(2, joint, cap, LANES)
    lag_tab = lag_table(length, LAGS, LAGS + 1)
    result = None
    for chunk, send in enumerate(sends):
        got = lax.all_to_all(
            send.reshape(owners, cap // chunks, length), "ev", split_axis=0, concat_axis=0, tiled=True
        )
        result = correlate(
            chunk, chunks, geo, tile_station, tile_count, pairs, got, weight, lag_tab, result
        )
    return result.reshape(tiles_dev * LANES, LAGS)


def solution(mesh):
    in_specs = (
        P(("grp", "ev"), None, None, None),
        P(("grp", "ev"), None, None),
        P(("grp", "ev"), None),
        P(("grp", "ev"), None),
        P(("grp", "ev")),
        P(("grp", "ev")),
        P(None, ("grp", "ev")),
    )
    out_specs = P(("grp", "ev"), None)
    return jax.shard_map(shards, mesh=mesh, in_specs=in_specs, out_specs=out_specs, check_vma=False)
```

```python
from functools import partial
import math

import jax
import jax.numpy as jnp
import numpy as np
from jax import lax
from jax.experimental import pallas as pl
from jax.experimental.pallas import tpu as pltpu
from jax.sharding import PartitionSpec as P

LAGS = 255
SUB = 8
LANES = 128
CHUNKS = 2

epsilon = 1e-06
F32 = jnp.float32
BF16 = jnp.bfloat16


def spectral_table(length):
    half_len = length // 2
    samples = np.arange(length)[:, None]
    frequency = np.arange(half_len)[None, :]
    angles = (samples * frequency % length) * (2.0 * math.pi / length)
    factor = 1.0 / math.sqrt(length)
    table = np.concatenate([np.cos(angles) * factor, -np.sin(angles) * factor], axis=1)
    return jnp.asarray(table.astype(np.float32)).astype(BF16)


def lag_table(length, lag_count, width):
    half_len = length // 2
    frequency = np.arange(half_len)[:, None]
    shifts = np.arange(lag_count)[None, :] - lag_count // 2
    angles = (frequency * shifts % length) * (2.0 * math.pi / length)
    factor = 1.0 / math.sqrt(half_len)
    table = np.concatenate([np.cos(angles) * factor, -np.sin(angles) * factor], axis=0)
    table = np.pad(table, ((0, 0), (0, width - lag_count)))
    return jnp.asarray(table.astype(np.float32)).astype(BF16)


def column(values):
    return jnp.transpose(jnp.broadcast_to(values, (LANES, LANES)))


def one_hot(values, width):
    down = column(values)
    lane = lax.broadcasted_iota(jnp.int32, (LANES, LANES), 1)
    parts = [
        jnp.where(down == lane + LANES * j, 1.0, 0.0).astype(BF16) for j in range(width // LANES)
    ]
    return jnp.concatenate(parts, axis=1)


def split_high(values):
    high = values.astype(BF16)
    rest = (values - high.astype(F32)).astype(BF16)
    return jnp.concatenate([high, rest], axis=-1)


def join_high(values):
    width = values.shape[-1] // 2
    return values[..., :width].astype(F32) + values[..., width:].astype(F32)


def spectra_kernel(steps, half_ref, win_ref, rot_ref, inv_ref, table_ref, index_ref, rows_ref, power_ref):
    step = pl.program_id(0)
    events, comps, stations, length = win_ref.shape
    half_len = length // 2
    blocks = []
    turns = rot_ref[...].astype(F32)
    for e in range(events):
        turn = turns[:, e, :]
        for s in range(1, steps):
            turn = jnp.where(step == s, turns[:, s * events + e, :], turn)
        rot = jnp.transpose(turn)
        total = rot[:, 0:1] * win_ref[e, 0].astype(F32)
        for c in range(1, comps):
            total += rot[:, c : c + 1] * win_ref[e, c].astype(F32)
        blocks.append(total.astype(BF16))
    transverse = jnp.concatenate(blocks, axis=0)
    spectrum = jnp.dot(transverse, table_ref[...], preferred_element_type=F32)
    gains = inv_ref[...].astype(F32)
    power = jnp.zeros((stations, half_len), F32)
    for e in range(events):
        re_in = spectrum[e * stations : (e + 1) * stations, :half_len]
        im_in = spectrum[e * stations : (e + 1) * stations, half_len:]
        gain = gains[e : e + 1, :]
        for s in range(1, steps):
            gain = jnp.where(step == s, gains[s * events + e : s * events + e + 1, :], gain)
        re_g, im_g = gain[:, :half_len], gain[:, half_len:]
        re = re_in * re_g - im_in * im_g
        im = re_in * im_g + im_in * re_g
        power += re * re + im * im
        base = pl.multiple_of((step * events + e) * stations, stations)
        rows_ref[pl.ds(base, stations), :half_len] = re.astype(BF16)
        rows_ref[pl.ds(base, stations), half_len:] = im.astype(BF16)

    @pl.when(step == 0)
    def _():
        power_ref[...] = power
        owners, cap = index_ref.shape
        peers = owners // 2
        other = pl.multiple_of((1 - half_ref[0]) * peers, peers)
        wanted = index_ref[pl.ds(other, peers), :]
        tail = rows_ref.shape[0] - peers
        rows_ref[tail:, :] = jnp.zeros((peers, length), BF16)
        rows_ref[tail:, :cap] = (wanted // LANES).astype(F32).astype(BF16)
        rows_ref[tail:, LANES : LANES + cap] = (wanted % LANES).astype(F32).astype(BF16)

    @pl.when(step > 0)
    def _():
        power_ref[...] += power


def event_rows(half, windows, rotation, source_inverse, send_rows, table):
    ev_dev, comps, stations, length = windows.shape
    owners, cap = send_rows.shape
    steps = 2 if ev_dev % 2 == 0 else 1
    events = ev_dev // steps
    total = ev_dev * stations + owners // 2
    whole = lambda *shape: pl.BlockSpec(shape, lambda i, *_: (0,) * len(shape))
    return pl.pallas_call(
        partial(spectra_kernel, steps),
        grid_spec=pltpu.PrefetchScalarGridSpec(
            num_scalar_prefetch=1,
            grid=(steps,),
            in_specs=[
                pl.BlockSpec((events, comps, stations, length), lambda i, *_: (i, 0, 0, 0)),
                whole(comps, ev_dev, stations),
                whole(ev_dev, length),
                whole(length, length),
                whole(owners, cap),
            ],
            out_specs=[whole(total, length), whole(stations, length // 2)],
        ),
        out_shape=[
            jax.ShapeDtypeStruct((total, length), BF16),
            jax.ShapeDtypeStruct((stations, length // 2), F32),
        ],
        compiler_params=pltpu.CompilerParams(vmem_limit_bytes=48 << 20),
        name="spectra",
    )(half, windows, rotation.swapaxes(0, 1), source_inverse, table, send_rows)


def pick_rows(index, rows, store):
    peers, cap = index.shape
    lines = LANES // cap
    for first in range(0, peers, lines):
        line = jnp.concatenate([index[first + j : first + j + 1, :] for j in range(lines)], axis=1)
        picked = jnp.dot(one_hot(line, rows.shape[0]), rows, preferred_element_type=F32)
        picked = picked.astype(BF16)
        for j in range(lines):
            store(first + j, picked[j * cap : (j + 1) * cap])


def own_kernel(half_ref, rows_ref, power_ref, index_ref, send_ref, pad_ref):
    peers, total, length = send_ref.shape
    cap = index_ref.shape[1]
    stations = power_ref.shape[0]
    share = stations // peers
    mine = pl.multiple_of(half_ref[0] * peers, peers)

    def store(peer, picked):
        send_ref[peer, :cap, :] = picked

    pick_rows(index_ref[pl.ds(mine, peers), :], rows_ref[...], store)
    pad_ref[:stations, :] = power_ref[...]
    pad_ref[stations:, :] = jnp.zeros((SUB, length // 2), F32)
    for peer in range(peers):
        send_ref[peer, cap:, :] = split_high(pad_ref[peer * share : peer * share + SUB, :])


def own_sends(half, rows, power, send_rows):
    owners, cap = send_rows.shape
    peers = owners // 2
    length = rows.shape[1]
    stations = power.shape[0]
    whole = lambda *shape: pl.BlockSpec(shape, lambda i, *_: (0,) * len(shape))
    return pl.pallas_call(
        own_kernel,
        grid_spec=pltpu.PrefetchScalarGridSpec(
            num_scalar_prefetch=1,
            grid=(1,),
            in_specs=[
                whole(rows.shape[0] - peers, length),
                whole(*power.shape),
                whole(owners, cap),
            ],
            out_specs=whole(peers, cap + SUB, length),
            scratch_shapes=[pltpu.VMEM((stations + SUB, length // 2), F32)],
        ),
        out_shape=jax.ShapeDtypeStruct((peers, cap + SUB, length), BF16),
        compiler_params=pltpu.CompilerParams(vmem_limit_bytes=48 << 20),
        name="own",
    )(half, rows, power, send_rows)


def relay_kernel(cap, rows_ref, weight_ref, *send_refs):
    peers, length = send_refs[0].shape[0], send_refs[0].shape[2]
    tail = rows_ref.shape[0] - peers
    rows_c = cap // len(send_refs)
    digits = rows_ref[tail:, :].astype(F32).astype(jnp.int32)
    index = digits[:, :cap] * LANES + digits[:, LANES : LANES + cap]

    def store(peer, picked):
        for c, ref in enumerate(send_refs):
            ref[peer, :rows_c, :] = picked[c * rows_c : (c + 1) * rows_c]

    pick_rows(index, rows_ref[:tail, :], store)
    for peer in range(peers):
        send_refs[0][peer, rows_c:, :] = weight_ref[...]


def relay_sends(rows, weight, peers, cap, chunks):
    length = rows.shape[1]
    rows_c = cap // chunks
    sizes = [rows_c + SUB] + [rows_c] * (chunks - 1)
    return pl.pallas_call(
        partial(relay_kernel, cap),
        out_shape=[jax.ShapeDtypeStruct((peers, size, length), BF16) for size in sizes],
        compiler_params=pltpu.CompilerParams(vmem_limit_bytes=48 << 20),
        name="relay",
    )(rows, weight)


def pair_kernel(geo, first, station_ref, count_ref, place_ref, own_ref, far_ref, weight_ref, lag_ref, *refs):
    out_ref = refs[-1]
    peers, cap, joint = geo
    group = pl.program_id(0) + first
    length = own_ref.shape[-1]
    half_len = length // 2
    rows = jnp.concatenate(
        [ref[...].reshape(peers * SUB, length) for ref in (own_ref, far_ref)], axis=0
    )
    width = rows.shape[0]
    for j in range(joint):
        for i in range(SUB):
            tile = j * cap + group * SUB + i
            picks = [one_hot(place_ref[m, j, i : i + 1, :], width) for m in range(2)]
            members = jnp.dot(jnp.concatenate(picks, axis=0), rows, preferred_element_type=F32)
            a, b = members[:LANES], members[LANES:]
            re_a, im_a = a[:, :half_len], a[:, half_len:]
            re_b, im_b = b[:, :half_len], b[:, half_len:]
            scale = weight_ref[pl.ds(station_ref[tile], 1), :]
            cross = jnp.concatenate(
                [
                    ((re_a * re_b + im_a * im_b) * scale).astype(BF16),
                    ((im_a * re_b - re_a * im_b) * scale).astype(BF16),
                ],
                axis=1,
            )
            lagged = jnp.dot(cross, lag_ref[...], preferred_element_type=F32)
            slot = lax.broadcasted_iota(jnp.int32, lagged.shape, 0)
            lagged = jnp.where(slot < count_ref[tile], lagged, 0.0)
            out_ref[j, i * LANES : (i + 1) * LANES, :] = lagged[:, :LAGS]


def correlate(chunk, chunks, geo, stations_of, counts, places, own, far, weight, lag_tab, previous):
    peers, cap, joint = geo
    steps = cap // SUB // chunks
    first = chunk * steps
    length = own.shape[-1]
    stations = weight.shape[0]
    in_specs = [
        pl.BlockSpec((2, joint, SUB, LANES), lambda i, *_: (0, 0, i + first, 0)),
        pl.BlockSpec((peers, SUB, length), lambda i, *_: (0, i + first, 0)),
        pl.BlockSpec((peers, SUB, length), lambda i, *_: (0, i, 0)),
        pl.BlockSpec((stations, length // 2), lambda i, *_: (0, 0)),
        pl.BlockSpec(lag_tab.shape, lambda i, *_: (0, 0)),
    ]
    args = [places, own, far, weight, lag_tab]
    aliases = {}
    if previous is not None:
        in_specs.append(pl.BlockSpec(memory_space=pl.ANY))
        args.append(previous)
        aliases = {7: 0}
    tiles = joint * steps * SUB
    macs = tiles * LANES * length * (2 * 2 * peers * SUB + lag_tab.shape[1])
    return pl.pallas_call(
        partial(pair_kernel, geo, first),
        grid_spec=pltpu.PrefetchScalarGridSpec(
            num_scalar_prefetch=2,
            grid=(steps,),
            in_specs=in_specs,
            out_specs=pl.BlockSpec((joint, SUB * LANES, LAGS), lambda i, *_: (0, i + first, 0)),
        ),
        out_shape=jax.ShapeDtypeStruct((joint, cap * LANES, LAGS), F32),
        input_output_aliases=aliases,
        compiler_params=pltpu.CompilerParams(vmem_limit_bytes=48 << 20),
        cost_estimate=pl.CostEstimate(
            flops=2 * macs, bytes_accessed=tiles * LANES * LAGS * 4, transcendentals=0
        ),
        name="pairs",
    )(stations_of, counts, *args)


def shards(windows, rotation, source_inverse, send_rows, tile_station, tile_count, pair_rows):
    ev_dev, comps, stations, length = windows.shape
    owners = lax.axis_size("ev")
    cap = send_rows.shape[1]
    tiles_dev = tile_station.shape[0]
    joint = tiles_dev // cap
    chunks = CHUNKS
    peers = owners // 2
    share = stations // peers
    half = lax.axis_index("ev") // peers
    halves = [list(range(peers)), list(range(peers, owners))]
    across = [(i, (i + peers) % owners) for i in range(owners)]
    to_peers = partial(
        lax.all_to_all,
        axis_name="ev",
        split_axis=0,
        concat_axis=0,
        axis_index_groups=halves,
        tiled=True,
    )
    half_arg = half.astype(jnp.int32).reshape(1)

    rows, power = event_rows(
        half_arg, windows, rotation, source_inverse, send_rows, spectral_table(length)
    )
    swapped = lax.ppermute(rows, "ev", across)
    own = to_peers(own_sends(half_arg, rows, power, send_rows))
    part = jnp.sum(join_high(own[:, cap : cap + share, :]), axis=0)
    power_sum = part + lax.ppermute(part, "ev", across)
    weight = 1.0 / (power_sum / (ev_dev * owners) + epsilon)
    weight = jnp.pad(split_high(weight), ((0, SUB - share), (0, 0)))
    sends = relay_sends(swapped, weight, peers, cap, chunks)

    source = pair_rows // cap
    side = source // peers != half
    places = jnp.where(side, peers * SUB, 0) + source % peers * SUB + pair_rows % SUB
    places = places.reshape(2, joint, cap, LANES)
    lag_tab = lag_table(length, LAGS, LAGS + 1)
    geo = (peers, cap, joint)
    result = None
    for chunk, send in enumerate(sends):
        far = to_peers(send)
        if chunk == 0:
            table = join_high(far[:, cap // chunks :][:, :share]).reshape(stations, length // 2)
        result = correlate(
            chunk, chunks, geo, tile_station, tile_count, places, own, far, table, lag_tab, result
        )
    return result.reshape(tiles_dev * LANES, LAGS)


def solution(mesh):
    in_specs = (
        P(("grp", "ev"), None, None, None),
        P(("grp", "ev"), None, None),
        P(("grp", "ev"), None),
        P(("grp", "ev"), None),
        P(("grp", "ev")),
        P(("grp", "ev")),
        P(None, ("grp", "ev")),
    )
    out_specs = P(("grp", "ev"), None)
    return jax.shard_map(shards, mesh=mesh, in_specs=in_specs, out_specs=out_specs, check_vma=False)
```

```python
from functools import partial
import math

import jax
import jax.numpy as jnp
import numpy as np
from jax import lax
from jax.experimental import pallas as pl
from jax.experimental.pallas import tpu as pltpu
from jax.sharding import PartitionSpec as P


LAGS = 255
SUB = 8
LANES = 128
CHUNKS = 1
TOGETHER = 2
VMEM = 60 << 20

epsilon = 1e-06
F32 = jnp.float32
BF16 = jnp.bfloat16


def spectral_table(length):
    half_len = length // 2
    samples = np.arange(length)[:, None]
    frequency = np.arange(half_len)[None, :]
    angles = (samples * frequency % length) * (2.0 * math.pi / length)
    factor = 1.0 / math.sqrt(length)
    table = np.concatenate([np.cos(angles) * factor, -np.sin(angles) * factor], axis=1)
    return jnp.asarray(table.astype(np.float32)).astype(BF16)


def lag_table(length, lag_count, width):
    half_len = length // 2
    frequency = np.arange(half_len)[:, None]
    shifts = np.arange(lag_count)[None, :] - lag_count // 2
    angles = (frequency * shifts % length) * (2.0 * math.pi / length)
    factor = 1.0 / math.sqrt(half_len)
    table = np.concatenate([np.cos(angles) * factor, -np.sin(angles) * factor], axis=0)
    table = np.pad(table, ((0, 0), (0, width - lag_count)))
    return jnp.asarray(table.astype(np.float32)).astype(BF16)


def column(values):
    return jnp.transpose(jnp.broadcast_to(values, (LANES, LANES)))


def one_hot(values, width):
    down = column(values)
    lane = lax.broadcasted_iota(jnp.int32, (LANES, LANES), 1)
    parts = [
        jnp.where(down == lane + LANES * j, 1.0, 0.0).astype(BF16) for j in range(width // LANES)
    ]
    return jnp.concatenate(parts, axis=1)


def split_high(values):
    high = values.astype(BF16)
    rest = (values - high.astype(F32)).astype(BF16)
    return jnp.concatenate([high, rest], axis=-1)


def join_high(values):
    width = values.shape[-1] // 2
    return values[..., :width].astype(F32) + values[..., width:].astype(F32)


def spectra_kernel(steps, half_ref, win_ref, rot_ref, inv_ref, table_ref, index_ref, rows_ref, power_ref):
    step = pl.program_id(0)
    events, comps, stations, length = win_ref.shape
    half_len = length // 2
    blocks = []
    turns = rot_ref[...].astype(F32)
    for e in range(events):
        turn = turns[:, e, :]
        for s in range(1, steps):
            turn = jnp.where(step == s, turns[:, s * events + e, :], turn)
        rot = jnp.transpose(turn)
        total = rot[:, 0:1] * win_ref[e, 0].astype(F32)
        for c in range(1, comps):
            total += rot[:, c : c + 1] * win_ref[e, c].astype(F32)
        blocks.append(total.astype(BF16))
    transverse = jnp.concatenate(blocks, axis=0)
    spectrum = jnp.dot(transverse, table_ref[...], preferred_element_type=F32)
    gains = inv_ref[...].astype(F32)
    power = jnp.zeros((stations, half_len), F32)
    for e in range(events):
        re_in = spectrum[e * stations : (e + 1) * stations, :half_len]
        im_in = spectrum[e * stations : (e + 1) * stations, half_len:]
        gain = gains[e : e + 1, :]
        for s in range(1, steps):
            gain = jnp.where(step == s, gains[s * events + e : s * events + e + 1, :], gain)
        re_g, im_g = gain[:, :half_len], gain[:, half_len:]
        re = re_in * re_g - im_in * im_g
        im = re_in * im_g + im_in * re_g
        power += re * re + im * im
        base = pl.multiple_of((step * events + e) * stations, stations)
        rows_ref[pl.ds(base, stations), :half_len] = re.astype(BF16)
        rows_ref[pl.ds(base, stations), half_len:] = im.astype(BF16)

    @pl.when(step == 0)
    def _():
        power_ref[...] = power
        owners, cap = index_ref.shape
        peers = owners // 2
        other = pl.multiple_of((1 - half_ref[0]) * peers, peers)
        wanted = index_ref[pl.ds(other, peers), :]
        tail = rows_ref.shape[0] - peers
        rows_ref[tail:, :] = jnp.zeros((peers, length), BF16)
        rows_ref[tail:, :cap] = (wanted // LANES).astype(F32).astype(BF16)
        rows_ref[tail:, LANES : LANES + cap] = (wanted % LANES).astype(F32).astype(BF16)

    @pl.when(step > 0)
    def _():
        power_ref[...] += power


def event_rows(half, windows, rotation, source_inverse, send_rows, table):
    ev_dev, comps, stations, length = windows.shape
    owners, cap = send_rows.shape
    steps = 2 if ev_dev % 2 == 0 else 1
    events = ev_dev // steps
    total = ev_dev * stations + owners // 2
    whole = lambda *shape: pl.BlockSpec(shape, lambda i, *_: (0,) * len(shape))
    return pl.pallas_call(
        partial(spectra_kernel, steps),
        grid_spec=pltpu.PrefetchScalarGridSpec(
            num_scalar_prefetch=1,
            grid=(steps,),
            in_specs=[
                pl.BlockSpec((events, comps, stations, length), lambda i, *_: (i, 0, 0, 0)),
                whole(comps, ev_dev, stations),
                whole(ev_dev, length),
                whole(length, length),
                whole(owners, cap),
            ],
            out_specs=[whole(total, length), whole(stations, length // 2)],
        ),
        out_shape=[
            jax.ShapeDtypeStruct((total, length), BF16),
            jax.ShapeDtypeStruct((stations, length // 2), F32),
        ],
        compiler_params=pltpu.CompilerParams(vmem_limit_bytes=VMEM),
        name="spectra",
    )(half, windows, rotation.swapaxes(0, 1), source_inverse, table, send_rows)


def pick_rows(index, rows, store):
    peers, cap = index.shape
    lines = LANES // cap
    for first in range(0, peers, lines):
        line = jnp.concatenate([index[first + j : first + j + 1, :] for j in range(lines)], axis=1)
        picked = jnp.dot(one_hot(line, rows.shape[0]), rows, preferred_element_type=F32)
        picked = picked.astype(BF16)
        for j in range(lines):
            store(first + j, picked[j * cap : (j + 1) * cap])


def own_kernel(half_ref, rows_ref, power_ref, index_ref, send_ref, pad_ref):
    peers, _, length = send_ref.shape
    cap = index_ref.shape[1]
    stations = power_ref.shape[0]
    share = stations // peers
    mine = pl.multiple_of(half_ref[0] * peers, peers)

    def store(peer, picked):
        send_ref[peer, :cap, :] = picked

    pick_rows(index_ref[pl.ds(mine, peers), :], rows_ref[...], store)
    pad_ref[:stations, :] = power_ref[...]
    pad_ref[stations:, :] = jnp.zeros((SUB, length // 2), F32)
    for peer in range(peers):
        send_ref[peer, cap:, :] = split_high(pad_ref[peer * share : peer * share + SUB, :])


def own_sends(half, rows, power, send_rows):
    owners, cap = send_rows.shape
    peers = owners // 2
    length = rows.shape[1]
    stations = power.shape[0]
    whole = lambda *shape: pl.BlockSpec(shape, lambda i, *_: (0,) * len(shape))
    return pl.pallas_call(
        own_kernel,
        grid_spec=pltpu.PrefetchScalarGridSpec(
            num_scalar_prefetch=1,
            grid=(1,),
            in_specs=[
                whole(rows.shape[0] - peers, length),
                whole(*power.shape),
                whole(owners, cap),
            ],
            out_specs=whole(peers, cap + SUB, length),
            scratch_shapes=[pltpu.VMEM((stations + SUB, length // 2), F32)],
        ),
        out_shape=jax.ShapeDtypeStruct((peers, cap + SUB, length), BF16),
        compiler_params=pltpu.CompilerParams(vmem_limit_bytes=VMEM),
        name="own",
    )(half, rows, power, send_rows)


def relay_kernel(cap, events, rows_ref, mine_ref, other_ref, *refs):
    *send_refs, pad_ref = refs
    peers = send_refs[0].shape[0]
    share = mine_ref.shape[0]
    tail = rows_ref.shape[0] - peers
    rows_c = cap // len(send_refs)
    digits = rows_ref[tail:, :].astype(F32).astype(jnp.int32)
    index = digits[:, :cap] * LANES + digits[:, LANES : LANES + cap]

    def store(peer, picked):
        for c, ref in enumerate(send_refs):
            ref[peer, :rows_c, :] = picked[c * rows_c : (c + 1) * rows_c]

    pick_rows(index, rows_ref[:tail, :], store)
    pad_ref[...] = jnp.ones_like(pad_ref)
    pad_ref[:share, :] = 1.0 / ((mine_ref[...] + other_ref[...]) / events + epsilon)
    weight = split_high(pad_ref[...])
    for peer in range(peers):
        send_refs[0][peer, rows_c:, :] = weight


def relay_sends(rows, mine, other, peers, cap, chunks, events):
    length = rows.shape[1]
    rows_c = cap // chunks
    sizes = [rows_c + SUB] + [rows_c] * (chunks - 1)
    return pl.pallas_call(
        partial(relay_kernel, cap, events),
        out_shape=[jax.ShapeDtypeStruct((peers, size, length), BF16) for size in sizes],
        scratch_shapes=[pltpu.VMEM((SUB, length // 2), F32)],
        compiler_params=pltpu.CompilerParams(vmem_limit_bytes=VMEM),
        name="relay",
    )(rows, mine, other)


def pair_kernel(geo, first, station_ref, count_ref, place_ref, own_ref, far_ref, got_ref, lag_ref, *refs):
    *_, out_ref, weight_ref = refs
    peers, cap, joint = geo
    group = pl.program_id(0) + first
    length = own_ref.shape[-1]
    half_len = length // 2
    share = weight_ref.shape[0] // peers

    @pl.when(pl.program_id(0) == 0)
    def _():
        for peer in range(peers):
            weight_ref[peer * share : (peer + 1) * share, :] = join_high(got_ref[peer])[:share]

    rows = jnp.concatenate(
        [ref[...].reshape(peers * SUB, length) for ref in (own_ref, far_ref)], axis=0
    )
    width = rows.shape[0]
    many = TOGETHER * LANES
    for j in range(joint):
        for i in range(0, SUB, TOGETHER):
            picks = [
                one_hot(place_ref[m, j, i + n : i + n + 1, :], width)
                for m in range(2)
                for n in range(TOGETHER)
            ]
            members = jnp.dot(jnp.concatenate(picks, axis=0), rows, preferred_element_type=F32)
            halves = []
            for n in range(TOGETHER):
                a = members[n * LANES : (n + 1) * LANES]
                b = members[many + n * LANES : many + (n + 1) * LANES]
                re_a, im_a = a[:, :half_len], a[:, half_len:]
                re_b, im_b = b[:, :half_len], b[:, half_len:]
                tile = j * cap + group * SUB + i + n
                scale = weight_ref[pl.ds(station_ref[tile], 1), :]
                halves.append(
                    jnp.concatenate(
                        [
                            ((re_a * re_b + im_a * im_b) * scale).astype(BF16),
                            ((im_a * re_b - re_a * im_b) * scale).astype(BF16),
                        ],
                        axis=1,
                    )
                )
            cross = jnp.concatenate(halves, axis=0)
            lagged = jnp.dot(cross, lag_ref[...], preferred_element_type=F32)
            for n in range(TOGETHER):
                tile = j * cap + group * SUB + i + n
                piece = lagged[n * LANES : (n + 1) * LANES]
                slot = lax.broadcasted_iota(jnp.int32, piece.shape, 0)
                piece = jnp.where(slot < count_ref[tile], piece, 0.0)
                out_ref[j, (i + n) * LANES : (i + n + 1) * LANES, :] = piece[:, :LAGS]


def correlate(chunk, chunks, geo, stations, stations_of, counts, places, own, far, got, lag_tab, previous):
    peers, cap, joint = geo
    steps = cap // SUB // chunks
    first = chunk * steps
    length = own.shape[-1]
    in_specs = [
        pl.BlockSpec((2, joint, SUB, LANES), lambda i, *_: (0, 0, i + first, 0)),
        pl.BlockSpec((peers, SUB, length), lambda i, *_: (0, i + first, 0)),
        pl.BlockSpec((peers, SUB, length), lambda i, *_: (0, i, 0)),
        pl.BlockSpec((peers, SUB, length), lambda i, *_: (0, steps, 0)),
        pl.BlockSpec(lag_tab.shape, lambda i, *_: (0, 0)),
    ]
    args = [places, own, far, got, lag_tab]
    aliases = {}
    if previous is not None:
        in_specs.append(pl.BlockSpec(memory_space=pl.ANY))
        args.append(previous)
        aliases = {7: 0}
    tiles = joint * steps * SUB
    macs = tiles * LANES * length * (2 * 2 * peers * SUB + lag_tab.shape[1])
    return pl.pallas_call(
        partial(pair_kernel, geo, first),
        grid_spec=pltpu.PrefetchScalarGridSpec(
            num_scalar_prefetch=2,
            grid=(steps,),
            in_specs=in_specs,
            out_specs=pl.BlockSpec((joint, SUB * LANES, LAGS), lambda i, *_: (0, i + first, 0)),
            scratch_shapes=[pltpu.VMEM((stations, length // 2), F32)],
        ),
        out_shape=jax.ShapeDtypeStruct((joint, cap * LANES, LAGS), F32),
        input_output_aliases=aliases,
        compiler_params=pltpu.CompilerParams(vmem_limit_bytes=VMEM),
        cost_estimate=pl.CostEstimate(
            flops=2 * macs, bytes_accessed=tiles * LANES * LAGS * 4, transcendentals=0
        ),
        name="pairs",
    )(stations_of, counts, *args)


def shards(windows, rotation, source_inverse, send_rows, tile_station, tile_count, pair_rows):
    ev_dev, _, stations, length = windows.shape
    owners = lax.axis_size("ev")
    cap = send_rows.shape[1]
    tiles_dev = tile_station.shape[0]
    joint = tiles_dev // cap
    chunks = CHUNKS
    peers = owners // 2
    share = stations // peers
    half = lax.axis_index("ev") // peers
    halves = [list(range(peers)), list(range(peers, owners))]
    across = [(i, (i + peers) % owners) for i in range(owners)]
    to_peers = partial(
        lax.all_to_all,
        axis_name="ev",
        split_axis=0,
        concat_axis=0,
        axis_index_groups=halves,
        tiled=True,
    )
    half_arg = half.astype(jnp.int32).reshape(1)

    rows, power = event_rows(
        half_arg, windows, rotation, source_inverse, send_rows, spectral_table(length)
    )
    swapped = lax.ppermute(rows, "ev", across)
    sends = own_sends(half_arg, rows, power, send_rows)
    own = to_peers(sends)
    mine = jnp.sum(join_high(own[:, cap : cap + share, :]), axis=0)
    other = lax.ppermute(mine, "ev", across)
    sends = relay_sends(swapped, mine, other, peers, cap, chunks, ev_dev * owners)

    source = pair_rows // cap
    side = source // peers != half
    places = jnp.where(side, peers * SUB, 0) + source % peers * SUB + pair_rows % SUB
    places = places.reshape(2, joint, cap, LANES)
    lag_tab = lag_table(length, LAGS, LAGS + 1)
    geo = (peers, cap, joint)
    result = None
    for chunk, send in enumerate(sends):
        far = to_peers(send)
        if chunk == 0:
            got = far
        result = correlate(
            chunk, chunks, geo, stations, tile_station, tile_count, places, own, far, got, lag_tab, result
        )
    return result.reshape(tiles_dev * LANES, LAGS)


def solution(mesh):
    in_specs = (
        P(("grp", "ev"), None, None, None),
        P(("grp", "ev"), None, None),
        P(("grp", "ev"), None),
        P(("grp", "ev"), None),
        P(("grp", "ev")),
        P(("grp", "ev")),
        P(None, ("grp", "ev")),
    )
    out_specs = P(("grp", "ev"), None)
    return jax.shard_map(shards, mesh=mesh, in_specs=in_specs, out_specs=out_specs, check_vma=False)
```

```python
from functools import partial
import math

import jax
import jax.numpy as jnp
import numpy as np
from jax import lax
from jax.experimental import pallas as pl
from jax.experimental.pallas import tpu as pltpu
from jax.sharding import PartitionSpec as P


LAGS = 255
SUB = 8
LANES = 128
SPLIT = (6, 2)
TOGETHER = 2
VMEM = 60 << 20
SMALL = 20 << 20

epsilon = 1e-06
F32 = jnp.float32
BF16 = jnp.bfloat16


def spectral_table(length):
    half_len = length // 2
    samples = np.arange(length)[:, None]
    frequency = np.arange(half_len)[None, :]
    angles = (samples * frequency % length) * (2.0 * math.pi / length)
    factor = 1.0 / math.sqrt(length)
    table = np.concatenate([np.cos(angles) * factor, -np.sin(angles) * factor], axis=1)
    return jnp.asarray(table.astype(np.float32)).astype(BF16)


def lag_table(length, lag_count, width):
    half_len = length // 2
    frequency = np.arange(half_len)[:, None]
    shifts = np.arange(lag_count)[None, :] - lag_count // 2
    angles = (frequency * shifts % length) * (2.0 * math.pi / length)
    factor = 1.0 / math.sqrt(half_len)
    table = np.concatenate([np.cos(angles) * factor, -np.sin(angles) * factor], axis=0)
    table = np.pad(table, ((0, 0), (0, width - lag_count)))
    return jnp.asarray(table.astype(np.float32)).astype(BF16)


def column(values):
    return jnp.transpose(jnp.broadcast_to(values, (LANES, LANES)))


def one_hot(values, width):
    down = column(values)
    lane = lax.broadcasted_iota(jnp.int32, (LANES, LANES), 1)
    parts = [
        jnp.where(down == lane + LANES * j, 1.0, 0.0).astype(BF16) for j in range(width // LANES)
    ]
    return jnp.concatenate(parts, axis=1)


def spectra_kernel(steps, half_ref, win_ref, rot_ref, inv_ref, table_ref, index_ref, rows_ref, power_ref):
    step = pl.program_id(0)
    events, comps, stations, length = win_ref.shape
    half_len = length // 2
    blocks = []
    turns = rot_ref[...].astype(F32)
    for e in range(events):
        turn = turns[:, e, :]
        for s in range(1, steps):
            turn = jnp.where(step == s, turns[:, s * events + e, :], turn)
        rot = jnp.transpose(turn)
        total = rot[:, 0:1] * win_ref[e, 0].astype(F32)
        for c in range(1, comps):
            total += rot[:, c : c + 1] * win_ref[e, c].astype(F32)
        blocks.append(total.astype(BF16))
    transverse = jnp.concatenate(blocks, axis=0)
    spectrum = jnp.dot(transverse, table_ref[...], preferred_element_type=F32)
    gains = inv_ref[...].astype(F32)
    power = jnp.zeros((stations, half_len), F32)
    for e in range(events):
        re_in = spectrum[e * stations : (e + 1) * stations, :half_len]
        im_in = spectrum[e * stations : (e + 1) * stations, half_len:]
        gain = gains[e : e + 1, :]
        for s in range(1, steps):
            gain = jnp.where(step == s, gains[s * events + e : s * events + e + 1, :], gain)
        re_g, im_g = gain[:, :half_len], gain[:, half_len:]
        re = re_in * re_g - im_in * im_g
        im = re_in * im_g + im_in * re_g
        power += re * re + im * im
        base = pl.multiple_of((step * events + e) * stations, stations)
        rows_ref[pl.ds(base, stations), :half_len] = re.astype(BF16)
        rows_ref[pl.ds(base, stations), half_len:] = im.astype(BF16)

    @pl.when(step == 0)
    def _():
        power_ref[...] = power
        owners, cap = index_ref.shape
        peers = owners // 2
        other = pl.multiple_of((1 - half_ref[0]) * peers, peers)
        wanted = index_ref[pl.ds(other, peers), :]
        tail = rows_ref.shape[0] - peers
        rows_ref[tail:, :] = jnp.zeros((peers, length), BF16)
        rows_ref[tail:, :cap] = (wanted // LANES).astype(F32).astype(BF16)
        rows_ref[tail:, LANES : LANES + cap] = (wanted % LANES).astype(F32).astype(BF16)

    @pl.when(step > 0)
    def _():
        power_ref[...] += power


def event_rows(half, windows, rotation, source_inverse, send_rows, table):
    ev_dev, comps, stations, length = windows.shape
    owners, cap = send_rows.shape
    steps = 2 if ev_dev % 2 == 0 else 1
    events = ev_dev // steps
    total = ev_dev * stations + owners // 2
    whole = lambda *shape: pl.BlockSpec(shape, lambda i, *_: (0,) * len(shape))
    return pl.pallas_call(
        partial(spectra_kernel, steps),
        grid_spec=pltpu.PrefetchScalarGridSpec(
            num_scalar_prefetch=1,
            grid=(steps,),
            in_specs=[
                pl.BlockSpec((events, comps, stations, length), lambda i, *_: (i, 0, 0, 0)),
                whole(comps, ev_dev, stations),
                whole(ev_dev, length),
                whole(length, length),
                whole(owners, cap),
            ],
            out_specs=[whole(total, length), whole(stations, length // 2)],
        ),
        out_shape=[
            jax.ShapeDtypeStruct((total, length), BF16),
            jax.ShapeDtypeStruct((stations, length // 2), F32),
        ],
        compiler_params=pltpu.CompilerParams(vmem_limit_bytes=VMEM),
        name="spectra",
    )(half, windows, rotation.swapaxes(0, 1), source_inverse, table, send_rows)


def pick_rows(index, rows, store):
    peers, cap = index.shape
    lines = LANES // cap
    for first in range(0, peers, lines):
        line = jnp.concatenate([index[first + j : first + j + 1, :] for j in range(lines)], axis=1)
        picked = jnp.dot(one_hot(line, rows.shape[0]), rows, preferred_element_type=F32)
        picked = picked.astype(BF16)
        for j in range(lines):
            store(first + j, picked[j * cap : (j + 1) * cap])


def own_kernel(half_ref, rows_ref, index_ref, send_ref):
    peers = send_ref.shape[0]
    mine = pl.multiple_of(half_ref[0] * peers, peers)

    def store(peer, picked):
        send_ref[peer] = picked

    pick_rows(index_ref[pl.ds(mine, peers), :], rows_ref[...], store)


def own_sends(half, rows, send_rows):
    owners, cap = send_rows.shape
    peers = owners // 2
    length = rows.shape[1]
    whole = lambda *shape: pl.BlockSpec(shape, lambda i, *_: (0,) * len(shape))
    return pl.pallas_call(
        own_kernel,
        grid_spec=pltpu.PrefetchScalarGridSpec(
            num_scalar_prefetch=1,
            grid=(1,),
            in_specs=[whole(rows.shape[0] - peers, length), whole(owners, cap)],
            out_specs=whole(peers, cap, length),
        ),
        out_shape=jax.ShapeDtypeStruct((peers, cap, length), BF16),
        compiler_params=pltpu.CompilerParams(vmem_limit_bytes=SMALL),
        name="own",
    )(half, rows, send_rows)


def relay_kernel(rows_ref, *send_refs):
    peers = send_refs[0].shape[0]
    cap = sum(ref.shape[1] for ref in send_refs)
    tail = rows_ref.shape[0] - peers
    digits = rows_ref[tail:, :].astype(F32).astype(jnp.int32)
    index = digits[:, :cap] * LANES + digits[:, LANES : LANES + cap]

    def store(peer, picked):
        start = 0
        for ref in send_refs:
            ref[peer] = picked[start : start + ref.shape[1]]
            start += ref.shape[1]

    pick_rows(index, rows_ref[:tail, :], store)


def relay_sends(rows, peers, sizes):
    length = rows.shape[1]
    return pl.pallas_call(
        relay_kernel,
        out_shape=[jax.ShapeDtypeStruct((peers, size * SUB, length), BF16) for size in sizes],
        compiler_params=pltpu.CompilerParams(vmem_limit_bytes=SMALL),
        name="relay",
    )(rows)


def pair_kernel(geo, first, station_ref, count_ref, place_ref, own_ref, far_ref, weight_ref, lag_ref, *refs):
    out_ref = refs[-1]
    peers, cap, joint = geo
    group = pl.program_id(0) + first
    length = own_ref.shape[-1]
    half_len = length // 2

    rows = jnp.concatenate(
        [ref[...].reshape(peers * SUB, length) for ref in (own_ref, far_ref)], axis=0
    )
    width = rows.shape[0]
    many = TOGETHER * LANES
    for j in range(joint):
        for i in range(0, SUB, TOGETHER):
            picks = [
                one_hot(place_ref[m, j, i + n : i + n + 1, :], width)
                for m in range(2)
                for n in range(TOGETHER)
            ]
            members = jnp.dot(jnp.concatenate(picks, axis=0), rows, preferred_element_type=F32)
            halves = []
            for n in range(TOGETHER):
                a = members[n * LANES : (n + 1) * LANES]
                b = members[many + n * LANES : many + (n + 1) * LANES]
                re_a, im_a = a[:, :half_len], a[:, half_len:]
                re_b, im_b = b[:, :half_len], b[:, half_len:]
                tile = j * cap + group * SUB + i + n
                scale = weight_ref[pl.ds(station_ref[tile], 1), :]
                halves.append(
                    jnp.concatenate(
                        [
                            ((re_a * re_b + im_a * im_b) * scale).astype(BF16),
                            ((im_a * re_b - re_a * im_b) * scale).astype(BF16),
                        ],
                        axis=1,
                    )
                )
            cross = jnp.concatenate(halves, axis=0)
            lagged = jnp.dot(cross, lag_ref[...], preferred_element_type=F32)
            for n in range(TOGETHER):
                tile = j * cap + group * SUB + i + n
                piece = lagged[n * LANES : (n + 1) * LANES]
                slot = lax.broadcasted_iota(jnp.int32, piece.shape, 0)
                piece = jnp.where(slot < count_ref[tile], piece, 0.0)
                out_ref[j, (i + n) * LANES : (i + n + 1) * LANES, :] = piece[:, :LAGS]


def correlate(first, steps, geo, stations_of, counts, places, own, far, weight, lag_tab, previous):
    peers, cap, joint = geo
    length = own.shape[-1]
    in_specs = [
        pl.BlockSpec((2, joint, SUB, LANES), lambda i, *_: (0, 0, i + first, 0)),
        pl.BlockSpec((peers, SUB, length), lambda i, *_: (0, i + first, 0)),
        pl.BlockSpec((peers, SUB, length), lambda i, *_: (0, i, 0)),
        pl.BlockSpec(weight.shape, lambda i, *_: (0, 0)),
        pl.BlockSpec(lag_tab.shape, lambda i, *_: (0, 0)),
    ]
    args = [places, own, far, weight, lag_tab]
    aliases = {}
    if previous is not None:
        in_specs.append(pl.BlockSpec(memory_space=pl.ANY))
        args.append(previous)
        aliases = {7: 0}
    tiles = joint * steps * SUB
    macs = tiles * LANES * length * (2 * 2 * peers * SUB + lag_tab.shape[1])
    return pl.pallas_call(
        partial(pair_kernel, geo, first),
        grid_spec=pltpu.PrefetchScalarGridSpec(
            num_scalar_prefetch=2,
            grid=(steps,),
            in_specs=in_specs,
            out_specs=pl.BlockSpec((joint, SUB * LANES, LAGS), lambda i, *_: (0, i + first, 0)),
        ),
        out_shape=jax.ShapeDtypeStruct((joint, cap * LANES, LAGS), F32),
        input_output_aliases=aliases,
        compiler_params=pltpu.CompilerParams(vmem_limit_bytes=VMEM),
        cost_estimate=pl.CostEstimate(
            flops=2 * macs, bytes_accessed=tiles * LANES * LAGS * 4, transcendentals=0
        ),
        name="pairs",
    )(stations_of, counts, *args)


def power_total(power, owners):
    if owners & (owners - 1):
        return lax.psum(power, "ev")
    step = 1
    while step < owners:
        power += lax.ppermute(power, "ev", [(i, i ^ step) for i in range(owners)])
        step *= 2
    return power


def shards(windows, rotation, source_inverse, send_rows, tile_station, tile_count, pair_rows):
    ev_dev, _, _, length = windows.shape
    owners = lax.axis_size("ev")
    cap = send_rows.shape[1]
    tiles_dev = tile_station.shape[0]
    joint = tiles_dev // cap
    peers = owners // 2
    half = lax.axis_index("ev") // peers
    halves = [list(range(peers)), list(range(peers, owners))]
    across = [(i, (i + peers) % owners) for i in range(owners)]
    to_peers = partial(
        lax.all_to_all,
        axis_name="ev",
        split_axis=0,
        concat_axis=0,
        axis_index_groups=halves,
        tiled=True,
    )
    half_arg = half.astype(jnp.int32).reshape(1)

    rows, power = event_rows(
        half_arg, windows, rotation, source_inverse, send_rows, spectral_table(length)
    )
    swapped = lax.ppermute(rows, "ev", across)
    sends = own_sends(half_arg, rows, send_rows)
    own = to_peers(sends)
    weight = 1.0 / (power_total(power, owners) / (ev_dev * owners) + epsilon)
    groups = cap // SUB
    parts = [groups * part // sum(SPLIT) for part in SPLIT[:-1]]
    sizes = parts + [groups - sum(parts)]
    sends = relay_sends(swapped, peers, sizes)

    source = pair_rows // cap
    side = source // peers != half
    places = jnp.where(side, peers * SUB, 0) + source % peers * SUB + pair_rows % SUB
    places = places.reshape(2, joint, cap, LANES)
    lag_tab = lag_table(length, LAGS, LAGS + 1)
    geo = (peers, cap, joint)
    result = None
    first = 0
    for steps, send in zip(sizes, sends):
        far = to_peers(send)
        result = correlate(
            first, steps, geo, tile_station, tile_count, places, own, far, weight, lag_tab, result
        )
        first += steps
    return result.reshape(tiles_dev * LANES, LAGS)


def solution(mesh):
    in_specs = (
        P(("grp", "ev"), None, None, None),
        P(("grp", "ev"), None, None),
        P(("grp", "ev"), None),
        P(("grp", "ev"), None),
        P(("grp", "ev")),
        P(("grp", "ev")),
        P(None, ("grp", "ev")),
    )
    out_specs = P(("grp", "ev"), None)
    return jax.shard_map(shards, mesh=mesh, in_specs=in_specs, out_specs=out_specs, check_vma=False)
```

```python
from functools import partial
import math

import jax
import jax.numpy as jnp
import numpy as np
from jax import lax
from jax.experimental import pallas as pl
from jax.experimental.pallas import tpu as pltpu
from jax.sharding import PartitionSpec as P


LAGS = 255
SUB = 8
LANES = 128
SPLIT = (6, 2)
TOGETHER = 2
VMEM = 60 << 20
SMALL = 20 << 20

epsilon = 1e-06
F32 = jnp.float32
BF16 = jnp.bfloat16


def spectral_table(length):
    half_len = length // 2
    samples = np.arange(length)[:, None]
    frequency = np.arange(half_len)[None, :]
    angles = (samples * frequency % length) * (2.0 * math.pi / length)
    factor = 1.0 / math.sqrt(length)
    table = np.concatenate([np.cos(angles) * factor, -np.sin(angles) * factor], axis=1)
    return jnp.asarray(table.astype(np.float32)).astype(BF16)


def lag_table(length, lag_count, width):
    half_len = length // 2
    frequency = np.arange(half_len)[:, None]
    shifts = np.arange(lag_count)[None, :] - lag_count // 2
    angles = (frequency * shifts % length) * (2.0 * math.pi / length)
    factor = 1.0 / math.sqrt(half_len)
    table = np.concatenate([np.cos(angles) * factor, -np.sin(angles) * factor], axis=0)
    table = np.pad(table, ((0, 0), (0, width - lag_count)))
    return jnp.asarray(table.astype(np.float32)).astype(BF16)


def column(values):
    return jnp.transpose(jnp.broadcast_to(values, (LANES, LANES)))


def one_hot(values, width):
    down = column(values)
    lane = lax.broadcasted_iota(jnp.int32, (LANES, LANES), 1)
    parts = [
        jnp.where(down == lane + LANES * j, 1.0, 0.0).astype(BF16) for j in range(width // LANES)
    ]
    return jnp.concatenate(parts, axis=1)


def spectra_kernel(steps, half_ref, win_ref, rot_ref, inv_ref, table_ref, index_ref, rows_ref, power_ref):
    step = pl.program_id(0)
    events, comps, stations, length = win_ref.shape
    half_len = length // 2
    blocks = []
    turns = rot_ref[...].astype(F32)
    for e in range(events):
        turn = turns[:, e, :]
        for s in range(1, steps):
            turn = jnp.where(step == s, turns[:, s * events + e, :], turn)
        rot = jnp.transpose(turn)
        total = rot[:, 0:1] * win_ref[e, 0].astype(F32)
        for c in range(1, comps):
            total += rot[:, c : c + 1] * win_ref[e, c].astype(F32)
        blocks.append(total.astype(BF16))
    transverse = jnp.concatenate(blocks, axis=0)
    spectrum = jnp.dot(transverse, table_ref[...], preferred_element_type=F32)
    gains = inv_ref[...].astype(F32)
    power = jnp.zeros((stations, half_len), F32)
    for e in range(events):
        re_in = spectrum[e * stations : (e + 1) * stations, :half_len]
        im_in = spectrum[e * stations : (e + 1) * stations, half_len:]
        gain = gains[e : e + 1, :]
        for s in range(1, steps):
            gain = jnp.where(step == s, gains[s * events + e : s * events + e + 1, :], gain)
        re_g, im_g = gain[:, :half_len], gain[:, half_len:]
        re = re_in * re_g - im_in * im_g
        im = re_in * im_g + im_in * re_g
        power += re * re + im * im
        base = pl.multiple_of((step * events + e) * stations, stations)
        rows_ref[pl.ds(base, stations), :half_len] = re.astype(BF16)
        rows_ref[pl.ds(base, stations), half_len:] = im.astype(BF16)

    @pl.when(step == 0)
    def _():
        power_ref[...] = power
        owners, cap = index_ref.shape
        peers = owners // 2
        other = pl.multiple_of((1 - half_ref[0]) * peers, peers)
        wanted = index_ref[pl.ds(other, peers), :]
        tail = rows_ref.shape[0] - peers
        rows_ref[tail:, :] = jnp.zeros((peers, length), BF16)
        rows_ref[tail:, :cap] = (wanted // LANES).astype(F32).astype(BF16)
        rows_ref[tail:, LANES : LANES + cap] = (wanted % LANES).astype(F32).astype(BF16)

    @pl.when(step > 0)
    def _():
        power_ref[...] += power


def event_rows(half, windows, rotation, source_inverse, send_rows, table):
    ev_dev, comps, stations, length = windows.shape
    owners, cap = send_rows.shape
    steps = 2 if ev_dev % 2 == 0 else 1
    events = ev_dev // steps
    total = ev_dev * stations + owners // 2
    whole = lambda *shape: pl.BlockSpec(shape, lambda i, *_: (0,) * len(shape))
    return pl.pallas_call(
        partial(spectra_kernel, steps),
        grid_spec=pltpu.PrefetchScalarGridSpec(
            num_scalar_prefetch=1,
            grid=(steps,),
            in_specs=[
                pl.BlockSpec((events, comps, stations, length), lambda i, *_: (i, 0, 0, 0)),
                whole(comps, ev_dev, stations),
                whole(ev_dev, length),
                whole(length, length),
                whole(owners, cap),
            ],
            out_specs=[whole(total, length), whole(stations, length // 2)],
        ),
        out_shape=[
            jax.ShapeDtypeStruct((total, length), BF16),
            jax.ShapeDtypeStruct((stations, length // 2), F32),
        ],
        compiler_params=pltpu.CompilerParams(vmem_limit_bytes=VMEM),
        name="spectra",
    )(half, windows, rotation.swapaxes(0, 1), source_inverse, table, send_rows)


def pick_rows(index, rows, store):
    peers, cap = index.shape
    lines = LANES // cap
    for first in range(0, peers, lines):
        line = jnp.concatenate([index[first + j : first + j + 1, :] for j in range(lines)], axis=1)
        picked = jnp.dot(one_hot(line, rows.shape[0]), rows, preferred_element_type=F32)
        picked = picked.astype(BF16)
        for j in range(lines):
            store(first + j, picked[j * cap : (j + 1) * cap])


def own_kernel(half_ref, rows_ref, index_ref, send_ref):
    peers = send_ref.shape[0]
    mine = pl.multiple_of(half_ref[0] * peers, peers)

    def store(peer, picked):
        send_ref[peer] = picked

    pick_rows(index_ref[pl.ds(mine, peers), :], rows_ref[...], store)


def own_sends(half, rows, send_rows):
    owners, cap = send_rows.shape
    peers = owners // 2
    length = rows.shape[1]
    whole = lambda *shape: pl.BlockSpec(shape, lambda i, *_: (0,) * len(shape))
    return pl.pallas_call(
        own_kernel,
        grid_spec=pltpu.PrefetchScalarGridSpec(
            num_scalar_prefetch=1,
            grid=(1,),
            in_specs=[whole(rows.shape[0] - peers, length), whole(owners, cap)],
            out_specs=whole(peers, cap, length),
        ),
        out_shape=jax.ShapeDtypeStruct((peers, cap, length), BF16),
        compiler_params=pltpu.CompilerParams(vmem_limit_bytes=SMALL),
        name="own",
    )(half, rows, send_rows)


def relay_kernel(rows_ref, *send_refs):
    peers = send_refs[0].shape[0]
    cap = sum(ref.shape[1] for ref in send_refs)
    tail = rows_ref.shape[0] - peers
    digits = rows_ref[tail:, :].astype(F32).astype(jnp.int32)
    index = digits[:, :cap] * LANES + digits[:, LANES : LANES + cap]

    def store(peer, picked):
        start = 0
        for ref in send_refs:
            ref[peer] = picked[start : start + ref.shape[1]]
            start += ref.shape[1]

    pick_rows(index, rows_ref[:tail, :], store)


def relay_sends(rows, peers, sizes):
    length = rows.shape[1]
    return pl.pallas_call(
        relay_kernel,
        out_shape=[jax.ShapeDtypeStruct((peers, size * SUB, length), BF16) for size in sizes],
        compiler_params=pltpu.CompilerParams(vmem_limit_bytes=SMALL),
        name="relay",
    )(rows)


def pair_kernel(geo, first, station_ref, count_ref, place_ref, own_ref, far_ref, weight_ref, lag_ref, *refs):
    out_ref = refs[-1]
    peers, cap, joint = geo
    group = pl.program_id(0) + first
    length = own_ref.shape[-1]
    half_len = length // 2

    rows = jnp.concatenate(
        [ref[...].reshape(peers * SUB, length) for ref in (own_ref, far_ref)], axis=0
    )
    width = rows.shape[0]
    many = TOGETHER * LANES
    for j in range(joint):
        for i in range(0, SUB, TOGETHER):
            picks = [
                one_hot(place_ref[m, j, i + n : i + n + 1, :], width)
                for m in range(2)
                for n in range(TOGETHER)
            ]
            members = jnp.dot(jnp.concatenate(picks, axis=0), rows, preferred_element_type=F32)
            halves = []
            for n in range(TOGETHER):
                a = members[n * LANES : (n + 1) * LANES]
                b = members[many + n * LANES : many + (n + 1) * LANES]
                re_a, im_a = a[:, :half_len], a[:, half_len:]
                re_b, im_b = b[:, :half_len], b[:, half_len:]
                tile = j * cap + group * SUB + i + n
                scale = weight_ref[pl.ds(station_ref[tile], 1), :]
                halves.append(
                    jnp.concatenate(
                        [
                            ((re_a * re_b + im_a * im_b) * scale).astype(BF16),
                            ((im_a * re_b - re_a * im_b) * scale).astype(BF16),
                        ],
                        axis=1,
                    )
                )
            cross = jnp.concatenate(halves, axis=0)
            lagged = jnp.dot(cross, lag_ref[...], preferred_element_type=F32)
            for n in range(TOGETHER):
                tile = j * cap + group * SUB + i + n
                piece = lagged[n * LANES : (n + 1) * LANES]
                slot = lax.broadcasted_iota(jnp.int32, piece.shape, 0)
                piece = jnp.where(slot < count_ref[tile], piece, 0.0)
                out_ref[j, (i + n) * LANES : (i + n + 1) * LANES, :] = piece[:, :LAGS]


def correlate(first, steps, geo, stations_of, counts, places, own, far, weight, lag_tab, previous):
    peers, cap, joint = geo
    length = own.shape[-1]
    in_specs = [
        pl.BlockSpec((2, joint, SUB, LANES), lambda i, *_: (0, 0, i + first, 0)),
        pl.BlockSpec((peers, SUB, length), lambda i, *_: (0, i + first, 0)),
        pl.BlockSpec((peers, SUB, length), lambda i, *_: (0, i, 0)),
        pl.BlockSpec(weight.shape, lambda i, *_: (0, 0)),
        pl.BlockSpec(lag_tab.shape, lambda i, *_: (0, 0)),
    ]
    args = [places, own, far, weight, lag_tab]
    aliases = {}
    if previous is not None:
        in_specs.append(pl.BlockSpec(memory_space=pl.ANY))
        args.append(previous)
        aliases = {7: 0}
    tiles = joint * steps * SUB
    macs = tiles * LANES * length * (2 * 2 * peers * SUB + lag_tab.shape[1])
    return pl.pallas_call(
        partial(pair_kernel, geo, first),
        grid_spec=pltpu.PrefetchScalarGridSpec(
            num_scalar_prefetch=2,
            grid=(steps,),
            in_specs=in_specs,
            out_specs=pl.BlockSpec((joint, SUB * LANES, LAGS), lambda i, *_: (0, i + first, 0)),
        ),
        out_shape=jax.ShapeDtypeStruct((joint, cap * LANES, LAGS), F32),
        input_output_aliases=aliases,
        compiler_params=pltpu.CompilerParams(vmem_limit_bytes=VMEM),
        cost_estimate=pl.CostEstimate(
            flops=2 * macs, bytes_accessed=tiles * LANES * LAGS * 4, transcendentals=0
        ),
        name="pairs",
    )(stations_of, counts, *args)


def add_across(power, step, owners):
    return power + lax.ppermute(power, "ev", [(i, i ^ step) for i in range(owners)])


def shards(windows, rotation, source_inverse, send_rows, tile_station, tile_count, pair_rows):
    ev_dev, _, _, length = windows.shape
    owners = lax.axis_size("ev")
    cap = send_rows.shape[1]
    tiles_dev = tile_station.shape[0]
    joint = tiles_dev // cap
    peers = owners // 2
    half = lax.axis_index("ev") // peers
    halves = [list(range(peers)), list(range(peers, owners))]
    across = [(i, (i + peers) % owners) for i in range(owners)]
    to_peers = partial(
        lax.all_to_all,
        axis_name="ev",
        split_axis=0,
        concat_axis=0,
        axis_index_groups=halves,
        tiled=True,
    )
    half_arg = half.astype(jnp.int32).reshape(1)

    rows, power = event_rows(
        half_arg, windows, rotation, source_inverse, send_rows, spectral_table(length)
    )
    swapped = lax.ppermute(rows, "ev", across)
    sends = own_sends(half_arg, rows, send_rows)
    step = 1
    while step < peers // 2:
        power = add_across(power, step, owners)
        step *= 2
    sends, power = lax.optimization_barrier((sends, power))
    power = add_across(power, step, owners)
    own = to_peers(sends)
    groups = cap // SUB
    parts = [groups * part // sum(SPLIT) for part in SPLIT[:-1]]
    sizes = parts + [groups - sum(parts)]
    sends = relay_sends(swapped, peers, sizes)

    sends, own, power = lax.optimization_barrier((sends, own, power))
    power = add_across(power, peers, owners)
    weight = 1.0 / (power / (ev_dev * owners) + epsilon)
    source = pair_rows // cap
    side = source // peers != half
    places = jnp.where(side, peers * SUB, 0) + source % peers * SUB + pair_rows % SUB
    places = places.reshape(2, joint, cap, LANES)
    lag_tab = lag_table(length, LAGS, LAGS + 1)
    geo = (peers, cap, joint)
    result = None
    first = 0
    for steps, send in zip(sizes, sends):
        far = to_peers(send)
        result = correlate(
            first, steps, geo, tile_station, tile_count, places, own, far, weight, lag_tab, result
        )
        first += steps
    return result.reshape(tiles_dev * LANES, LAGS)


def solution(mesh):
    in_specs = (
        P(("grp", "ev"), None, None, None),
        P(("grp", "ev"), None, None),
        P(("grp", "ev"), None),
        P(("grp", "ev"), None),
        P(("grp", "ev")),
        P(("grp", "ev")),
        P(None, ("grp", "ev")),
    )
    out_specs = P(("grp", "ev"), None)
    return jax.shard_map(shards, mesh=mesh, in_specs=in_specs, out_specs=out_specs, check_vma=False)
```

```python
from functools import partial
import math

import jax
import jax.numpy as jnp
import numpy as np
from jax import lax
from jax.experimental import pallas as pl
from jax.experimental.pallas import tpu as pltpu
from jax.sharding import PartitionSpec as P


LAGS = 255
SUB = 8
LANES = 128
SPLIT = (6, 2)
TOGETHER = 2
VMEM = 60 << 20
SMALL = 20 << 20

epsilon = 1e-06
F32 = jnp.float32
BF16 = jnp.bfloat16


def spectral_table(length):
    half_len = length // 2
    samples = np.arange(length)[:, None]
    frequency = np.arange(half_len)[None, :]
    angles = (samples * frequency % length) * (2.0 * math.pi / length)
    factor = 1.0 / math.sqrt(length)
    table = np.concatenate([np.cos(angles) * factor, -np.sin(angles) * factor], axis=1)
    return jnp.asarray(table.astype(np.float32)).astype(BF16)


def lag_table(length, lag_count, width):
    half_len = length // 2
    frequency = np.arange(half_len)[:, None]
    shifts = np.arange(lag_count)[None, :] - lag_count // 2
    angles = (frequency * shifts % length) * (2.0 * math.pi / length)
    factor = 1.0 / math.sqrt(half_len)
    table = np.concatenate([np.cos(angles) * factor, -np.sin(angles) * factor], axis=0)
    table = np.pad(table, ((0, 0), (0, width - lag_count)))
    return jnp.asarray(table.astype(np.float32)).astype(BF16)


def column(values):
    return jnp.transpose(jnp.broadcast_to(values, (LANES, LANES)))


def one_hot(values, width):
    down = column(values)
    lane = lax.broadcasted_iota(jnp.int32, (LANES, LANES), 1)
    parts = [
        jnp.where(down == lane + LANES * j, 1.0, 0.0).astype(BF16) for j in range(width // LANES)
    ]
    return jnp.concatenate(parts, axis=1)


def spectra_kernel(steps, half_ref, win_ref, rot_ref, inv_ref, table_ref, index_ref, rows_ref, power_ref):
    step = pl.program_id(0)
    events, comps, stations, length = win_ref.shape
    half_len = length // 2
    blocks = []
    turns = rot_ref[...].astype(F32)
    for e in range(events):
        turn = turns[:, e, :]
        for s in range(1, steps):
            turn = jnp.where(step == s, turns[:, s * events + e, :], turn)
        rot = jnp.transpose(turn)
        total = rot[:, 0:1] * win_ref[e, 0].astype(F32)
        for c in range(1, comps):
            total += rot[:, c : c + 1] * win_ref[e, c].astype(F32)
        blocks.append(total.astype(BF16))
    transverse = jnp.concatenate(blocks, axis=0)
    spectrum = jnp.dot(transverse, table_ref[...], preferred_element_type=F32)
    gains = inv_ref[...].astype(F32)
    power = jnp.zeros((stations, half_len), F32)
    for e in range(events):
        re_in = spectrum[e * stations : (e + 1) * stations, :half_len]
        im_in = spectrum[e * stations : (e + 1) * stations, half_len:]
        gain = gains[e : e + 1, :]
        for s in range(1, steps):
            gain = jnp.where(step == s, gains[s * events + e : s * events + e + 1, :], gain)
        re_g, im_g = gain[:, :half_len], gain[:, half_len:]
        re = re_in * re_g - im_in * im_g
        im = re_in * im_g + im_in * re_g
        power += re * re + im * im
        base = pl.multiple_of((step * events + e) * stations, stations)
        rows_ref[pl.ds(base, stations), :half_len] = re.astype(BF16)
        rows_ref[pl.ds(base, stations), half_len:] = im.astype(BF16)

    @pl.when(step == 0)
    def _():
        power_ref[...] = power
        owners, cap = index_ref.shape
        peers = owners // 2
        other = pl.multiple_of((1 - half_ref[0]) * peers, peers)
        wanted = index_ref[pl.ds(other, peers), :]
        tail = rows_ref.shape[0] - peers
        rows_ref[tail:, :] = jnp.zeros((peers, length), BF16)
        rows_ref[tail:, :cap] = (wanted // LANES).astype(F32).astype(BF16)
        rows_ref[tail:, LANES : LANES + cap] = (wanted % LANES).astype(F32).astype(BF16)

    @pl.when(step > 0)
    def _():
        power_ref[...] += power


def event_rows(half, windows, rotation, source_inverse, send_rows, table):
    ev_dev, comps, stations, length = windows.shape
    owners, cap = send_rows.shape
    steps = 2 if ev_dev % 2 == 0 else 1
    events = ev_dev // steps
    total = ev_dev * stations + owners // 2
    whole = lambda *shape: pl.BlockSpec(shape, lambda i, *_: (0,) * len(shape))
    return pl.pallas_call(
        partial(spectra_kernel, steps),
        grid_spec=pltpu.PrefetchScalarGridSpec(
            num_scalar_prefetch=1,
            grid=(steps,),
            in_specs=[
                pl.BlockSpec((events, comps, stations, length), lambda i, *_: (i, 0, 0, 0)),
                whole(comps, ev_dev, stations),
                whole(ev_dev, length),
                whole(length, length),
                whole(owners, cap),
            ],
            out_specs=[whole(total, length), whole(stations, length // 2)],
        ),
        out_shape=[
            jax.ShapeDtypeStruct((total, length), BF16),
            jax.ShapeDtypeStruct((stations, length // 2), F32),
        ],
        compiler_params=pltpu.CompilerParams(vmem_limit_bytes=VMEM),
        name="spectra",
    )(half, windows, rotation.swapaxes(0, 1), source_inverse, table, send_rows)


def pick_rows(index, rows, store):
    peers, cap = index.shape
    lines = LANES // cap
    for first in range(0, peers, lines):
        line = jnp.concatenate([index[first + j : first + j + 1, :] for j in range(lines)], axis=1)
        picked = jnp.dot(one_hot(line, rows.shape[0]), rows, preferred_element_type=F32)
        picked = picked.astype(BF16)
        for j in range(lines):
            store(first + j, picked[j * cap : (j + 1) * cap])


def spread(index, rows, refs, skips):
    def store(peer, picked):
        start = 0
        for ref, skip in zip(refs, skips):
            count = ref.shape[1] - skip
            ref[peer, skip:, :] = picked[start : start + count]
            start += count

    pick_rows(index, rows, store)


def own_kernel(half_ref, rows_ref, index_ref, *send_refs):
    peers = send_refs[0].shape[0]
    mine = pl.multiple_of(half_ref[0] * peers, peers)
    spread(index_ref[pl.ds(mine, peers), :], rows_ref[...], send_refs, (0, 0))


def own_sends(half, rows, send_rows, sizes):
    owners, cap = send_rows.shape
    peers = owners // 2
    length = rows.shape[1]
    whole = lambda *shape: pl.BlockSpec(shape, lambda i, *_: (0,) * len(shape))
    shapes = [(peers, size * SUB, length) for size in sizes]
    return pl.pallas_call(
        own_kernel,
        grid_spec=pltpu.PrefetchScalarGridSpec(
            num_scalar_prefetch=1,
            grid=(1,),
            in_specs=[whole(rows.shape[0] - peers, length), whole(owners, cap)],
            out_specs=[whole(*shape) for shape in shapes],
        ),
        out_shape=[jax.ShapeDtypeStruct(shape, BF16) for shape in shapes],
        compiler_params=pltpu.CompilerParams(vmem_limit_bytes=SMALL),
        name="own",
    )(half, rows, send_rows)


def relay_kernel(cap, rows_ref, rest_ref, first_ref, last_ref):
    peers, kept, _ = rest_ref.shape
    tail = rows_ref.shape[0] - peers
    digits = rows_ref[tail:, :].astype(F32).astype(jnp.int32)
    index = digits[:, :cap] * LANES + digits[:, LANES : LANES + cap]
    spread(index, rows_ref[:tail, :], (first_ref, last_ref), (0, kept))
    last_ref[:, :kept, :] = rest_ref[...]


def relay_sends(rows, rest, cap):
    peers, kept, length = rest.shape
    shapes = [(peers, cap - kept, length), (peers, 2 * kept, length)]
    return pl.pallas_call(
        partial(relay_kernel, cap),
        out_shape=[jax.ShapeDtypeStruct(shape, BF16) for shape in shapes],
        compiler_params=pltpu.CompilerParams(vmem_limit_bytes=SMALL),
        name="relay",
    )(rows, rest)


def place_kernel(peers, half_ref, pair_ref, place_ref):
    cap = pair_ref.shape[2]
    pair = pair_ref[...]
    source = lax.div(pair, cap)
    side = lax.div(source, peers) != half_ref[0]
    offset = jnp.where(side, peers * SUB, 0)
    place_ref[...] = offset + lax.rem(source, peers) * SUB + lax.rem(pair, SUB)


def place_rows(half, pairs, peers):
    return pl.pallas_call(
        partial(place_kernel, peers),
        in_specs=[pl.BlockSpec(memory_space=pltpu.SMEM), pl.BlockSpec(memory_space=pltpu.VMEM)],
        out_shape=jax.ShapeDtypeStruct(pairs.shape, jnp.int32),
        compiler_params=pltpu.CompilerParams(vmem_limit_bytes=SMALL),
        name="places",
    )(half, pairs)


def pair_kernel(geo, first, station_ref, count_ref, place_ref, own_ref, far_ref, weight_ref, lag_ref, *refs):
    out_ref = refs[-1]
    peers, cap, joint = geo
    group = pl.program_id(0) + first
    length = own_ref.shape[-1]
    half_len = length // 2

    rows = jnp.concatenate(
        [ref[...].reshape(peers * SUB, length) for ref in (own_ref, far_ref)], axis=0
    )
    width = rows.shape[0]
    many = TOGETHER * LANES
    for j in range(joint):
        for i in range(0, SUB, TOGETHER):
            picks = [
                one_hot(place_ref[m, j, i + n : i + n + 1, :], width)
                for m in range(2)
                for n in range(TOGETHER)
            ]
            members = jnp.dot(jnp.concatenate(picks, axis=0), rows, preferred_element_type=F32)
            halves = []
            for n in range(TOGETHER):
                a = members[n * LANES : (n + 1) * LANES]
                b = members[many + n * LANES : many + (n + 1) * LANES]
                re_a, im_a = a[:, :half_len], a[:, half_len:]
                re_b, im_b = b[:, :half_len], b[:, half_len:]
                tile = j * cap + group * SUB + i + n
                scale = weight_ref[pl.ds(station_ref[tile], 1), :]
                halves.append(
                    jnp.concatenate(
                        [
                            ((re_a * re_b + im_a * im_b) * scale).astype(BF16),
                            ((im_a * re_b - re_a * im_b) * scale).astype(BF16),
                        ],
                        axis=1,
                    )
                )
            cross = jnp.concatenate(halves, axis=0)
            lagged = jnp.dot(cross, lag_ref[...], preferred_element_type=F32)
            for n in range(TOGETHER):
                tile = j * cap + group * SUB + i + n
                piece = lagged[n * LANES : (n + 1) * LANES]
                slot = lax.broadcasted_iota(jnp.int32, piece.shape, 0)
                piece = jnp.where(slot < count_ref[tile], piece, 0.0)
                out_ref[j, (i + n) * LANES : (i + n + 1) * LANES, :] = piece[:, :LAGS]


def correlate(first, steps, geo, stations_of, counts, places, own, far, weight, lag_tab, previous):
    (own, own_at), (far, far_at) = own, far
    peers, cap, joint = geo
    length = own.shape[-1]
    in_specs = [
        pl.BlockSpec((2, joint, SUB, LANES), lambda i, *_: (0, 0, i + first, 0)),
        pl.BlockSpec((peers, SUB, length), lambda i, *_: (0, i + own_at, 0)),
        pl.BlockSpec((peers, SUB, length), lambda i, *_: (0, i + far_at, 0)),
        pl.BlockSpec(weight.shape, lambda i, *_: (0, 0)),
        pl.BlockSpec(lag_tab.shape, lambda i, *_: (0, 0)),
    ]
    args = [places, own, far, weight, lag_tab]
    aliases = {}
    if previous is not None:
        in_specs.append(pl.BlockSpec(memory_space=pl.ANY))
        args.append(previous)
        aliases = {7: 0}
    tiles = joint * steps * SUB
    macs = tiles * LANES * length * (2 * 2 * peers * SUB + lag_tab.shape[1])
    return pl.pallas_call(
        partial(pair_kernel, geo, first),
        grid_spec=pltpu.PrefetchScalarGridSpec(
            num_scalar_prefetch=2,
            grid=(steps,),
            in_specs=in_specs,
            out_specs=pl.BlockSpec((joint, SUB * LANES, LAGS), lambda i, *_: (0, i + first, 0)),
        ),
        out_shape=jax.ShapeDtypeStruct((joint, cap * LANES, LAGS), F32),
        input_output_aliases=aliases,
        compiler_params=pltpu.CompilerParams(vmem_limit_bytes=VMEM),
        cost_estimate=pl.CostEstimate(
            flops=2 * macs, bytes_accessed=tiles * LANES * LAGS * 4, transcendentals=0
        ),
        name="pairs",
    )(stations_of, counts, *args)


def add_across(power, step, owners):
    return power + lax.ppermute(power, "ev", [(i, i ^ step) for i in range(owners)])


def shards(windows, rotation, source_inverse, send_rows, tile_station, tile_count, pair_rows):
    ev_dev, _, _, length = windows.shape
    owners = lax.axis_size("ev")
    cap = send_rows.shape[1]
    tiles_dev = tile_station.shape[0]
    joint = tiles_dev // cap
    peers = owners // 2
    half = lax.axis_index("ev") // peers
    halves = [list(range(peers)), list(range(peers, owners))]
    across = [(i, (i + peers) % owners) for i in range(owners)]
    to_peers = partial(
        lax.all_to_all,
        axis_name="ev",
        split_axis=0,
        concat_axis=0,
        axis_index_groups=halves,
        tiled=True,
    )
    half_arg = half.astype(jnp.int32).reshape(1)

    rows, power = event_rows(
        half_arg, windows, rotation, source_inverse, send_rows, spectral_table(length)
    )
    groups = cap // SUB
    early = groups * SPLIT[0] // sum(SPLIT)
    sizes = (early, groups - early)
    swapped = lax.ppermute(rows, "ev", across)
    send, rest = own_sends(half_arg, rows, send_rows, sizes)
    step = 1
    while step < peers // 2:
        power = add_across(power, step, owners)
        step *= 2
    send, power = lax.optimization_barrier((send, power))
    power = add_across(power, step, owners)
    own = to_peers(send)
    sends = relay_sends(swapped, rest, cap)
    sends, own, power = lax.optimization_barrier((sends, own, power))
    power = add_across(power, peers, owners)
    weight = 1.0 / (power / (ev_dev * owners) + epsilon)
    places = place_rows(half_arg, pair_rows.reshape(2, joint, cap, LANES), peers)
    lag_tab = lag_table(length, LAGS, LAGS + 1)
    geo = (peers, cap, joint)
    far = to_peers(sends[0])
    last = to_peers(sends[1])
    run = partial(correlate, geo=geo, stations_of=tile_station, counts=tile_count, places=places)
    run = partial(run, weight=weight, lag_tab=lag_tab)
    result = run(0, sizes[0], own=(own, 0), far=(far, 0), previous=None)
    result = run(early, sizes[1], own=(last, 0), far=(last, sizes[1]), previous=result)
    return result.reshape(tiles_dev * LANES, LAGS)


def solution(mesh):
    in_specs = (
        P(("grp", "ev"), None, None, None),
        P(("grp", "ev"), None, None),
        P(("grp", "ev"), None),
        P(("grp", "ev"), None),
        P(("grp", "ev")),
        P(("grp", "ev")),
        P(None, ("grp", "ev")),
    )
    out_specs = P(("grp", "ev"), None)
    return jax.shard_map(shards, mesh=mesh, in_specs=in_specs, out_specs=out_specs, check_vma=False)
```

```python
from functools import partial
import math

import jax
import jax.numpy as jnp
import numpy as np
from jax import lax
from jax.experimental import pallas as pl
from jax.experimental.pallas import tpu as pltpu
from jax.sharding import PartitionSpec as P


LAGS = 255
SUB = 8
LANES = 128
SPLIT = (6, 2)
TOGETHER = 2
SMALL = 20 << 20

epsilon = 1e-06
F32 = jnp.float32
BF16 = jnp.bfloat16


def spectral_table(length):
    half_len = length // 2
    samples = np.arange(length)[:, None]
    frequency = np.arange(half_len)[None, :]
    angles = (samples * frequency % length) * (2.0 * math.pi / length)
    factor = 1.0 / math.sqrt(length)
    table = np.concatenate([np.cos(angles) * factor, -np.sin(angles) * factor], axis=1)
    return jnp.asarray(table.astype(np.float32)).astype(BF16)


def lag_table(length, lag_count, width):
    half_len = length // 2
    frequency = np.arange(half_len)[:, None]
    shifts = np.arange(lag_count)[None, :] - lag_count // 2
    angles = (frequency * shifts % length) * (2.0 * math.pi / length)
    factor = 1.0 / math.sqrt(half_len)
    table = np.concatenate([np.cos(angles) * factor, -np.sin(angles) * factor], axis=0)
    table = np.pad(table, ((0, 0), (0, width - lag_count)))
    return jnp.asarray(table.astype(np.float32)).astype(BF16)


def column(values):
    return jnp.transpose(jnp.broadcast_to(values, (LANES, LANES)))


def one_hot(values, width):
    down = column(values)
    lane = lax.broadcasted_iota(jnp.int32, (LANES, LANES), 1)
    parts = [
        jnp.where(down == lane + LANES * j, 1.0, 0.0).astype(BF16) for j in range(width // LANES)
    ]
    return jnp.concatenate(parts, axis=1)


def spectra_kernel(steps, half_ref, win_ref, rot_ref, inv_ref, table_ref, index_ref, rows_ref, power_ref):
    step = pl.program_id(0)
    events, comps, stations, length = win_ref.shape
    half_len = length // 2
    blocks = []
    turns = rot_ref[...].astype(F32)
    for e in range(events):
        turn = turns[:, e, :]
        for s in range(1, steps):
            turn = jnp.where(step == s, turns[:, s * events + e, :], turn)
        rot = jnp.transpose(turn)
        total = rot[:, 0:1] * win_ref[e, 0].astype(F32)
        for c in range(1, comps):
            total += rot[:, c : c + 1] * win_ref[e, c].astype(F32)
        blocks.append(total.astype(BF16))
    transverse = jnp.concatenate(blocks, axis=0)
    spectrum = jnp.dot(transverse, table_ref[...], preferred_element_type=F32)
    gains = inv_ref[...].astype(F32)
    power = jnp.zeros((stations, half_len), F32)
    for e in range(events):
        re_in = spectrum[e * stations : (e + 1) * stations, :half_len]
        im_in = spectrum[e * stations : (e + 1) * stations, half_len:]
        gain = gains[e : e + 1, :]
        for s in range(1, steps):
            gain = jnp.where(step == s, gains[s * events + e : s * events + e + 1, :], gain)
        re_g, im_g = gain[:, :half_len], gain[:, half_len:]
        re = re_in * re_g - im_in * im_g
        im = re_in * im_g + im_in * re_g
        power += re * re + im * im
        base = pl.multiple_of((step * events + e) * stations, stations)
        rows_ref[pl.ds(base, stations), :half_len] = re.astype(BF16)
        rows_ref[pl.ds(base, stations), half_len:] = im.astype(BF16)

    @pl.when(step == 0)
    def _():
        power_ref[...] = power
        owners, cap = index_ref.shape
        peers = owners // 2
        other = pl.multiple_of((1 - half_ref[0]) * peers, peers)
        wanted = index_ref[pl.ds(other, peers), :]
        tail = rows_ref.shape[0] - peers
        rows_ref[tail:, :] = jnp.zeros((peers, length), BF16)
        rows_ref[tail:, :cap] = (wanted // LANES).astype(F32).astype(BF16)
        rows_ref[tail:, LANES : LANES + cap] = (wanted % LANES).astype(F32).astype(BF16)

    @pl.when(step > 0)
    def _():
        power_ref[...] += power


def event_rows(half, windows, rotation, source_inverse, send_rows, table):
    ev_dev, comps, stations, length = windows.shape
    owners, cap = send_rows.shape
    steps = 2 if ev_dev % 2 == 0 else 1
    events = ev_dev // steps
    total = ev_dev * stations + owners // 2
    args = (windows, rotation.swapaxes(0, 1), source_inverse, table, send_rows)
    args = [pltpu.with_memory_space_constraint(x, pltpu.HBM) for x in args]
    whole = lambda *shape: pl.BlockSpec(shape, lambda i, *_: (0,) * len(shape))
    return pl.pallas_call(
        partial(spectra_kernel, steps),
        grid_spec=pltpu.PrefetchScalarGridSpec(
            num_scalar_prefetch=1,
            grid=(steps,),
            in_specs=[
                pl.BlockSpec((events, comps, stations, length), lambda i, *_: (i, 0, 0, 0)),
                whole(comps, ev_dev, stations),
                whole(ev_dev, length),
                whole(length, length),
                whole(owners, cap),
            ],
            out_specs=[whole(total, length), whole(stations, length // 2)],
        ),
        out_shape=[
            jax.ShapeDtypeStruct((total, length), BF16),
            jax.ShapeDtypeStruct((stations, length // 2), F32),
        ],
        compiler_params=pltpu.CompilerParams(vmem_limit_bytes=SMALL),
        name="spectra",
    )(half, *args)


def pick_rows(index, rows, store):
    peers, cap = index.shape
    lines = LANES // cap
    for first in range(0, peers, lines):
        line = jnp.concatenate([index[first + j : first + j + 1, :] for j in range(lines)], axis=1)
        picked = jnp.dot(one_hot(line, rows.shape[0]), rows, preferred_element_type=F32)
        picked = picked.astype(BF16)
        for j in range(lines):
            store(first + j, picked[j * cap : (j + 1) * cap])


def spread(index, rows, refs, skips):
    def store(peer, picked):
        start = 0
        for ref, skip in zip(refs, skips):
            count = ref.shape[1] - skip
            ref[peer, skip:, :] = picked[start : start + count]
            start += count

    pick_rows(index, rows, store)


def own_kernel(half_ref, rows_ref, index_ref, *send_refs):
    peers = send_refs[0].shape[0]
    mine = pl.multiple_of(half_ref[0] * peers, peers)
    spread(index_ref[pl.ds(mine, peers), :], rows_ref[...], send_refs, (0, 0))


def own_sends(half, rows, send_rows, sizes):
    owners, cap = send_rows.shape
    peers = owners // 2
    length = rows.shape[1]
    whole = lambda *shape: pl.BlockSpec(shape, lambda i, *_: (0,) * len(shape))
    shapes = [(peers, size * SUB, length) for size in sizes]
    return pl.pallas_call(
        own_kernel,
        grid_spec=pltpu.PrefetchScalarGridSpec(
            num_scalar_prefetch=1,
            grid=(1,),
            in_specs=[whole(rows.shape[0] - peers, length), whole(owners, cap)],
            out_specs=[whole(*shape) for shape in shapes],
        ),
        out_shape=[jax.ShapeDtypeStruct(shape, BF16) for shape in shapes],
        compiler_params=pltpu.CompilerParams(vmem_limit_bytes=SMALL),
        name="own",
    )(half, rows, send_rows)


def relay_kernel(cap, rows_ref, rest_ref, first_ref, last_ref):
    peers, kept, _ = rest_ref.shape
    tail = rows_ref.shape[0] - peers
    digits = rows_ref[tail:, :].astype(F32).astype(jnp.int32)
    index = digits[:, :cap] * LANES + digits[:, LANES : LANES + cap]
    spread(index, rows_ref[:tail, :], (first_ref, last_ref), (0, kept))
    last_ref[:, :kept, :] = rest_ref[...]


def relay_sends(rows, rest, cap):
    peers, kept, length = rest.shape
    shapes = [(peers, cap - kept, length), (peers, 2 * kept, length)]
    return pl.pallas_call(
        partial(relay_kernel, cap),
        out_shape=[jax.ShapeDtypeStruct(shape, BF16) for shape in shapes],
        compiler_params=pltpu.CompilerParams(vmem_limit_bytes=SMALL),
        name="relay",
    )(rows, rest)


def place_kernel(peers, half_ref, pair_ref, place_ref):
    cap = pair_ref.shape[2]
    pair = pair_ref[...]
    source = lax.div(pair, cap)
    side = lax.div(source, peers) != half_ref[0]
    offset = jnp.where(side, peers * SUB, 0)
    place_ref[...] = offset + lax.rem(source, peers) * SUB + lax.rem(pair, SUB)


def place_rows(half, pairs, peers):
    return pl.pallas_call(
        partial(place_kernel, peers),
        in_specs=[pl.BlockSpec(memory_space=pltpu.SMEM), pl.BlockSpec(memory_space=pltpu.VMEM)],
        out_shape=jax.ShapeDtypeStruct(pairs.shape, jnp.int32),
        compiler_params=pltpu.CompilerParams(vmem_limit_bytes=SMALL),
        name="places",
    )(half, pairs)


def pair_kernel(geo, first, station_ref, count_ref, place_ref, own_ref, far_ref, weight_ref, lag_ref, *refs):
    out_ref = refs[-1]
    peers, cap, joint = geo
    group = pl.program_id(0) + first
    length = own_ref.shape[-1]
    half_len = length // 2

    rows = jnp.concatenate(
        [ref[...].reshape(peers * SUB, length) for ref in (own_ref, far_ref)], axis=0
    )
    width = rows.shape[0]
    many = TOGETHER * LANES
    for j in range(joint):
        for i in range(0, SUB, TOGETHER):
            picks = [
                one_hot(place_ref[m, j, i + n : i + n + 1, :], width)
                for m in range(2)
                for n in range(TOGETHER)
            ]
            members = jnp.dot(jnp.concatenate(picks, axis=0), rows, preferred_element_type=F32)
            halves = []
            for n in range(TOGETHER):
                a = members[n * LANES : (n + 1) * LANES]
                b = members[many + n * LANES : many + (n + 1) * LANES]
                re_a, im_a = a[:, :half_len], a[:, half_len:]
                re_b, im_b = b[:, :half_len], b[:, half_len:]
                tile = j * cap + group * SUB + i + n
                scale = weight_ref[pl.ds(station_ref[tile], 1), :]
                halves.append(
                    jnp.concatenate(
                        [
                            ((re_a * re_b + im_a * im_b) * scale).astype(BF16),
                            ((im_a * re_b - re_a * im_b) * scale).astype(BF16),
                        ],
                        axis=1,
                    )
                )
            cross = jnp.concatenate(halves, axis=0)
            lagged = jnp.dot(cross, lag_ref[...], preferred_element_type=F32)
            for n in range(TOGETHER):
                tile = j * cap + group * SUB + i + n
                piece = lagged[n * LANES : (n + 1) * LANES]
                slot = lax.broadcasted_iota(jnp.int32, piece.shape, 0)
                piece = jnp.where(slot < count_ref[tile], piece, 0.0)
                out_ref[j, (i + n) * LANES : (i + n + 1) * LANES, :] = piece[:, :LAGS]


def correlate(first, steps, geo, stations_of, counts, places, own, far, weight, lag_tab, previous):
    (own, own_at), (far, far_at) = own, far
    peers, cap, joint = geo
    length = own.shape[-1]
    in_specs = [
        pl.BlockSpec((2, joint, SUB, LANES), lambda i, *_: (0, 0, i + first, 0)),
        pl.BlockSpec((peers, SUB, length), lambda i, *_: (0, i + own_at, 0)),
        pl.BlockSpec((peers, SUB, length), lambda i, *_: (0, i + far_at, 0)),
        pl.BlockSpec(weight.shape, lambda i, *_: (0, 0)),
        pl.BlockSpec(lag_tab.shape, lambda i, *_: (0, 0)),
    ]
    args = [places, own, far, weight, lag_tab]
    aliases = {}
    if previous is not None:
        in_specs.append(pl.BlockSpec(memory_space=pl.ANY))
        args.append(previous)
        aliases = {7: 0}
    tiles = joint * steps * SUB
    macs = tiles * LANES * length * (2 * 2 * peers * SUB + lag_tab.shape[1])
    return pl.pallas_call(
        partial(pair_kernel, geo, first),
        grid_spec=pltpu.PrefetchScalarGridSpec(
            num_scalar_prefetch=2,
            grid=(steps,),
            in_specs=in_specs,
            out_specs=pl.BlockSpec((joint, SUB * LANES, LAGS), lambda i, *_: (0, i + first, 0)),
        ),
        out_shape=jax.ShapeDtypeStruct((joint, cap * LANES, LAGS), F32),
        input_output_aliases=aliases,
        compiler_params=pltpu.CompilerParams(vmem_limit_bytes=SMALL),
        cost_estimate=pl.CostEstimate(
            flops=2 * macs, bytes_accessed=tiles * LANES * LAGS * 4, transcendentals=0
        ),
        name="pairs",
    )(stations_of, counts, *args)


def add_across(power, step, owners):
    return power + lax.ppermute(power, "ev", [(i, i ^ step) for i in range(owners)])


def shards(windows, rotation, source_inverse, send_rows, tile_station, tile_count, pair_rows):
    ev_dev, _, _, length = windows.shape
    owners = lax.axis_size("ev")
    cap = send_rows.shape[1]
    tiles_dev = tile_station.shape[0]
    joint = tiles_dev // cap
    peers = owners // 2
    half = lax.axis_index("ev") // peers
    halves = [list(range(peers)), list(range(peers, owners))]
    across = [(i, (i + peers) % owners) for i in range(owners)]
    to_peers = partial(
        lax.all_to_all,
        axis_name="ev",
        split_axis=0,
        concat_axis=0,
        axis_index_groups=halves,
        tiled=True,
    )
    half_arg = half.astype(jnp.int32).reshape(1)

    rows, power = event_rows(
        half_arg, windows, rotation, source_inverse, send_rows, spectral_table(length)
    )
    groups = cap // SUB
    early = groups * SPLIT[0] // sum(SPLIT)
    sizes = (early, groups - early)
    swapped = lax.ppermute(rows, "ev", across)
    send, rest = own_sends(half_arg, rows, send_rows, sizes)
    step = 1
    while step < peers // 2:
        power = add_across(power, step, owners)
        step *= 2
    power = add_across(power, step, owners)
    own = to_peers(send)
    sends = relay_sends(swapped, rest, cap)
    sends, own, power = lax.optimization_barrier((sends, own, power))
    power = add_across(power, peers, owners)
    weight = 1.0 / (power / (ev_dev * owners) + epsilon)
    places = place_rows(half_arg, pair_rows.reshape(2, joint, cap, LANES), peers)
    lag_tab = lag_table(length, LAGS, LAGS + 1)
    geo = (peers, cap, joint)
    far = to_peers(sends[0])
    last = to_peers(sends[1])
    run = partial(correlate, geo=geo, stations_of=tile_station, counts=tile_count, places=places)
    run = partial(run, weight=weight, lag_tab=lag_tab)
    far = pltpu.with_memory_space_constraint(far, pltpu.HBM)
    result = run(0, sizes[0], own=(own, 0), far=(far, 0), previous=None)
    result = run(early, sizes[1], own=(last, 0), far=(last, sizes[1]), previous=result)
    return result.reshape(tiles_dev * LANES, LAGS)


def solution(mesh):
    in_specs = (
        P(("grp", "ev"), None, None, None),
        P(("grp", "ev"), None, None),
        P(("grp", "ev"), None),
        P(("grp", "ev"), None),
        P(("grp", "ev")),
        P(("grp", "ev")),
        P(None, ("grp", "ev")),
    )
    out_specs = P(("grp", "ev"), None)
    return jax.shard_map(shards, mesh=mesh, in_specs=in_specs, out_specs=out_specs, check_vma=False)
```

```python
from functools import partial
import math

import jax
import jax.numpy as jnp
import numpy as np
from jax import lax
from jax.experimental import pallas as pl
from jax.experimental.pallas import tpu as pltpu
from jax.sharding import PartitionSpec as P


LAGS = 255
SUB = 8
LANES = 128
SPLIT = (6, 2)
TOGETHER = 2
SMALL = 20 << 20

epsilon = 1e-06
F32 = jnp.float32
BF16 = jnp.bfloat16


def spectral_table(length):
    half_len = length // 2
    samples = np.arange(length)[:, None]
    frequency = np.arange(half_len)[None, :]
    angles = (samples * frequency % length) * (2.0 * math.pi / length)
    factor = 1.0 / math.sqrt(length)
    table = np.concatenate([np.cos(angles) * factor, -np.sin(angles) * factor], axis=1)
    return jnp.asarray(table.astype(np.float32)).astype(BF16)


def lag_table(length, lag_count, width):
    half_len = length // 2
    frequency = np.arange(half_len)[:, None]
    shifts = np.arange(lag_count)[None, :] - lag_count // 2
    angles = (frequency * shifts % length) * (2.0 * math.pi / length)
    factor = 1.0 / math.sqrt(half_len)
    table = np.concatenate([np.cos(angles) * factor, -np.sin(angles) * factor], axis=0)
    table = np.pad(table, ((0, 0), (0, width - lag_count)))
    return jnp.asarray(table.astype(np.float32)).astype(BF16)


def column(values):
    return jnp.transpose(jnp.broadcast_to(values, (LANES, LANES)))


def one_hot(values, width):
    down = column(values)
    lane = lax.broadcasted_iota(jnp.int32, (LANES, LANES), 1)
    parts = [
        jnp.where(down == lane + LANES * j, 1.0, 0.0).astype(BF16) for j in range(width // LANES)
    ]
    return jnp.concatenate(parts, axis=1)


def spectra_kernel(steps, half_ref, win_ref, rot_ref, inv_ref, table_ref, index_ref, rows_ref, power_ref):
    step = pl.program_id(0)
    events, comps, stations, length = win_ref.shape
    half_len = length // 2
    blocks = []
    turns = rot_ref[...].astype(F32)
    for e in range(events):
        turn = turns[:, e, :]
        for s in range(1, steps):
            turn = jnp.where(step == s, turns[:, s * events + e, :], turn)
        rot = jnp.transpose(turn)
        total = rot[:, 0:1] * win_ref[e, 0].astype(F32)
        for c in range(1, comps):
            total += rot[:, c : c + 1] * win_ref[e, c].astype(F32)
        blocks.append(total.astype(BF16))
    transverse = jnp.concatenate(blocks, axis=0)
    spectrum = jnp.dot(transverse, table_ref[...], preferred_element_type=F32)
    gains = inv_ref[...].astype(F32)
    power = jnp.zeros((stations, half_len), F32)
    for e in range(events):
        re_in = spectrum[e * stations : (e + 1) * stations, :half_len]
        im_in = spectrum[e * stations : (e + 1) * stations, half_len:]
        gain = gains[e : e + 1, :]
        for s in range(1, steps):
            gain = jnp.where(step == s, gains[s * events + e : s * events + e + 1, :], gain)
        re_g, im_g = gain[:, :half_len], gain[:, half_len:]
        re = re_in * re_g - im_in * im_g
        im = re_in * im_g + im_in * re_g
        power += re * re + im * im
        base = pl.multiple_of((step * events + e) * stations, stations)
        rows_ref[pl.ds(base, stations), :half_len] = re.astype(BF16)
        rows_ref[pl.ds(base, stations), half_len:] = im.astype(BF16)

    @pl.when(step == 0)
    def _():
        power_ref[...] = power
        owners, cap = index_ref.shape
        peers = owners // 2
        other = pl.multiple_of((1 - half_ref[0]) * peers, peers)
        wanted = index_ref[pl.ds(other, peers), :]
        tail = rows_ref.shape[0] - peers
        rows_ref[tail:, :] = jnp.zeros((peers, length), BF16)
        rows_ref[tail:, :cap] = (wanted // LANES).astype(F32).astype(BF16)
        rows_ref[tail:, LANES : LANES + cap] = (wanted % LANES).astype(F32).astype(BF16)

    @pl.when(step > 0)
    def _():
        power_ref[...] += power


def event_rows(half, windows, rotation, source_inverse, send_rows, table):
    ev_dev, comps, stations, length = windows.shape
    owners, cap = send_rows.shape
    steps = 2 if ev_dev % 2 == 0 else 1
    events = ev_dev // steps
    total = ev_dev * stations + owners // 2
    args = (windows, rotation.swapaxes(0, 1), source_inverse, table, send_rows)
    args = [pltpu.with_memory_space_constraint(x, pltpu.HBM) for x in args]
    whole = lambda *shape: pl.BlockSpec(shape, lambda i, *_: (0,) * len(shape))
    return pl.pallas_call(
        partial(spectra_kernel, steps),
        grid_spec=pltpu.PrefetchScalarGridSpec(
            num_scalar_prefetch=1,
            grid=(steps,),
            in_specs=[
                pl.BlockSpec((events, comps, stations, length), lambda i, *_: (i, 0, 0, 0)),
                whole(comps, ev_dev, stations),
                whole(ev_dev, length),
                whole(length, length),
                whole(owners, cap),
            ],
            out_specs=[whole(total, length), whole(stations, length // 2)],
        ),
        out_shape=[
            jax.ShapeDtypeStruct((total, length), BF16),
            jax.ShapeDtypeStruct((stations, length // 2), F32),
        ],
        compiler_params=pltpu.CompilerParams(vmem_limit_bytes=SMALL),
        name="spectra",
    )(half, *args)


def pick_rows(index, rows, store):
    peers, cap = index.shape
    lines = LANES // cap
    for first in range(0, peers, lines):
        line = jnp.concatenate([index[first + j : first + j + 1, :] for j in range(lines)], axis=1)
        picked = jnp.dot(one_hot(line, rows.shape[0]), rows, preferred_element_type=F32)
        picked = picked.astype(BF16)
        for j in range(lines):
            store(first + j, picked[j * cap : (j + 1) * cap])


def spread(index, rows, refs, skips):
    def store(peer, picked):
        start = 0
        for ref, skip in zip(refs, skips):
            count = ref.shape[1] - skip
            ref[peer, skip:, :] = picked[start : start + count]
            start += count

    pick_rows(index, rows, store)


def own_kernel(half_ref, rows_ref, index_ref, *send_refs):
    peers = send_refs[0].shape[0]
    mine = pl.multiple_of(half_ref[0] * peers, peers)
    spread(index_ref[pl.ds(mine, peers), :], rows_ref[...], send_refs, (0, 0))


def own_sends(half, rows, send_rows, sizes):
    owners, cap = send_rows.shape
    peers = owners // 2
    length = rows.shape[1]
    whole = lambda *shape: pl.BlockSpec(shape, lambda i, *_: (0,) * len(shape))
    shapes = [(peers, size * SUB, length) for size in sizes]
    return pl.pallas_call(
        own_kernel,
        grid_spec=pltpu.PrefetchScalarGridSpec(
            num_scalar_prefetch=1,
            grid=(1,),
            in_specs=[whole(rows.shape[0] - peers, length), whole(owners, cap)],
            out_specs=[whole(*shape) for shape in shapes],
        ),
        out_shape=[jax.ShapeDtypeStruct(shape, BF16) for shape in shapes],
        compiler_params=pltpu.CompilerParams(vmem_limit_bytes=SMALL),
        name="own",
    )(half, rows, send_rows)


def relay_kernel(cap, rows_ref, rest_ref, first_ref, last_ref):
    peers, kept, _ = rest_ref.shape
    tail = rows_ref.shape[0] - peers
    digits = rows_ref[tail:, :].astype(F32).astype(jnp.int32)
    index = digits[:, :cap] * LANES + digits[:, LANES : LANES + cap]
    spread(index, rows_ref[:tail, :], (first_ref, last_ref), (0, kept))
    last_ref[:, :kept, :] = rest_ref[...]


def relay_sends(rows, rest, cap):
    peers, kept, length = rest.shape
    shapes = [(peers, cap - kept, length), (peers, 2 * kept, length)]
    return pl.pallas_call(
        partial(relay_kernel, cap),
        out_shape=[jax.ShapeDtypeStruct(shape, BF16) for shape in shapes],
        compiler_params=pltpu.CompilerParams(vmem_limit_bytes=SMALL),
        name="relay",
    )(rows, rest)


def place_kernel(peers, half_ref, pair_ref, place_ref):
    cap = pair_ref.shape[2]
    pair = pair_ref[...]
    source = lax.div(pair, cap)
    side = lax.div(source, peers) != half_ref[0]
    offset = jnp.where(side, peers * SUB, 0)
    place_ref[...] = offset + lax.rem(source, peers) * SUB + lax.rem(pair, SUB)


def place_rows(half, pairs, peers):
    return pl.pallas_call(
        partial(place_kernel, peers),
        in_specs=[pl.BlockSpec(memory_space=pltpu.SMEM), pl.BlockSpec(memory_space=pltpu.VMEM)],
        out_shape=jax.ShapeDtypeStruct(pairs.shape, jnp.int32),
        compiler_params=pltpu.CompilerParams(vmem_limit_bytes=SMALL),
        name="places",
    )(half, pairs)


def pair_kernel(geo, first, station_ref, count_ref, place_ref, own_ref, far_ref, weight_ref, lag_ref, *refs):
    out_ref = refs[-1]
    peers, cap, joint = geo
    group = pl.program_id(0) + first
    length = own_ref.shape[-1]
    half_len = length // 2

    rows = jnp.concatenate(
        [ref[...].reshape(peers * SUB, length) for ref in (own_ref, far_ref)], axis=0
    )
    width = rows.shape[0]
    many = TOGETHER * LANES
    for j in range(joint):
        for i in range(0, SUB, TOGETHER):
            picks = [
                one_hot(place_ref[m, j, i + n : i + n + 1, :], width)
                for m in range(2)
                for n in range(TOGETHER)
            ]
            members = jnp.dot(jnp.concatenate(picks, axis=0), rows, preferred_element_type=F32)
            halves = []
            for n in range(TOGETHER):
                a = members[n * LANES : (n + 1) * LANES]
                b = members[many + n * LANES : many + (n + 1) * LANES]
                re_a, im_a = a[:, :half_len], a[:, half_len:]
                re_b, im_b = b[:, :half_len], b[:, half_len:]
                tile = j * cap + group * SUB + i + n
                scale = weight_ref[pl.ds(station_ref[tile], 1), :]
                halves.append(
                    jnp.concatenate(
                        [
                            ((re_a * re_b + im_a * im_b) * scale).astype(BF16),
                            ((im_a * re_b - re_a * im_b) * scale).astype(BF16),
                        ],
                        axis=1,
                    )
                )
            cross = jnp.concatenate(halves, axis=0)
            lagged = jnp.dot(cross, lag_ref[...], preferred_element_type=F32)
            for n in range(TOGETHER):
                tile = j * cap + group * SUB + i + n
                piece = lagged[n * LANES : (n + 1) * LANES]
                slot = lax.broadcasted_iota(jnp.int32, piece.shape, 0)
                piece = jnp.where(slot < count_ref[tile], piece, 0.0)
                out_ref[j, (i + n) * LANES : (i + n + 1) * LANES, :] = piece[:, :LAGS]


def correlate(first, steps, geo, stations_of, counts, places, own, far, weight, lag_tab, previous):
    (own, own_at), (far, far_at) = own, far
    peers, cap, joint = geo
    length = own.shape[-1]
    in_specs = [
        pl.BlockSpec((2, joint, SUB, LANES), lambda i, *_: (0, 0, i + first, 0)),
        pl.BlockSpec((peers, SUB, length), lambda i, *_: (0, i + own_at, 0)),
        pl.BlockSpec((peers, SUB, length), lambda i, *_: (0, i + far_at, 0)),
        pl.BlockSpec(weight.shape, lambda i, *_: (0, 0)),
        pl.BlockSpec(lag_tab.shape, lambda i, *_: (0, 0)),
    ]
    args = [places, own, far, weight, lag_tab]
    aliases = {}
    if previous is not None:
        in_specs.append(pl.BlockSpec(memory_space=pl.ANY))
        args.append(previous)
        aliases = {7: 0}
    tiles = joint * steps * SUB
    macs = tiles * LANES * length * (2 * 2 * peers * SUB + lag_tab.shape[1])
    return pl.pallas_call(
        partial(pair_kernel, geo, first),
        grid_spec=pltpu.PrefetchScalarGridSpec(
            num_scalar_prefetch=2,
            grid=(steps,),
            in_specs=in_specs,
            out_specs=pl.BlockSpec((joint, SUB * LANES, LAGS), lambda i, *_: (0, i + first, 0)),
        ),
        out_shape=jax.ShapeDtypeStruct((joint, cap * LANES, LAGS), F32),
        input_output_aliases=aliases,
        compiler_params=pltpu.CompilerParams(vmem_limit_bytes=SMALL),
        cost_estimate=pl.CostEstimate(
            flops=2 * macs, bytes_accessed=tiles * LANES * LAGS * 4, transcendentals=0
        ),
        name="pairs",
    )(stations_of, counts, *args)


def pair_up(value, step, owners):
    return lax.ppermute(value, "ev", [(i, i ^ step) for i in range(owners)])


def shards(windows, rotation, source_inverse, send_rows, tile_station, tile_count, pair_rows):
    ev_dev, _, stations, length = windows.shape
    owners = lax.axis_size("ev")
    cap = send_rows.shape[1]
    tiles_dev = tile_station.shape[0]
    joint = tiles_dev // cap
    peers = owners // 2
    half = lax.axis_index("ev") // peers
    halves = [list(range(peers)), list(range(peers, owners))]
    across = [(i, (i + peers) % owners) for i in range(owners)]
    to_peers = partial(
        lax.all_to_all,
        axis_name="ev",
        split_axis=0,
        concat_axis=0,
        axis_index_groups=halves,
        tiled=True,
    )
    half_arg = half.astype(jnp.int32).reshape(1)

    rows, power = event_rows(
        half_arg, windows, rotation, source_inverse, send_rows, spectral_table(length)
    )
    groups = cap // SUB
    early = groups * SPLIT[0] // sum(SPLIT)
    sizes = (early, groups - early)
    swapped = lax.ppermute(rows, "ev", across)
    send, rest = own_sends(half_arg, rows, send_rows, sizes)
    stations = power.shape[0]
    share = stations // 2
    low = lax.axis_index("ev") % 2 == 0
    parts = power[:share], power[share:]
    kept, passed = (jnp.where(low, *parts), jnp.where(low, *parts[::-1]))
    part = kept + pair_up(passed, 1, owners)
    step = 2
    while step < peers:
        part += pair_up(part, step, owners)
        step *= 2
    own = to_peers(send)
    sends = relay_sends(swapped, rest, cap)
    sends = [pltpu.with_memory_space_constraint(send, pltpu.HBM) for send in sends]
    sends, own, part = lax.optimization_barrier((sends, own, part))
    part += pair_up(part, peers, owners)
    twin = pair_up(part, 1, owners)
    power = jnp.concatenate([jnp.where(low, part, twin), jnp.where(low, twin, part)], axis=0)
    weight = 1.0 / (power / (ev_dev * owners) + epsilon)
    places = place_rows(half_arg, pair_rows.reshape(2, joint, cap, LANES), peers)
    lag_tab = lag_table(length, LAGS, LAGS + 1)
    geo = (peers, cap, joint)
    far = to_peers(sends[0])
    last = to_peers(sends[1])
    run = partial(correlate, geo=geo, stations_of=tile_station, counts=tile_count, places=places)
    run = partial(run, weight=weight, lag_tab=lag_tab)
    far = pltpu.with_memory_space_constraint(far, pltpu.HBM)
    result = run(0, sizes[0], own=(own, 0), far=(far, 0), previous=None)
    result = run(early, sizes[1], own=(last, 0), far=(last, sizes[1]), previous=result)
    return result.reshape(tiles_dev * LANES, LAGS)


def solution(mesh):
    in_specs = (
        P(("grp", "ev"), None, None, None),
        P(("grp", "ev"), None, None),
        P(("grp", "ev"), None),
        P(("grp", "ev"), None),
        P(("grp", "ev")),
        P(("grp", "ev")),
        P(None, ("grp", "ev")),
    )
    out_specs = P(("grp", "ev"), None)
    return jax.shard_map(shards, mesh=mesh, in_specs=in_specs, out_specs=out_specs, check_vma=False)
```

```python
from functools import partial
import math

import jax
import jax.numpy as jnp
import numpy as np
from jax import lax
from jax.experimental import pallas as pl
from jax.experimental.pallas import tpu as pltpu
from jax.sharding import PartitionSpec as P


LAGS = 255
SUB = 8
LANES = 128
SPLIT = (6, 2)
TOGETHER = 8
SMALL = 20 << 20

epsilon = 1e-06
F32 = jnp.float32
BF16 = jnp.bfloat16


def spectral_table(length):
    half_len = length // 2
    samples = np.arange(length)[:, None]
    frequency = np.arange(half_len)[None, :]
    angles = (samples * frequency % length) * (2.0 * math.pi / length)
    factor = 1.0 / math.sqrt(length)
    table = np.concatenate([np.cos(angles) * factor, -np.sin(angles) * factor], axis=1)
    return jnp.asarray(table.astype(np.float32)).astype(BF16)


def lag_table(length, lag_count, width):
    half_len = length // 2
    frequency = np.arange(half_len)[:, None]
    shifts = np.arange(lag_count)[None, :] - lag_count // 2
    angles = (frequency * shifts % length) * (2.0 * math.pi / length)
    factor = 1.0 / math.sqrt(half_len)
    table = np.concatenate([np.cos(angles) * factor, -np.sin(angles) * factor], axis=0)
    table = np.pad(table, ((0, 0), (0, width - lag_count)))
    return jnp.asarray(table.astype(np.float32)).astype(BF16)


def column(values):
    return jnp.transpose(jnp.broadcast_to(values, (LANES, LANES)))


def one_hot(values, width):
    down = column(values)
    lane = lax.broadcasted_iota(jnp.int32, (LANES, LANES), 1)
    parts = [
        jnp.where(down == lane + LANES * j, 1.0, 0.0).astype(BF16) for j in range(width // LANES)
    ]
    return jnp.concatenate(parts, axis=1)


def spectra_kernel(steps, half_ref, win_ref, rot_ref, inv_ref, table_ref, index_ref, rows_ref, power_ref):
    step = pl.program_id(0)
    events, comps, stations, length = win_ref.shape
    half_len = length // 2
    blocks = []
    turns = rot_ref[...].astype(F32)
    for e in range(events):
        turn = turns[:, e, :]
        for s in range(1, steps):
            turn = jnp.where(step == s, turns[:, s * events + e, :], turn)
        rot = jnp.transpose(turn)
        total = rot[:, 0:1] * win_ref[e, 0].astype(F32)
        for c in range(1, comps):
            total += rot[:, c : c + 1] * win_ref[e, c].astype(F32)
        blocks.append(total.astype(BF16))
    transverse = jnp.concatenate(blocks, axis=0)
    spectrum = jnp.dot(transverse, table_ref[...], preferred_element_type=F32)
    gains = inv_ref[...].astype(F32)
    power = jnp.zeros((stations, half_len), F32)
    for e in range(events):
        re_in = spectrum[e * stations : (e + 1) * stations, :half_len]
        im_in = spectrum[e * stations : (e + 1) * stations, half_len:]
        gain = gains[e : e + 1, :]
        for s in range(1, steps):
            gain = jnp.where(step == s, gains[s * events + e : s * events + e + 1, :], gain)
        re_g, im_g = gain[:, :half_len], gain[:, half_len:]
        re = re_in * re_g - im_in * im_g
        im = re_in * im_g + im_in * re_g
        power += re * re + im * im
        base = pl.multiple_of((step * events + e) * stations, stations)
        rows_ref[pl.ds(base, stations), :half_len] = re.astype(BF16)
        rows_ref[pl.ds(base, stations), half_len:] = im.astype(BF16)

    @pl.when(step == 0)
    def _():
        power_ref[...] = power
        owners, cap = index_ref.shape
        peers = owners // 2
        other = pl.multiple_of((1 - half_ref[0]) * peers, peers)
        wanted = index_ref[pl.ds(other, peers), :]
        tail = rows_ref.shape[0] - peers
        rows_ref[tail:, :] = jnp.zeros((peers, length), BF16)
        rows_ref[tail:, :cap] = (wanted // LANES).astype(F32).astype(BF16)
        rows_ref[tail:, LANES : LANES + cap] = (wanted % LANES).astype(F32).astype(BF16)

    @pl.when(step > 0)
    def _():
        power_ref[...] += power


def event_rows(half, windows, rotation, source_inverse, send_rows, table):
    ev_dev, comps, stations, length = windows.shape
    owners, cap = send_rows.shape
    steps = 4 if ev_dev % 4 == 0 else 1
    events = ev_dev // steps
    total = ev_dev * stations + owners // 2
    args = (windows, rotation.swapaxes(0, 1), source_inverse, table, send_rows)
    args = [pltpu.with_memory_space_constraint(x, pltpu.HBM) for x in args]
    whole = lambda *shape: pl.BlockSpec(shape, lambda i, *_: (0,) * len(shape))
    return pl.pallas_call(
        partial(spectra_kernel, steps),
        grid_spec=pltpu.PrefetchScalarGridSpec(
            num_scalar_prefetch=1,
            grid=(steps,),
            in_specs=[
                pl.BlockSpec((events, comps, stations, length), lambda i, *_: (i, 0, 0, 0)),
                whole(comps, ev_dev, stations),
                whole(ev_dev, length),
                whole(length, length),
                whole(owners, cap),
            ],
            out_specs=[whole(total, length), whole(stations, length // 2)],
        ),
        out_shape=[
            jax.ShapeDtypeStruct((total, length), BF16),
            jax.ShapeDtypeStruct((stations, length // 2), F32),
        ],
        compiler_params=pltpu.CompilerParams(vmem_limit_bytes=SMALL),
        name="spectra",
    )(half, *args)


def pick_rows(index, rows, store):
    peers, cap = index.shape
    lines = LANES // cap
    for first in range(0, peers, lines):
        line = jnp.concatenate([index[first + j : first + j + 1, :] for j in range(lines)], axis=1)
        picked = jnp.dot(one_hot(line, rows.shape[0]), rows, preferred_element_type=F32)
        picked = picked.astype(BF16)
        for j in range(lines):
            store(first + j, picked[j * cap : (j + 1) * cap])


def spread(index, rows, refs, skips):
    def store(peer, picked):
        start = 0
        for ref, skip in zip(refs, skips):
            count = ref.shape[1] - skip
            ref[peer, skip:, :] = picked[start : start + count]
            start += count

    pick_rows(index, rows, store)


def own_kernel(half_ref, rows_ref, index_ref, *send_refs):
    peers = send_refs[0].shape[0]
    mine = pl.multiple_of(half_ref[0] * peers, peers)
    spread(index_ref[pl.ds(mine, peers), :], rows_ref[...], send_refs, (0, 0))


def own_sends(half, rows, send_rows, sizes):
    owners, cap = send_rows.shape
    peers = owners // 2
    length = rows.shape[1]
    whole = lambda *shape: pl.BlockSpec(shape, lambda i, *_: (0,) * len(shape))
    shapes = [(peers, size * SUB, length) for size in sizes]
    return pl.pallas_call(
        own_kernel,
        grid_spec=pltpu.PrefetchScalarGridSpec(
            num_scalar_prefetch=1,
            grid=(1,),
            in_specs=[whole(rows.shape[0] - peers, length), whole(owners, cap)],
            out_specs=[whole(*shape) for shape in shapes],
        ),
        out_shape=[jax.ShapeDtypeStruct(shape, BF16) for shape in shapes],
        compiler_params=pltpu.CompilerParams(vmem_limit_bytes=SMALL),
        name="own",
    )(half, rows, send_rows)


def relay_kernel(cap, rows_ref, rest_ref, first_ref, last_ref):
    peers, kept, _ = rest_ref.shape
    tail = rows_ref.shape[0] - peers
    digits = rows_ref[tail:, :].astype(F32).astype(jnp.int32)
    index = digits[:, :cap] * LANES + digits[:, LANES : LANES + cap]
    spread(index, rows_ref[:tail, :], (first_ref, last_ref), (0, kept))
    last_ref[:, :kept, :] = rest_ref[...]


def relay_sends(rows, rest, cap):
    peers, kept, length = rest.shape
    shapes = [(peers, cap - kept, length), (peers, 2 * kept, length)]
    return pl.pallas_call(
        partial(relay_kernel, cap),
        out_shape=[jax.ShapeDtypeStruct(shape, BF16) for shape in shapes],
        compiler_params=pltpu.CompilerParams(vmem_limit_bytes=SMALL),
        name="relay",
    )(rows, rest)


def place_kernel(peers, half_ref, pair_ref, place_ref):
    cap = pair_ref.shape[2]
    pair = pair_ref[...]
    source = lax.div(pair, cap)
    side = lax.div(source, peers) != half_ref[0]
    offset = jnp.where(side, peers * SUB, 0)
    place_ref[...] = offset + lax.rem(source, peers) * SUB + lax.rem(pair, SUB)


def place_rows(half, pairs, peers):
    return pl.pallas_call(
        partial(place_kernel, peers),
        in_specs=[pl.BlockSpec(memory_space=pltpu.SMEM), pl.BlockSpec(memory_space=pltpu.VMEM)],
        out_shape=jax.ShapeDtypeStruct(pairs.shape, jnp.int32),
        compiler_params=pltpu.CompilerParams(vmem_limit_bytes=SMALL),
        name="places",
    )(half, pairs)


def pair_kernel(geo, first, station_ref, count_ref, place_ref, own_ref, far_ref, weight_ref, lag_ref, *refs):
    out_ref = refs[-1]
    peers, cap, joint = geo
    group = pl.program_id(0) + first
    length = own_ref.shape[-1]
    half_len = length // 2

    rows = jnp.concatenate(
        [ref[...].reshape(peers * SUB, length) for ref in (own_ref, far_ref)], axis=0
    )
    width = rows.shape[0]
    many = TOGETHER * LANES
    for j in range(joint):
        for i in range(0, SUB, TOGETHER):
            picks = [
                one_hot(place_ref[m, j, i + n : i + n + 1, :], width)
                for m in range(2)
                for n in range(TOGETHER)
            ]
            members = jnp.dot(jnp.concatenate(picks, axis=0), rows, preferred_element_type=F32)
            halves = []
            for n in range(TOGETHER):
                a = members[n * LANES : (n + 1) * LANES]
                b = members[many + n * LANES : many + (n + 1) * LANES]
                re_a, im_a = a[:, :half_len], a[:, half_len:]
                re_b, im_b = b[:, :half_len], b[:, half_len:]
                tile = j * cap + group * SUB + i + n
                scale = weight_ref[pl.ds(station_ref[tile], 1), :]
                halves.append(
                    jnp.concatenate(
                        [
                            ((re_a * re_b + im_a * im_b) * scale).astype(BF16),
                            ((im_a * re_b - re_a * im_b) * scale).astype(BF16),
                        ],
                        axis=1,
                    )
                )
            cross = jnp.concatenate(halves, axis=0)
            lagged = jnp.concatenate(
                [
                    jnp.dot(piece, lag_ref[...], preferred_element_type=F32)
                    for piece in (cross[: many // 2], cross[many // 2 :])
                ],
                axis=0,
            )
            for n in range(TOGETHER):
                tile = j * cap + group * SUB + i + n
                piece = lagged[n * LANES : (n + 1) * LANES]
                slot = lax.broadcasted_iota(jnp.int32, piece.shape, 0)
                piece = jnp.where(slot < count_ref[tile], piece, 0.0)
                out_ref[j, (i + n) * LANES : (i + n + 1) * LANES, :] = piece[:, :LAGS]


def correlate(first, steps, geo, stations_of, counts, places, own, far, weight, lag_tab, previous):
    (own, own_at), (far, far_at) = own, far
    peers, cap, joint = geo
    length = own.shape[-1]
    in_specs = [
        pl.BlockSpec((2, joint, SUB, LANES), lambda i, *_: (0, 0, i + first, 0)),
        pl.BlockSpec((peers, SUB, length), lambda i, *_: (0, i + own_at, 0)),
        pl.BlockSpec((peers, SUB, length), lambda i, *_: (0, i + far_at, 0)),
        pl.BlockSpec(weight.shape, lambda i, *_: (0, 0)),
        pl.BlockSpec(lag_tab.shape, lambda i, *_: (0, 0)),
    ]
    args = [places, own, far, weight, lag_tab]
    aliases = {}
    if previous is not None:
        in_specs.append(pl.BlockSpec(memory_space=pl.ANY))
        args.append(previous)
        aliases = {7: 0}
    tiles = joint * steps * SUB
    macs = tiles * LANES * length * (2 * 2 * peers * SUB + lag_tab.shape[1])
    return pl.pallas_call(
        partial(pair_kernel, geo, first),
        grid_spec=pltpu.PrefetchScalarGridSpec(
            num_scalar_prefetch=2,
            grid=(steps,),
            in_specs=in_specs,
            out_specs=pl.BlockSpec((joint, SUB * LANES, LAGS), lambda i, *_: (0, i + first, 0)),
        ),
        out_shape=jax.ShapeDtypeStruct((joint, cap * LANES, LAGS), F32),
        input_output_aliases=aliases,
        compiler_params=pltpu.CompilerParams(vmem_limit_bytes=SMALL),
        cost_estimate=pl.CostEstimate(
            flops=2 * macs, bytes_accessed=tiles * LANES * LAGS * 4, transcendentals=0
        ),
        name="pairs",
    )(stations_of, counts, *args)


def pair_up(value, step, owners):
    return lax.ppermute(value, "ev", [(i, i ^ step) for i in range(owners)])


def shards(windows, rotation, source_inverse, send_rows, tile_station, tile_count, pair_rows):
    ev_dev, _, stations, length = windows.shape
    owners = lax.axis_size("ev")
    cap = send_rows.shape[1]
    tiles_dev = tile_station.shape[0]
    joint = tiles_dev // cap
    peers = owners // 2
    half = lax.axis_index("ev") // peers
    halves = [list(range(peers)), list(range(peers, owners))]
    across = [(i, (i + peers) % owners) for i in range(owners)]
    to_peers = partial(
        lax.all_to_all,
        axis_name="ev",
        split_axis=0,
        concat_axis=0,
        axis_index_groups=halves,
        tiled=True,
    )
    half_arg = half.astype(jnp.int32).reshape(1)

    rows, power = event_rows(
        half_arg, windows, rotation, source_inverse, send_rows, spectral_table(length)
    )
    groups = cap // SUB
    early = groups * SPLIT[0] // sum(SPLIT)
    sizes = (early, groups - early)
    swapped = lax.ppermute(rows, "ev", across)
    send, rest = own_sends(half_arg, rows, send_rows, sizes)
    stations = power.shape[0]
    share = stations // 2
    low = lax.axis_index("ev") % 2 == 0
    parts = power[:share], power[share:]
    kept, passed = (jnp.where(low, *parts), jnp.where(low, *parts[::-1]))
    part = kept + pair_up(passed, 1, owners)
    step = 2
    while step < peers:
        part += pair_up(part, step, owners)
        step *= 2
    own = to_peers(send)
    sends = relay_sends(swapped, rest, cap)
    sends, own, part = lax.optimization_barrier((sends, own, part))
    part += pair_up(part, peers, owners)
    twin = pair_up(part, 1, owners)
    power = jnp.concatenate([jnp.where(low, part, twin), jnp.where(low, twin, part)], axis=0)
    weight = 1.0 / (power / (ev_dev * owners) + epsilon)
    places = place_rows(half_arg, pair_rows.reshape(2, joint, cap, LANES), peers)
    lag_tab = lag_table(length, LAGS, LAGS + 1)
    geo = (peers, cap, joint)
    far = to_peers(sends[0])
    last = to_peers(sends[1])
    run = partial(correlate, geo=geo, stations_of=tile_station, counts=tile_count, places=places)
    run = partial(run, weight=weight, lag_tab=lag_tab)
    far = pltpu.with_memory_space_constraint(far, pltpu.HBM)
    result = run(0, sizes[0], own=(own, 0), far=(far, 0), previous=None)
    result = run(early, sizes[1], own=(last, 0), far=(last, sizes[1]), previous=result)
    return result.reshape(tiles_dev * LANES, LAGS)


def solution(mesh):
    in_specs = (
        P(("grp", "ev"), None, None, None),
        P(("grp", "ev"), None, None),
        P(("grp", "ev"), None),
        P(("grp", "ev"), None),
        P(("grp", "ev")),
        P(("grp", "ev")),
        P(None, ("grp", "ev")),
    )
    out_specs = P(("grp", "ev"), None)
    return jax.shard_map(shards, mesh=mesh, in_specs=in_specs, out_specs=out_specs, check_vma=False)
```

```python
from functools import partial
import math

import jax
import jax.numpy as jnp
import numpy as np
from jax import lax
from jax.experimental import pallas as pl
from jax.experimental.pallas import tpu as pltpu
from jax.sharding import PartitionSpec as P


LAGS = 255
SUB = 8
LANES = 128
SPLIT = (5, 3)
TOGETHER = 8
SMALL = 20 << 20


epsilon = 1e-06
F32 = jnp.float32
BF16 = jnp.bfloat16


def spectral_table(length):
    half_len = length // 2
    samples = np.arange(length)[:, None]
    frequency = np.arange(half_len)[None, :]
    angles = (samples * frequency % length) * (2.0 * math.pi / length)
    factor = 1.0 / math.sqrt(length)
    table = np.concatenate([np.cos(angles) * factor, -np.sin(angles) * factor], axis=1)
    return jnp.asarray(table.astype(np.float32)).astype(BF16)


def lag_table(length, lag_count, width):
    half_len = length // 2
    frequency = np.arange(half_len)[:, None]
    shifts = np.arange(lag_count)[None, :] - lag_count // 2
    angles = (frequency * shifts % length) * (2.0 * math.pi / length)
    factor = 1.0 / math.sqrt(half_len)
    table = np.concatenate([np.cos(angles) * factor, -np.sin(angles) * factor], axis=0)
    table = np.pad(table, ((0, 0), (0, width - lag_count)))
    return jnp.asarray(table.astype(np.float32)).astype(BF16)


def column(values):
    return jnp.transpose(jnp.broadcast_to(values, (LANES, LANES)))


def one_hot(values, width):
    down = column(values)
    lane = lax.broadcasted_iota(jnp.int32, (LANES, LANES), 1)
    parts = [
        jnp.where(down == lane + LANES * j, 1.0, 0.0).astype(BF16) for j in range(width // LANES)
    ]
    return jnp.concatenate(parts, axis=1)


def spectra_kernel(steps, half_ref, win_ref, rot_ref, inv_ref, table_ref, index_ref, rows_ref, power_ref):
    step = pl.program_id(0)
    events, comps, stations, length = win_ref.shape
    half_len = length // 2
    blocks = []
    turns = rot_ref[...].astype(F32)
    for e in range(events):
        turn = turns[:, e, :]
        for s in range(1, steps):
            turn = jnp.where(step == s, turns[:, s * events + e, :], turn)
        rot = jnp.transpose(turn)
        total = rot[:, 0:1] * win_ref[e, 0].astype(F32)
        for c in range(1, comps):
            total += rot[:, c : c + 1] * win_ref[e, c].astype(F32)
        blocks.append(total.astype(BF16))
    transverse = jnp.concatenate(blocks, axis=0)
    spectrum = jnp.dot(transverse, table_ref[...], preferred_element_type=F32)
    gains = inv_ref[...].astype(F32)
    power = jnp.zeros((stations, half_len), F32)
    for e in range(events):
        re_in = spectrum[e * stations : (e + 1) * stations, :half_len]
        im_in = spectrum[e * stations : (e + 1) * stations, half_len:]
        gain = gains[e : e + 1, :]
        for s in range(1, steps):
            gain = jnp.where(step == s, gains[s * events + e : s * events + e + 1, :], gain)
        re_g, im_g = gain[:, :half_len], gain[:, half_len:]
        re = re_in * re_g - im_in * im_g
        im = re_in * im_g + im_in * re_g
        power += re * re + im * im
        base = pl.multiple_of((step * events + e) * stations, stations)
        rows_ref[pl.ds(base, stations), :half_len] = re.astype(BF16)
        rows_ref[pl.ds(base, stations), half_len:] = im.astype(BF16)

    @pl.when(step == 0)
    def _():
        power_ref[...] = power
        owners, cap = index_ref.shape
        peers = owners // 2
        other = pl.multiple_of((1 - half_ref[0]) * peers, peers)
        wanted = index_ref[pl.ds(other, peers), :]
        tail = rows_ref.shape[0] - peers
        rows_ref[tail:, :] = jnp.zeros((peers, length), BF16)
        rows_ref[tail:, :cap] = (wanted // LANES).astype(F32).astype(BF16)
        rows_ref[tail:, LANES : LANES + cap] = (wanted % LANES).astype(F32).astype(BF16)

    @pl.when(step > 0)
    def _():
        power_ref[...] += power


def event_rows(half, windows, rotation, source_inverse, send_rows, table):
    ev_dev, comps, stations, length = windows.shape
    owners, cap = send_rows.shape
    steps = 2 if ev_dev % 2 == 0 else 1
    events = ev_dev // steps
    total = ev_dev * stations + owners // 2
    args = (windows, rotation.swapaxes(0, 1), source_inverse, table, send_rows)
    args = [pltpu.with_memory_space_constraint(x, pltpu.HBM) for x in args]
    whole = lambda *shape: pl.BlockSpec(shape, lambda i, *_: (0,) * len(shape))
    return pl.pallas_call(
        partial(spectra_kernel, steps),
        grid_spec=pltpu.PrefetchScalarGridSpec(
            num_scalar_prefetch=1,
            grid=(steps,),
            in_specs=[
                pl.BlockSpec((events, comps, stations, length), lambda i, *_: (i, 0, 0, 0)),
                whole(comps, ev_dev, stations),
                whole(ev_dev, length),
                whole(length, length),
                whole(owners, cap),
            ],
            out_specs=[whole(total, length), whole(stations, length // 2)],
        ),
        out_shape=[
            jax.ShapeDtypeStruct((total, length), BF16),
            jax.ShapeDtypeStruct((stations, length // 2), F32),
        ],
        compiler_params=pltpu.CompilerParams(vmem_limit_bytes=SMALL),
        name="spectra",
    )(half, *args)


def pick_rows(index, rows, store):
    peers, cap = index.shape
    lines = LANES // cap
    for first in range(0, peers, lines):
        line = jnp.concatenate([index[first + j : first + j + 1, :] for j in range(lines)], axis=1)
        picked = jnp.dot(one_hot(line, rows.shape[0]), rows, preferred_element_type=F32)
        picked = picked.astype(BF16)
        for j in range(lines):
            store(first + j, picked[j * cap : (j + 1) * cap])


def spread(index, rows, refs, skips):
    def store(peer, picked):
        start = 0
        for ref, skip in zip(refs, skips):
            count = ref.shape[1] - skip
            ref[peer, skip:, :] = picked[start : start + count]
            start += count

    pick_rows(index, rows, store)


def own_kernel(half_ref, rows_ref, index_ref, *send_refs):
    peers = send_refs[0].shape[0]
    mine = pl.multiple_of(half_ref[0] * peers, peers)
    spread(index_ref[pl.ds(mine, peers), :], rows_ref[...], send_refs, (0, 0))


def own_sends(half, rows, send_rows, sizes):
    owners, cap = send_rows.shape
    peers = owners // 2
    length = rows.shape[1]
    whole = lambda *shape: pl.BlockSpec(shape, lambda i, *_: (0,) * len(shape))
    shapes = [(peers, size * SUB, length) for size in sizes]
    return pl.pallas_call(
        own_kernel,
        grid_spec=pltpu.PrefetchScalarGridSpec(
            num_scalar_prefetch=1,
            grid=(1,),
            in_specs=[whole(rows.shape[0] - peers, length), whole(owners, cap)],
            out_specs=[whole(*shape) for shape in shapes],
        ),
        out_shape=[jax.ShapeDtypeStruct(shape, BF16) for shape in shapes],
        compiler_params=pltpu.CompilerParams(vmem_limit_bytes=SMALL),
        name="own",
    )(half, rows, send_rows)


def relay_kernel(cap, me_ref, rows_ref, rest_ref, first_ref, *refs):
    *late_refs, held_ref = refs
    peers, kept, _ = rest_ref.shape
    tail = rows_ref.shape[0] - peers
    digits = rows_ref[tail:, :].astype(F32).astype(jnp.int32)
    index = digits[:, :cap] * LANES + digits[:, LANES : LANES + cap]
    spread(index, rows_ref[:tail, :], (first_ref, held_ref), (0, kept))
    held_ref[:, :kept, :] = rest_ref[...]
    for step, ref in enumerate(late_refs):
        ref[...] = held_ref[me_ref[0] ^ step]


def relay_sends(me, rows, rest, cap):
    peers, kept, length = rest.shape
    shapes = [(peers, cap - kept, length)] + [(2 * kept, length)] * peers
    vmem = pl.BlockSpec(memory_space=pltpu.VMEM)
    return pl.pallas_call(
        partial(relay_kernel, cap),
        in_specs=[pl.BlockSpec(memory_space=pltpu.SMEM), vmem, vmem],
        out_shape=[jax.ShapeDtypeStruct(shape, BF16) for shape in shapes],
        scratch_shapes=[pltpu.VMEM((peers, 2 * kept, length), BF16)],
        compiler_params=pltpu.CompilerParams(vmem_limit_bytes=SMALL),
        name="relay",
    )(me, rows, rest)


def place_kernel(peers, early, half_ref, me_ref, pair_ref, place_ref):
    cap = pair_ref.shape[2]
    pair = pair_ref[...]
    source = lax.div(pair, cap)
    side = lax.div(source, peers) != half_ref[0]
    offset = jnp.where(side, peers * SUB, 0)
    peer = lax.rem(source, peers)
    late = lax.broadcasted_iota(jnp.int32, pair.shape, 2) >= early * SUB
    peer = jnp.where(late, peer ^ me_ref[0], peer)
    place_ref[...] = offset + peer * SUB + lax.rem(pair, SUB)


def place_rows(half, me, pairs, peers, early):
    smem = pl.BlockSpec(memory_space=pltpu.SMEM)
    return pl.pallas_call(
        partial(place_kernel, peers, early),
        in_specs=[smem, smem, pl.BlockSpec(memory_space=pltpu.VMEM)],
        out_shape=jax.ShapeDtypeStruct(pairs.shape, jnp.int32),
        compiler_params=pltpu.CompilerParams(vmem_limit_bytes=SMALL),
        name="places",
    )(half, me, pairs)


def pair_kernel(geo, first, count, station_ref, count_ref, place_ref, weight_ref, lag_ref, *refs):
    row_refs, out_ref = refs[:count], refs[-1]
    _, cap, joint = geo
    group = pl.program_id(0) + first
    length = row_refs[0].shape[-1]
    half_len = length // 2

    rows = jnp.concatenate([ref[...].reshape(-1, length) for ref in row_refs], axis=0)
    width = rows.shape[0]
    many = TOGETHER * LANES
    for j in range(joint):
        for i in range(0, SUB, TOGETHER):
            picks = [
                one_hot(place_ref[m, j, i + n : i + n + 1, :], width)
                for m in range(2)
                for n in range(TOGETHER)
            ]
            members = jnp.dot(jnp.concatenate(picks, axis=0), rows, preferred_element_type=F32)
            halves = []
            for n in range(TOGETHER):
                a = members[n * LANES : (n + 1) * LANES]
                b = members[many + n * LANES : many + (n + 1) * LANES]
                re_a, im_a = a[:, :half_len], a[:, half_len:]
                re_b, im_b = b[:, :half_len], b[:, half_len:]
                tile = j * cap + group * SUB + i + n
                scale = weight_ref[pl.ds(station_ref[tile], 1), :]
                halves.append(
                    jnp.concatenate(
                        [
                            ((re_a * re_b + im_a * im_b) * scale).astype(BF16),
                            ((im_a * re_b - re_a * im_b) * scale).astype(BF16),
                        ],
                        axis=1,
                    )
                )
            cross = jnp.concatenate(halves, axis=0)
            lagged = jnp.concatenate(
                [
                    jnp.dot(piece, lag_ref[...], preferred_element_type=F32)
                    for piece in (cross[: many // 2], cross[many // 2 :])
                ],
                axis=0,
            )
            for n in range(TOGETHER):
                tile = j * cap + group * SUB + i + n
                piece = lagged[n * LANES : (n + 1) * LANES]
                slot = lax.broadcasted_iota(jnp.int32, piece.shape, 0)
                piece = jnp.where(slot < count_ref[tile], piece, 0.0)
                out_ref[j, (i + n) * LANES : (i + n + 1) * LANES, :] = piece[:, :LAGS]


def correlate(first, steps, sources, geo, stations_of, counts, places, weight, lag_tab, previous):
    peers, cap, joint = geo
    length = sources[0][0].shape[-1]
    in_specs = [
        pl.BlockSpec((2, joint, SUB, LANES), lambda i, *_: (0, 0, i + first, 0)),
        pl.BlockSpec(weight.shape, lambda i, *_: (0, 0)),
        pl.BlockSpec(lag_tab.shape, lambda i, *_: (0, 0)),
    ]
    args = [places, weight, lag_tab]
    for array, at in sources:
        if array.ndim == 3:
            spec = pl.BlockSpec((peers, SUB, length), lambda i, *_, at=at: (0, i + at, 0))
        else:
            spec = pl.BlockSpec((SUB, length), lambda i, *_, at=at: (i + at, 0))
        in_specs.append(spec)
        args.append(array)
    aliases = {}
    if previous is not None:
        in_specs.append(pl.BlockSpec(memory_space=pl.ANY))
        args.append(previous)
        aliases = {len(args) + 1: 0}
    tiles = joint * steps * SUB
    macs = tiles * LANES * length * (2 * 2 * peers * SUB + lag_tab.shape[1])
    return pl.pallas_call(
        partial(pair_kernel, geo, first, len(sources)),
        grid_spec=pltpu.PrefetchScalarGridSpec(
            num_scalar_prefetch=2,
            grid=(steps,),
            in_specs=in_specs,
            out_specs=pl.BlockSpec((joint, SUB * LANES, LAGS), lambda i, *_: (0, i + first, 0)),
        ),
        out_shape=jax.ShapeDtypeStruct((joint, cap * LANES, LAGS), F32),
        input_output_aliases=aliases,
        compiler_params=pltpu.CompilerParams(vmem_limit_bytes=SMALL),
        cost_estimate=pl.CostEstimate(
            flops=2 * macs, bytes_accessed=tiles * LANES * LAGS * 4, transcendentals=0
        ),
        name="pairs",
    )(stations_of, counts, *args)


def pair_up(value, step, owners):
    return lax.ppermute(value, "ev", [(i, i ^ step) for i in range(owners)])


def shards(windows, rotation, source_inverse, send_rows, tile_station, tile_count, pair_rows):
    ev_dev, _, stations, length = windows.shape
    owners = lax.axis_size("ev")
    cap = send_rows.shape[1]
    tiles_dev = tile_station.shape[0]
    joint = tiles_dev // cap
    peers = owners // 2
    half = lax.axis_index("ev") // peers
    halves = [list(range(peers)), list(range(peers, owners))]
    across = [(i, (i + peers) % owners) for i in range(owners)]
    to_peers = partial(
        lax.all_to_all,
        axis_name="ev",
        split_axis=0,
        concat_axis=0,
        axis_index_groups=halves,
        tiled=True,
    )
    half_arg = half.astype(jnp.int32).reshape(1)
    me_arg = (lax.axis_index("ev") % peers).astype(jnp.int32).reshape(1)

    rows, power = event_rows(
        half_arg, windows, rotation, source_inverse, send_rows, spectral_table(length)
    )
    groups = cap // SUB
    early = groups * SPLIT[0] // sum(SPLIT)
    sizes = (early, groups - early)
    swapped = lax.ppermute(rows, "ev", across)
    send, rest = own_sends(half_arg, rows, send_rows, sizes)
    stations = power.shape[0]
    share = stations // 2
    low = lax.axis_index("ev") % 2 == 0
    parts = power[:share], power[share:]
    kept, passed = (jnp.where(low, *parts), jnp.where(low, *parts[::-1]))
    part = kept + pair_up(passed, 1, owners)
    step = 2
    while step < peers:
        part += pair_up(part, step, owners)
        step *= 2
    own = to_peers(send)
    sends = relay_sends(me_arg, swapped, rest, cap)
    sends, own, part = lax.optimization_barrier((sends, own, part))
    part += pair_up(part, peers, owners)
    twin = pair_up(part, 1, owners)
    power = jnp.concatenate([jnp.where(low, part, twin), jnp.where(low, twin, part)], axis=0)
    weight = 1.0 / (power / (ev_dev * owners) + epsilon)
    places = place_rows(half_arg, me_arg, pair_rows.reshape(2, joint, cap, LANES), peers, early)
    lag_tab = lag_table(length, LAGS, LAGS + 1)
    geo = (peers, cap, joint)
    far = to_peers(sends[0])
    last = [sends[1]]
    for step in range(1, peers):
        last.append(pair_up(sends[1 + step], step, owners))
    run = partial(correlate, geo=geo, stations_of=tile_station, counts=tile_count, places=places)
    run = partial(run, weight=weight, lag_tab=lag_tab)
    far = pltpu.with_memory_space_constraint(far, pltpu.HBM)
    result = run(0, sizes[0], [(own, 0), (far, 0)], previous=None)
    late = [(array, at) for at in (0, sizes[1]) for array in last]
    result = run(early, sizes[1], late, previous=result)
    return result.reshape(tiles_dev * LANES, LAGS)


def solution(mesh):
    in_specs = (
        P(("grp", "ev"), None, None, None),
        P(("grp", "ev"), None, None),
        P(("grp", "ev"), None),
        P(("grp", "ev"), None),
        P(("grp", "ev")),
        P(("grp", "ev")),
        P(None, ("grp", "ev")),
    )
    out_specs = P(("grp", "ev"), None)
    return jax.shard_map(shards, mesh=mesh, in_specs=in_specs, out_specs=out_specs, check_vma=False)
```

```python
from functools import partial
import math

import jax
import jax.numpy as jnp
import numpy as np
from jax import lax
from jax.experimental import pallas as pl
from jax.experimental.pallas import tpu as pltpu
from jax.sharding import PartitionSpec as P


LAGS = 255
SUB = 8
LANES = 128
SPLIT = (6, 2)
TOGETHER = 8
SMALL = 20 << 20


epsilon = 1e-06
F32 = jnp.float32
BF16 = jnp.bfloat16


def spectral_table(length):
    half_len = length // 2
    samples = np.arange(length)[:, None]
    frequency = np.arange(half_len)[None, :]
    angles = (samples * frequency % length) * (2.0 * math.pi / length)
    factor = 1.0 / math.sqrt(length)
    table = np.concatenate([np.cos(angles) * factor, -np.sin(angles) * factor], axis=1)
    return jnp.asarray(table.astype(np.float32)).astype(BF16)


def lag_table(length, lag_count, width):
    half_len = length // 2
    frequency = np.arange(half_len)[:, None]
    shifts = np.arange(lag_count)[None, :] - lag_count // 2
    angles = (frequency * shifts % length) * (2.0 * math.pi / length)
    factor = 1.0 / math.sqrt(half_len)
    table = np.concatenate([np.cos(angles) * factor, -np.sin(angles) * factor], axis=0)
    table = np.pad(table, ((0, 0), (0, width - lag_count)))
    return jnp.asarray(table.astype(np.float32)).astype(BF16)


def column(values):
    return jnp.transpose(jnp.broadcast_to(values, (LANES, LANES)))


def one_hot(values, width):
    down = column(values)
    lane = lax.broadcasted_iota(jnp.int32, (LANES, LANES), 1)
    parts = [
        jnp.where(down == lane + LANES * j, 1.0, 0.0).astype(BF16) for j in range(width // LANES)
    ]
    return jnp.concatenate(parts, axis=1)


def spectra_kernel(steps, half_ref, win_ref, rot_ref, inv_ref, table_ref, index_ref, rows_ref, power_ref):
    step = pl.program_id(0)
    events, comps, stations, length = win_ref.shape
    half_len = length // 2
    blocks = []
    turns = rot_ref[...].astype(F32)
    for e in range(events):
        turn = turns[:, e, :]
        for s in range(1, steps):
            turn = jnp.where(step == s, turns[:, s * events + e, :], turn)
        rot = jnp.transpose(turn)
        total = rot[:, 0:1] * win_ref[e, 0].astype(F32)
        for c in range(1, comps):
            total += rot[:, c : c + 1] * win_ref[e, c].astype(F32)
        blocks.append(total.astype(BF16))
    transverse = jnp.concatenate(blocks, axis=0)
    spectrum = jnp.dot(transverse, table_ref[...], preferred_element_type=F32)
    gains = inv_ref[...].astype(F32)
    power = jnp.zeros((stations, half_len), F32)
    for e in range(events):
        re_in = spectrum[e * stations : (e + 1) * stations, :half_len]
        im_in = spectrum[e * stations : (e + 1) * stations, half_len:]
        gain = gains[e : e + 1, :]
        for s in range(1, steps):
            gain = jnp.where(step == s, gains[s * events + e : s * events + e + 1, :], gain)
        re_g, im_g = gain[:, :half_len], gain[:, half_len:]
        re = re_in * re_g - im_in * im_g
        im = re_in * im_g + im_in * re_g
        power += re * re + im * im
        base = pl.multiple_of((step * events + e) * stations, stations)
        rows_ref[pl.ds(base, stations), :half_len] = re.astype(BF16)
        rows_ref[pl.ds(base, stations), half_len:] = im.astype(BF16)

    @pl.when(step == 0)
    def _():
        power_ref[...] = power
        owners, cap = index_ref.shape
        peers = owners // 2
        other = pl.multiple_of((1 - half_ref[0]) * peers, peers)
        wanted = index_ref[pl.ds(other, peers), :]
        tail = rows_ref.shape[0] - peers
        rows_ref[tail:, :] = jnp.zeros((peers, length), BF16)
        rows_ref[tail:, :cap] = (wanted // LANES).astype(F32).astype(BF16)
        rows_ref[tail:, LANES : LANES + cap] = (wanted % LANES).astype(F32).astype(BF16)

    @pl.when(step > 0)
    def _():
        power_ref[...] += power


def event_rows(half, windows, rotation, source_inverse, send_rows, table):
    ev_dev, comps, stations, length = windows.shape
    owners, cap = send_rows.shape
    steps = 2 if ev_dev % 2 == 0 else 1
    events = ev_dev // steps
    total = ev_dev * stations + owners // 2
    args = (windows, rotation.swapaxes(0, 1), source_inverse, table, send_rows)
    args = [pltpu.with_memory_space_constraint(x, pltpu.HBM) for x in args]
    whole = lambda *shape: pl.BlockSpec(shape, lambda i, *_: (0,) * len(shape))
    return pl.pallas_call(
        partial(spectra_kernel, steps),
        grid_spec=pltpu.PrefetchScalarGridSpec(
            num_scalar_prefetch=1,
            grid=(steps,),
            in_specs=[
                pl.BlockSpec((events, comps, stations, length), lambda i, *_: (i, 0, 0, 0)),
                whole(comps, ev_dev, stations),
                whole(ev_dev, length),
                whole(length, length),
                whole(owners, cap),
            ],
            out_specs=[whole(total, length), whole(stations, length // 2)],
        ),
        out_shape=[
            jax.ShapeDtypeStruct((total, length), BF16),
            jax.ShapeDtypeStruct((stations, length // 2), F32),
        ],
        compiler_params=pltpu.CompilerParams(vmem_limit_bytes=SMALL),
        name="spectra",
    )(half, *args)


def pick_rows(index, rows, store):
    peers, cap = index.shape
    lines = LANES // cap
    for first in range(0, peers, lines):
        line = jnp.concatenate([index[first + j : first + j + 1, :] for j in range(lines)], axis=1)
        picked = jnp.dot(one_hot(line, rows.shape[0]), rows, preferred_element_type=F32)
        picked = picked.astype(BF16)
        for j in range(lines):
            store(first + j, picked[j * cap : (j + 1) * cap])


def spread(index, rows, refs, skips):
    def store(peer, picked):
        start = 0
        for ref, skip in zip(refs, skips):
            count = ref.shape[1] - skip
            ref[peer, skip:, :] = picked[start : start + count]
            start += count

    pick_rows(index, rows, store)


def own_kernel(half_ref, rows_ref, index_ref, *send_refs):
    peers = send_refs[0].shape[0]
    mine = pl.multiple_of(half_ref[0] * peers, peers)
    spread(index_ref[pl.ds(mine, peers), :], rows_ref[...], send_refs, (0, 0))


def own_sends(half, rows, send_rows, sizes):
    owners, cap = send_rows.shape
    peers = owners // 2
    length = rows.shape[1]
    whole = lambda *shape: pl.BlockSpec(shape, lambda i, *_: (0,) * len(shape))
    shapes = [(peers, size * SUB, length) for size in sizes]
    return pl.pallas_call(
        own_kernel,
        grid_spec=pltpu.PrefetchScalarGridSpec(
            num_scalar_prefetch=1,
            grid=(1,),
            in_specs=[whole(rows.shape[0] - peers, length), whole(owners, cap)],
            out_specs=[whole(*shape) for shape in shapes],
        ),
        out_shape=[jax.ShapeDtypeStruct(shape, BF16) for shape in shapes],
        compiler_params=pltpu.CompilerParams(vmem_limit_bytes=SMALL),
        name="own",
    )(half, rows, send_rows)


def relay_kernel(cap, me_ref, rows_ref, rest_ref, *refs):
    *first_refs, last_ref, held_ref = refs
    peers, kept, _ = rest_ref.shape
    tail = rows_ref.shape[0] - peers
    digits = rows_ref[tail:, :].astype(F32).astype(jnp.int32)
    index = digits[:, :cap] * LANES + digits[:, LANES : LANES + cap]
    spread(index, rows_ref[:tail, :], (held_ref, last_ref), (0, kept))
    last_ref[:, :kept, :] = rest_ref[...]
    for step, ref in enumerate(first_refs):
        ref[...] = held_ref[me_ref[0] ^ step]


def relay_sends(me, rows, rest, cap):
    peers, kept, length = rest.shape
    shapes = [(cap - kept, length)] * peers + [(peers, 2 * kept, length)]
    vmem = pl.BlockSpec(memory_space=pltpu.VMEM)
    return pl.pallas_call(
        partial(relay_kernel, cap),
        in_specs=[pl.BlockSpec(memory_space=pltpu.SMEM), vmem, vmem],
        out_shape=[jax.ShapeDtypeStruct(shape, BF16) for shape in shapes],
        scratch_shapes=[pltpu.VMEM((peers, cap - kept, length), BF16)],
        compiler_params=pltpu.CompilerParams(vmem_limit_bytes=SMALL),
        name="relay",
    )(me, rows, rest)


def place_kernel(peers, early, half_ref, me_ref, pair_ref, place_ref):
    cap = pair_ref.shape[2]
    pair = pair_ref[...]
    source = lax.div(pair, cap)
    side = lax.div(source, peers) != half_ref[0]
    offset = jnp.where(side, peers * SUB, 0)
    peer = lax.rem(source, peers)
    late = lax.broadcasted_iota(jnp.int32, pair.shape, 2) >= early * SUB
    peer = jnp.where(late | (offset == 0), peer, peer ^ me_ref[0])
    place_ref[...] = offset + peer * SUB + lax.rem(pair, SUB)


def place_rows(half, me, pairs, peers, early):
    smem = pl.BlockSpec(memory_space=pltpu.SMEM)
    return pl.pallas_call(
        partial(place_kernel, peers, early),
        in_specs=[smem, smem, pl.BlockSpec(memory_space=pltpu.VMEM)],
        out_shape=jax.ShapeDtypeStruct(pairs.shape, jnp.int32),
        compiler_params=pltpu.CompilerParams(vmem_limit_bytes=SMALL),
        name="places",
    )(half, me, pairs)


def pair_kernel(geo, first, count, station_ref, count_ref, place_ref, weight_ref, lag_ref, *refs):
    row_refs, out_ref = refs[:count], refs[-1]
    _, cap, joint = geo
    group = pl.program_id(0) + first
    length = row_refs[0].shape[-1]
    half_len = length // 2

    rows = jnp.concatenate([ref[...].reshape(-1, length) for ref in row_refs], axis=0)
    width = rows.shape[0]
    many = TOGETHER * LANES
    for j in range(joint):
        for i in range(0, SUB, TOGETHER):
            picks = [
                one_hot(place_ref[m, j, i + n : i + n + 1, :], width)
                for m in range(2)
                for n in range(TOGETHER)
            ]
            members = jnp.dot(jnp.concatenate(picks, axis=0), rows, preferred_element_type=F32)
            halves = []
            for n in range(TOGETHER):
                a = members[n * LANES : (n + 1) * LANES]
                b = members[many + n * LANES : many + (n + 1) * LANES]
                re_a, im_a = a[:, :half_len], a[:, half_len:]
                re_b, im_b = b[:, :half_len], b[:, half_len:]
                tile = j * cap + group * SUB + i + n
                scale = weight_ref[pl.ds(station_ref[tile], 1), :]
                halves.append(
                    jnp.concatenate(
                        [
                            ((re_a * re_b + im_a * im_b) * scale).astype(BF16),
                            ((im_a * re_b - re_a * im_b) * scale).astype(BF16),
                        ],
                        axis=1,
                    )
                )
            cross = jnp.concatenate(halves, axis=0)
            lagged = jnp.concatenate(
                [
                    jnp.dot(piece, lag_ref[...], preferred_element_type=F32)
                    for piece in (cross[: many // 2], cross[many // 2 :])
                ],
                axis=0,
            )
            for n in range(TOGETHER):
                tile = j * cap + group * SUB + i + n
                piece = lagged[n * LANES : (n + 1) * LANES]
                slot = lax.broadcasted_iota(jnp.int32, piece.shape, 0)
                piece = jnp.where(slot < count_ref[tile], piece, 0.0)
                out_ref[j, (i + n) * LANES : (i + n + 1) * LANES, :] = piece[:, :LAGS]


def correlate(first, steps, sources, geo, stations_of, counts, places, weight, lag_tab, previous):
    peers, cap, joint = geo
    length = sources[0][0].shape[-1]
    in_specs = [
        pl.BlockSpec((2, joint, SUB, LANES), lambda i, *_: (0, 0, i + first, 0)),
        pl.BlockSpec(weight.shape, lambda i, *_: (0, 0)),
        pl.BlockSpec(lag_tab.shape, lambda i, *_: (0, 0)),
    ]
    args = [places, weight, lag_tab]
    for array, at in sources:
        if array.ndim == 3:
            spec = pl.BlockSpec((peers, SUB, length), lambda i, *_, at=at: (0, i + at, 0))
        else:
            spec = pl.BlockSpec((SUB, length), lambda i, *_, at=at: (i + at, 0))
        in_specs.append(spec)
        args.append(array)
    aliases = {}
    if previous is not None:
        in_specs.append(pl.BlockSpec(memory_space=pl.ANY))
        args.append(previous)
        aliases = {len(args) + 1: 0}
    tiles = joint * steps * SUB
    macs = tiles * LANES * length * (2 * 2 * peers * SUB + lag_tab.shape[1])
    return pl.pallas_call(
        partial(pair_kernel, geo, first, len(sources)),
        grid_spec=pltpu.PrefetchScalarGridSpec(
            num_scalar_prefetch=2,
            grid=(steps,),
            in_specs=in_specs,
            out_specs=pl.BlockSpec((joint, SUB * LANES, LAGS), lambda i, *_: (0, i + first, 0)),
        ),
        out_shape=jax.ShapeDtypeStruct((joint, cap * LANES, LAGS), F32),
        input_output_aliases=aliases,
        compiler_params=pltpu.CompilerParams(vmem_limit_bytes=SMALL),
        cost_estimate=pl.CostEstimate(
            flops=2 * macs, bytes_accessed=tiles * LANES * LAGS * 4, transcendentals=0
        ),
        name="pairs",
    )(stations_of, counts, *args)


def pair_up(value, step, owners):
    return lax.ppermute(value, "ev", [(i, i ^ step) for i in range(owners)])


def shards(windows, rotation, source_inverse, send_rows, tile_station, tile_count, pair_rows):
    ev_dev, _, stations, length = windows.shape
    owners = lax.axis_size("ev")
    cap = send_rows.shape[1]
    tiles_dev = tile_station.shape[0]
    joint = tiles_dev // cap
    peers = owners // 2
    half = lax.axis_index("ev") // peers
    halves = [list(range(peers)), list(range(peers, owners))]
    across = [(i, (i + peers) % owners) for i in range(owners)]
    to_peers = partial(
        lax.all_to_all,
        axis_name="ev",
        split_axis=0,
        concat_axis=0,
        axis_index_groups=halves,
        tiled=True,
    )
    half_arg = half.astype(jnp.int32).reshape(1)
    me_arg = (lax.axis_index("ev") % peers).astype(jnp.int32).reshape(1)

    rows, power = event_rows(
        half_arg, windows, rotation, source_inverse, send_rows, spectral_table(length)
    )
    groups = cap // SUB
    early = groups * SPLIT[0] // sum(SPLIT)
    sizes = (early, groups - early)
    swapped = lax.ppermute(rows, "ev", across)
    send, rest = own_sends(half_arg, rows, send_rows, sizes)
    stations = power.shape[0]
    share = stations // 2
    low = lax.axis_index("ev") % 2 == 0
    parts = power[:share], power[share:]
    kept, passed = (jnp.where(low, *parts), jnp.where(low, *parts[::-1]))
    part = kept + pair_up(passed, 1, owners)
    step = 2
    while step < peers:
        part += pair_up(part, step, owners)
        step *= 2
    own = to_peers(send)
    sends = relay_sends(me_arg, swapped, rest, cap)
    part += pair_up(part, peers, owners)
    twin = pair_up(part, 1, owners)
    power = jnp.concatenate([jnp.where(low, part, twin), jnp.where(low, twin, part)], axis=0)
    weight = 1.0 / (power / (ev_dev * owners) + epsilon)
    places = place_rows(half_arg, me_arg, pair_rows.reshape(2, joint, cap, LANES), peers, early)
    lag_tab = lag_table(length, LAGS, LAGS + 1)
    geo = (peers, cap, joint)
    far = [sends[0]]
    for step in range(1, peers):
        far.append(pair_up(sends[step], step, owners))
    last = to_peers(sends[peers])
    run = partial(correlate, geo=geo, stations_of=tile_station, counts=tile_count, places=places)
    run = partial(run, weight=weight, lag_tab=lag_tab)
    result = run(0, sizes[0], [(own, 0)] + [(array, 0) for array in far], previous=None)
    result = run(early, sizes[1], [(last, 0), (last, sizes[1])], previous=result)
    return result.reshape(tiles_dev * LANES, LAGS)


def solution(mesh):
    in_specs = (
        P(("grp", "ev"), None, None, None),
        P(("grp", "ev"), None, None),
        P(("grp", "ev"), None),
        P(("grp", "ev"), None),
        P(("grp", "ev")),
        P(("grp", "ev")),
        P(None, ("grp", "ev")),
    )
    out_specs = P(("grp", "ev"), None)
    return jax.shard_map(shards, mesh=mesh, in_specs=in_specs, out_specs=out_specs, check_vma=False)
```

```python
from functools import partial
import math

import jax
import jax.numpy as jnp
import numpy as np
from jax import lax
from jax.experimental import pallas as pl
from jax.experimental.pallas import tpu as pltpu
from jax.sharding import PartitionSpec as P


LAGS = 255
SUB = 8
LANES = 128
SPLIT = (6, 2)
TOGETHER = 8
SMALL = 20 << 20


epsilon = 1e-06
F32 = jnp.float32
BF16 = jnp.bfloat16


def spectral_table(length):
    half_len = length // 2
    samples = np.arange(length)[:, None]
    frequency = np.arange(half_len)[None, :]
    angles = (samples * frequency % length) * (2.0 * math.pi / length)
    factor = 1.0 / math.sqrt(length)
    table = np.concatenate([np.cos(angles) * factor, -np.sin(angles) * factor], axis=1)
    return jnp.asarray(table.astype(np.float32)).astype(BF16)


def lag_table(length, lag_count, width):
    half_len = length // 2
    frequency = np.arange(half_len)[:, None]
    shifts = np.arange(lag_count)[None, :] - lag_count // 2
    angles = (frequency * shifts % length) * (2.0 * math.pi / length)
    factor = 1.0 / math.sqrt(half_len)
    table = np.concatenate([np.cos(angles) * factor, -np.sin(angles) * factor], axis=0)
    table = np.pad(table, ((0, 0), (0, width - lag_count)))
    return jnp.asarray(table.astype(np.float32)).astype(BF16)


def column(values):
    return jnp.transpose(jnp.broadcast_to(values, (LANES, LANES)))


def one_hot(values, width):
    down = column(values)
    lane = lax.broadcasted_iota(jnp.int32, (LANES, LANES), 1)
    parts = [
        jnp.where(down == lane + LANES * j, 1.0, 0.0).astype(BF16) for j in range(width // LANES)
    ]
    return jnp.concatenate(parts, axis=1)


def spectra_kernel(steps, half_ref, win_ref, rot_ref, inv_ref, table_ref, index_ref, rows_ref, power_ref):
    step = pl.program_id(0)
    events, comps, stations, length = win_ref.shape
    half_len = length // 2
    blocks = []
    turns = rot_ref[...].astype(F32)
    for e in range(events):
        turn = turns[:, e, :]
        for s in range(1, steps):
            turn = jnp.where(step == s, turns[:, s * events + e, :], turn)
        rot = jnp.transpose(turn)
        total = rot[:, 0:1] * win_ref[e, 0].astype(F32)
        for c in range(1, comps):
            total += rot[:, c : c + 1] * win_ref[e, c].astype(F32)
        blocks.append(total.astype(BF16))
    transverse = jnp.concatenate(blocks, axis=0)
    spectrum = jnp.dot(transverse, table_ref[...], preferred_element_type=F32)
    gains = inv_ref[...].astype(F32)
    power = jnp.zeros((stations, half_len), F32)
    for e in range(events):
        re_in = spectrum[e * stations : (e + 1) * stations, :half_len]
        im_in = spectrum[e * stations : (e + 1) * stations, half_len:]
        gain = gains[e : e + 1, :]
        for s in range(1, steps):
            gain = jnp.where(step == s, gains[s * events + e : s * events + e + 1, :], gain)
        re_g, im_g = gain[:, :half_len], gain[:, half_len:]
        re = re_in * re_g - im_in * im_g
        im = re_in * im_g + im_in * re_g
        power += re * re + im * im
        base = pl.multiple_of((step * events + e) * stations, stations)
        rows_ref[pl.ds(base, stations), :half_len] = re.astype(BF16)
        rows_ref[pl.ds(base, stations), half_len:] = im.astype(BF16)

    @pl.when(step == 0)
    def _():
        power_ref[...] = power
        owners, cap = index_ref.shape
        peers = owners // 2
        other = pl.multiple_of((1 - half_ref[0]) * peers, peers)
        wanted = index_ref[pl.ds(other, peers), :]
        tail = rows_ref.shape[0] - peers
        rows_ref[tail:, :] = jnp.zeros((peers, length), BF16)
        rows_ref[tail:, :cap] = (wanted // LANES).astype(F32).astype(BF16)
        rows_ref[tail:, LANES : LANES + cap] = (wanted % LANES).astype(F32).astype(BF16)

    @pl.when(step > 0)
    def _():
        power_ref[...] += power


def event_rows(half, windows, rotation, source_inverse, send_rows, table):
    ev_dev, comps, stations, length = windows.shape
    owners, cap = send_rows.shape
    steps = 2 if ev_dev % 2 == 0 else 1
    events = ev_dev // steps
    total = ev_dev * stations + owners // 2
    args = (windows, rotation.swapaxes(0, 1), source_inverse, table, send_rows)
    args = [pltpu.with_memory_space_constraint(x, pltpu.HBM) for x in args]
    whole = lambda *shape: pl.BlockSpec(shape, lambda i, *_: (0,) * len(shape))
    return pl.pallas_call(
        partial(spectra_kernel, steps),
        grid_spec=pltpu.PrefetchScalarGridSpec(
            num_scalar_prefetch=1,
            grid=(steps,),
            in_specs=[
                pl.BlockSpec((events, comps, stations, length), lambda i, *_: (i, 0, 0, 0)),
                whole(comps, ev_dev, stations),
                whole(ev_dev, length),
                whole(length, length),
                whole(owners, cap),
            ],
            out_specs=[whole(total, length), whole(stations, length // 2)],
        ),
        out_shape=[
            jax.ShapeDtypeStruct((total, length), BF16),
            jax.ShapeDtypeStruct((stations, length // 2), F32),
        ],
        compiler_params=pltpu.CompilerParams(vmem_limit_bytes=SMALL),
        name="spectra",
    )(half, *args)


def pick_rows(index, rows, store):
    peers, cap = index.shape
    lines = LANES // cap
    for first in range(0, peers, lines):
        line = jnp.concatenate([index[first + j : first + j + 1, :] for j in range(lines)], axis=1)
        picked = jnp.dot(one_hot(line, rows.shape[0]), rows, preferred_element_type=F32)
        picked = picked.astype(BF16)
        for j in range(lines):
            store(first + j, picked[j * cap : (j + 1) * cap])


def spread(index, rows, refs, skips):
    def store(peer, picked):
        start = 0
        for ref, skip in zip(refs, skips):
            count = ref.shape[1] - skip
            ref[peer, skip:, :] = picked[start : start + count]
            start += count

    pick_rows(index, rows, store)


def own_kernel(half_ref, rows_ref, index_ref, *send_refs):
    peers = send_refs[0].shape[0]
    mine = pl.multiple_of(half_ref[0] * peers, peers)
    spread(index_ref[pl.ds(mine, peers), :], rows_ref[...], send_refs, (0, 0))


def own_sends(half, rows, send_rows, sizes):
    owners, cap = send_rows.shape
    peers = owners // 2
    length = rows.shape[1]
    whole = lambda *shape: pl.BlockSpec(shape, lambda i, *_: (0,) * len(shape))
    shapes = [(peers, size * SUB, length) for size in sizes]
    return pl.pallas_call(
        own_kernel,
        grid_spec=pltpu.PrefetchScalarGridSpec(
            num_scalar_prefetch=1,
            grid=(1,),
            in_specs=[whole(rows.shape[0] - peers, length), whole(owners, cap)],
            out_specs=[whole(*shape) for shape in shapes],
        ),
        out_shape=[pltpu.HBM(shape, BF16) for shape in shapes],
        compiler_params=pltpu.CompilerParams(vmem_limit_bytes=SMALL),
        name="own",
    )(half, rows, send_rows)


def relay_kernel(cap, me_ref, rows_ref, rest_ref, *refs):
    *first_refs, last_ref, held_ref = refs
    peers, kept, _ = rest_ref.shape
    tail = rows_ref.shape[0] - peers
    digits = rows_ref[tail:, :].astype(F32).astype(jnp.int32)
    index = digits[:, :cap] * LANES + digits[:, LANES : LANES + cap]
    spread(index, rows_ref[:tail, :], (held_ref, last_ref), (0, kept))
    last_ref[:, :kept, :] = rest_ref[...]
    for step, ref in enumerate(first_refs):
        ref[...] = held_ref[me_ref[0] ^ step]


def relay_sends(me, rows, rest, cap):
    peers, kept, length = rest.shape
    shapes = [(cap - kept, length)] * peers + [(peers, 2 * kept, length)]
    vmem = pl.BlockSpec(memory_space=pltpu.VMEM)
    return pl.pallas_call(
        partial(relay_kernel, cap),
        in_specs=[pl.BlockSpec(memory_space=pltpu.SMEM), vmem, vmem],
        out_shape=[jax.ShapeDtypeStruct(shape, BF16) for shape in shapes[:-1]]
        + [pltpu.HBM(shapes[-1], BF16)],
        scratch_shapes=[pltpu.VMEM((peers, cap - kept, length), BF16)],
        compiler_params=pltpu.CompilerParams(vmem_limit_bytes=SMALL),
        name="relay",
    )(me, rows, rest)


def place_kernel(peers, early, half_ref, me_ref, pair_ref, place_ref):
    cap = pair_ref.shape[2]
    pair = pair_ref[...]
    source = lax.div(pair, cap)
    side = lax.div(source, peers) != half_ref[0]
    offset = jnp.where(side, peers * SUB, 0)
    peer = lax.rem(source, peers)
    late = lax.broadcasted_iota(jnp.int32, pair.shape, 2) >= early * SUB
    peer = jnp.where(late | (offset == 0), peer, peer ^ me_ref[0])
    place_ref[...] = offset + peer * SUB + lax.rem(pair, SUB)


def place_rows(half, me, pairs, peers, early):
    smem = pl.BlockSpec(memory_space=pltpu.SMEM)
    return pl.pallas_call(
        partial(place_kernel, peers, early),
        in_specs=[smem, smem, pl.BlockSpec(memory_space=pltpu.VMEM)],
        out_shape=jax.ShapeDtypeStruct(pairs.shape, jnp.int32),
        compiler_params=pltpu.CompilerParams(vmem_limit_bytes=SMALL),
        name="places",
    )(half, me, pairs)


def pair_kernel(geo, first, count, station_ref, count_ref, place_ref, weight_ref, lag_ref, *refs):
    row_refs, out_ref = refs[:count], refs[-1]
    _, cap, joint = geo
    group = pl.program_id(0) + first
    length = row_refs[0].shape[-1]
    half_len = length // 2

    rows = jnp.concatenate([ref[...].reshape(-1, length) for ref in row_refs], axis=0)
    width = rows.shape[0]
    many = TOGETHER * LANES
    for j in range(joint):
        for i in range(0, SUB, TOGETHER):
            picks = [
                one_hot(place_ref[m, j, i + n : i + n + 1, :], width)
                for m in range(2)
                for n in range(TOGETHER)
            ]
            members = jnp.dot(jnp.concatenate(picks, axis=0), rows, preferred_element_type=F32)
            halves = []
            for n in range(TOGETHER):
                a = members[n * LANES : (n + 1) * LANES]
                b = members[many + n * LANES : many + (n + 1) * LANES]
                re_a, im_a = a[:, :half_len], a[:, half_len:]
                re_b, im_b = b[:, :half_len], b[:, half_len:]
                tile = j * cap + group * SUB + i + n
                scale = weight_ref[pl.ds(station_ref[tile], 1), :]
                halves.append(
                    jnp.concatenate(
                        [
                            ((re_a * re_b + im_a * im_b) * scale).astype(BF16),
                            ((im_a * re_b - re_a * im_b) * scale).astype(BF16),
                        ],
                        axis=1,
                    )
                )
            cross = jnp.concatenate(halves, axis=0)
            lagged = jnp.concatenate(
                [
                    jnp.dot(piece, lag_ref[...], preferred_element_type=F32)
                    for piece in (cross[: many // 2], cross[many // 2 :])
                ],
                axis=0,
            )
            for n in range(TOGETHER):
                tile = j * cap + group * SUB + i + n
                piece = lagged[n * LANES : (n + 1) * LANES]
                slot = lax.broadcasted_iota(jnp.int32, piece.shape, 0)
                piece = jnp.where(slot < count_ref[tile], piece, 0.0)
                out_ref[j, (i + n) * LANES : (i + n + 1) * LANES, :] = piece[:, :LAGS]


def correlate(first, steps, sources, geo, stations_of, counts, places, weight, lag_tab, previous):
    peers, cap, joint = geo
    length = sources[0][0].shape[-1]
    in_specs = [
        pl.BlockSpec((2, joint, SUB, LANES), lambda i, *_: (0, 0, i + first, 0)),
        pl.BlockSpec(weight.shape, lambda i, *_: (0, 0)),
        pl.BlockSpec(lag_tab.shape, lambda i, *_: (0, 0)),
    ]
    args = [places, weight, lag_tab]
    for array, at in sources:
        if array.ndim == 3:
            spec = pl.BlockSpec((peers, SUB, length), lambda i, *_, at=at: (0, i + at, 0))
        else:
            spec = pl.BlockSpec((SUB, length), lambda i, *_, at=at: (i + at, 0))
        in_specs.append(spec)
        args.append(array)
    aliases = {}
    if previous is not None:
        in_specs.append(pl.BlockSpec(memory_space=pl.ANY))
        args.append(previous)
        aliases = {len(args) + 1: 0}
    tiles = joint * steps * SUB
    macs = tiles * LANES * length * (2 * 2 * peers * SUB + lag_tab.shape[1])
    return pl.pallas_call(
        partial(pair_kernel, geo, first, len(sources)),
        grid_spec=pltpu.PrefetchScalarGridSpec(
            num_scalar_prefetch=2,
            grid=(steps,),
            in_specs=in_specs,
            out_specs=pl.BlockSpec((joint, SUB * LANES, LAGS), lambda i, *_: (0, i + first, 0)),
        ),
        out_shape=jax.ShapeDtypeStruct((joint, cap * LANES, LAGS), F32),
        input_output_aliases=aliases,
        compiler_params=pltpu.CompilerParams(vmem_limit_bytes=SMALL),
        cost_estimate=pl.CostEstimate(
            flops=2 * macs, bytes_accessed=tiles * LANES * LAGS * 4, transcendentals=0
        ),
        name="pairs",
    )(stations_of, counts, *args)


def pair_up(value, step, owners):
    return lax.ppermute(value, "ev", [(i, i ^ step) for i in range(owners)])


def shards(windows, rotation, source_inverse, send_rows, tile_station, tile_count, pair_rows):
    ev_dev, _, stations, length = windows.shape
    owners = lax.axis_size("ev")
    cap = send_rows.shape[1]
    tiles_dev = tile_station.shape[0]
    joint = tiles_dev // cap
    peers = owners // 2
    half = lax.axis_index("ev") // peers
    halves = [list(range(peers)), list(range(peers, owners))]
    across = [(i, (i + peers) % owners) for i in range(owners)]
    to_peers = partial(
        lax.all_to_all,
        axis_name="ev",
        split_axis=0,
        concat_axis=0,
        axis_index_groups=halves,
        tiled=True,
    )
    half_arg = half.astype(jnp.int32).reshape(1)
    me_arg = (lax.axis_index("ev") % peers).astype(jnp.int32).reshape(1)

    rows, power = event_rows(
        half_arg, windows, rotation, source_inverse, send_rows, spectral_table(length)
    )
    groups = cap // SUB
    early = groups * SPLIT[0] // sum(SPLIT)
    sizes = (early, groups - early)
    swapped = lax.ppermute(rows, "ev", across)
    send, rest = own_sends(half_arg, rows, send_rows, sizes)
    stations = power.shape[0]
    share = stations // 2
    low = lax.axis_index("ev") % 2 == 0
    parts = power[:share], power[share:]
    kept, passed = (jnp.where(low, *parts), jnp.where(low, *parts[::-1]))
    part = kept + pair_up(passed, 1, owners)
    step = 2
    while step < peers:
        part += pair_up(part, step, owners)
        step *= 2
    own = to_peers(send)
    rest = pltpu.with_memory_space_constraint(rest, pltpu.HBM)
    sends = relay_sends(me_arg, swapped, rest, cap)
    part += pair_up(part, peers, owners)
    twin = pair_up(part, 1, owners)
    power = jnp.concatenate([jnp.where(low, part, twin), jnp.where(low, twin, part)], axis=0)
    weight = 1.0 / (power / (ev_dev * owners) + epsilon)
    places = place_rows(half_arg, me_arg, pair_rows.reshape(2, joint, cap, LANES), peers, early)
    lag_tab = lag_table(length, LAGS, LAGS + 1)
    geo = (peers, cap, joint)
    far = [sends[0]]
    for step in range(1, peers):
        far.append(pair_up(sends[step], step, owners))
    last = to_peers(sends[peers])
    run = partial(correlate, geo=geo, stations_of=tile_station, counts=tile_count, places=places)
    run = partial(run, weight=weight, lag_tab=lag_tab)
    result = run(0, sizes[0], [(own, 0)] + [(array, 0) for array in far], previous=None)
    result = run(early, sizes[1], [(last, 0), (last, sizes[1])], previous=result)
    return result.reshape(tiles_dev * LANES, LAGS)


def solution(mesh):
    in_specs = (
        P(("grp", "ev"), None, None, None),
        P(("grp", "ev"), None, None),
        P(("grp", "ev"), None),
        P(("grp", "ev"), None),
        P(("grp", "ev")),
        P(("grp", "ev")),
        P(None, ("grp", "ev")),
    )
    out_specs = P(("grp", "ev"), None)
    return jax.shard_map(shards, mesh=mesh, in_specs=in_specs, out_specs=out_specs, check_vma=False)
```

```python
from functools import partial
import math

import jax
import jax.numpy as jnp
import numpy as np
from jax import lax
from jax.experimental import pallas as pl
from jax.experimental.pallas import tpu as pltpu
from jax.sharding import PartitionSpec as P


LAGS = 255
SUB = 8
LANES = 128
SPLIT = (6, 2)
TOGETHER = 8
SMALL = 20 << 20


epsilon = 1e-06
F32 = jnp.float32
BF16 = jnp.bfloat16


def spectral_table(length):
    half_len = length // 2
    samples = np.arange(length)[:, None]
    frequency = np.arange(half_len)[None, :]
    angles = (samples * frequency % length) * (2.0 * math.pi / length)
    factor = 1.0 / math.sqrt(length)
    table = np.concatenate([np.cos(angles) * factor, -np.sin(angles) * factor], axis=1)
    return jnp.asarray(table.astype(np.float32)).astype(BF16)


def lag_table(length, lag_count, width):
    half_len = length // 2
    frequency = np.arange(half_len)[:, None]
    shifts = np.arange(lag_count)[None, :] - lag_count // 2
    angles = (frequency * shifts % length) * (2.0 * math.pi / length)
    factor = 1.0 / math.sqrt(half_len)
    table = np.concatenate([np.cos(angles) * factor, -np.sin(angles) * factor], axis=0)
    table = np.pad(table, ((0, 0), (0, width - lag_count)))
    return jnp.asarray(table.astype(np.float32)).astype(BF16)


def column(values):
    return jnp.transpose(jnp.broadcast_to(values, (LANES, LANES)))


def one_hot(values, width):
    down = column(values)
    lane = lax.broadcasted_iota(jnp.int32, (LANES, LANES), 1)
    parts = [
        jnp.where(down == lane + LANES * j, 1.0, 0.0).astype(BF16) for j in range(width // LANES)
    ]
    return jnp.concatenate(parts, axis=1)


def spectra_kernel(steps, half_ref, win_ref, rot_ref, inv_ref, table_ref, index_ref, rows_ref, power_ref):
    step = pl.program_id(0)
    events, comps, stations, length = win_ref.shape
    half_len = length // 2
    blocks = []
    turns = rot_ref[...].astype(F32)
    for e in range(events):
        turn = turns[:, e, :]
        for s in range(1, steps):
            turn = jnp.where(step == s, turns[:, s * events + e, :], turn)
        rot = jnp.transpose(turn)
        total = rot[:, 0:1] * win_ref[e, 0].astype(F32)
        for c in range(1, comps):
            total += rot[:, c : c + 1] * win_ref[e, c].astype(F32)
        blocks.append(total.astype(BF16))
    transverse = jnp.concatenate(blocks, axis=0)
    spectrum = jnp.dot(transverse, table_ref[...], preferred_element_type=F32)
    gains = inv_ref[...].astype(F32)
    power = jnp.zeros((stations, half_len), F32)
    for e in range(events):
        re_in = spectrum[e * stations : (e + 1) * stations, :half_len]
        im_in = spectrum[e * stations : (e + 1) * stations, half_len:]
        gain = gains[e : e + 1, :]
        for s in range(1, steps):
            gain = jnp.where(step == s, gains[s * events + e : s * events + e + 1, :], gain)
        re_g, im_g = gain[:, :half_len], gain[:, half_len:]
        re = re_in * re_g - im_in * im_g
        im = re_in * im_g + im_in * re_g
        power += re * re + im * im
        base = pl.multiple_of((step * events + e) * stations, stations)
        rows_ref[pl.ds(base, stations), :half_len] = re.astype(BF16)
        rows_ref[pl.ds(base, stations), half_len:] = im.astype(BF16)

    @pl.when(step == 0)
    def _():
        power_ref[...] = power
        owners, cap = index_ref.shape
        peers = owners // 2
        other = pl.multiple_of((1 - half_ref[0]) * peers, peers)
        wanted = index_ref[pl.ds(other, peers), :]
        tail = rows_ref.shape[0] - peers
        rows_ref[tail:, :] = jnp.zeros((peers, length), BF16)
        rows_ref[tail:, :cap] = (wanted // LANES).astype(F32).astype(BF16)
        rows_ref[tail:, LANES : LANES + cap] = (wanted % LANES).astype(F32).astype(BF16)

    @pl.when(step > 0)
    def _():
        power_ref[...] += power


def event_rows(half, windows, rotation, source_inverse, send_rows, table):
    ev_dev, comps, stations, length = windows.shape
    owners, cap = send_rows.shape
    steps = 2 if ev_dev % 2 == 0 else 1
    events = ev_dev // steps
    total = ev_dev * stations + owners // 2
    args = (windows, rotation.swapaxes(0, 1), source_inverse, table, send_rows)
    args = [pltpu.with_memory_space_constraint(x, pltpu.HBM) for x in args]
    whole = lambda *shape: pl.BlockSpec(shape, lambda i, *_: (0,) * len(shape))
    return pl.pallas_call(
        partial(spectra_kernel, steps),
        grid_spec=pltpu.PrefetchScalarGridSpec(
            num_scalar_prefetch=1,
            grid=(steps,),
            in_specs=[
                pl.BlockSpec((events, comps, stations, length), lambda i, *_: (i, 0, 0, 0)),
                whole(comps, ev_dev, stations),
                whole(ev_dev, length),
                whole(length, length),
                whole(owners, cap),
            ],
            out_specs=[whole(total, length), whole(stations, length // 2)],
        ),
        out_shape=[
            jax.ShapeDtypeStruct((total, length), BF16),
            jax.ShapeDtypeStruct((stations, length // 2), F32),
        ],
        compiler_params=pltpu.CompilerParams(vmem_limit_bytes=SMALL),
        name="spectra",
    )(half, *args)


def pick_rows(index, rows, store):
    peers, cap = index.shape
    lines = LANES // cap
    for first in range(0, peers, lines):
        line = jnp.concatenate([index[first + j : first + j + 1, :] for j in range(lines)], axis=1)
        picked = jnp.dot(one_hot(line, rows.shape[0]), rows, preferred_element_type=F32)
        picked = picked.astype(BF16)
        for j in range(lines):
            store(first + j, picked[j * cap : (j + 1) * cap])


def spread(index, rows, refs, skips):
    def store(peer, picked):
        start = 0
        for ref, skip in zip(refs, skips):
            count = ref.shape[1] - skip
            ref[peer, skip:, :] = picked[start : start + count]
            start += count

    pick_rows(index, rows, store)


def own_kernel(half_ref, rows_ref, index_ref, *send_refs):
    peers = send_refs[0].shape[0]
    mine = pl.multiple_of(half_ref[0] * peers, peers)
    spread(index_ref[pl.ds(mine, peers), :], rows_ref[...], send_refs, (0, 0))


def own_sends(half, rows, send_rows, sizes):
    owners, cap = send_rows.shape
    peers = owners // 2
    length = rows.shape[1]
    whole = lambda *shape: pl.BlockSpec(shape, lambda i, *_: (0,) * len(shape))
    shapes = [(peers, size * SUB, length) for size in sizes]
    return pl.pallas_call(
        own_kernel,
        grid_spec=pltpu.PrefetchScalarGridSpec(
            num_scalar_prefetch=1,
            grid=(1,),
            in_specs=[whole(rows.shape[0] - peers, length), whole(owners, cap)],
            out_specs=[whole(*shape) for shape in shapes],
        ),
        out_shape=[pltpu.HBM(shape, BF16) for shape in shapes],
        compiler_params=pltpu.CompilerParams(vmem_limit_bytes=SMALL),
        name="own",
    )(half, rows, send_rows)


def relay_kernel(cap, me_ref, rows_ref, rest_ref, *refs):
    *first_refs, last_ref, held_ref = refs
    peers, kept, _ = rest_ref.shape
    tail = rows_ref.shape[0] - peers
    digits = rows_ref[tail:, :].astype(F32).astype(jnp.int32)
    index = digits[:, :cap] * LANES + digits[:, LANES : LANES + cap]
    spread(index, rows_ref[:tail, :], (held_ref, last_ref), (0, kept))
    last_ref[:, :kept, :] = rest_ref[...]
    for step, ref in enumerate(first_refs):
        ref[...] = held_ref[me_ref[0] ^ step]


def relay_sends(me, rows, rest, cap):
    peers, kept, length = rest.shape
    shapes = [(cap - kept, length)] * peers + [(peers, 2 * kept, length)]
    vmem = pl.BlockSpec(memory_space=pltpu.VMEM)
    return pl.pallas_call(
        partial(relay_kernel, cap),
        in_specs=[pl.BlockSpec(memory_space=pltpu.SMEM), vmem, vmem],
        out_shape=[jax.ShapeDtypeStruct(shape, BF16) for shape in shapes[:-1]]
        + [pltpu.HBM(shapes[-1], BF16)],
        scratch_shapes=[pltpu.VMEM((peers, cap - kept, length), BF16)],
        compiler_params=pltpu.CompilerParams(vmem_limit_bytes=SMALL),
        name="relay",
    )(me, rows, rest)


def place_kernel(peers, early, half_ref, me_ref, pair_ref, place_ref):
    cap = pair_ref.shape[2]
    pair = pair_ref[...]
    source = lax.div(pair, cap)
    side = lax.div(source, peers) != half_ref[0]
    offset = jnp.where(side, peers * SUB, 0)
    peer = lax.rem(source, peers)
    late = lax.broadcasted_iota(jnp.int32, pair.shape, 2) >= early * SUB
    peer = jnp.where(late | (offset == 0), peer, peer ^ me_ref[0])
    place_ref[...] = offset + peer * SUB + lax.rem(pair, SUB)


def place_rows(half, me, pairs, peers, early):
    smem = pl.BlockSpec(memory_space=pltpu.SMEM)
    return pl.pallas_call(
        partial(place_kernel, peers, early),
        in_specs=[smem, smem, pl.BlockSpec(memory_space=pltpu.VMEM)],
        out_shape=jax.ShapeDtypeStruct(pairs.shape, jnp.int32),
        compiler_params=pltpu.CompilerParams(vmem_limit_bytes=SMALL),
        name="places",
    )(half, me, pairs)


def pair_kernel(geo, first, count, station_ref, count_ref, place_ref, weight_ref, lag_ref, *refs):
    row_refs, out_ref = refs[:count], refs[-1]
    _, cap, joint = geo
    group = pl.program_id(0) + first
    length = row_refs[0].shape[-1]
    half_len = length // 2

    rows = jnp.concatenate([ref[...].reshape(-1, length) for ref in row_refs], axis=0)
    width = rows.shape[0]
    many = TOGETHER * LANES
    for j in range(joint):
        for i in range(0, SUB, TOGETHER):
            picks = [
                one_hot(place_ref[m, j, i + n : i + n + 1, :], width)
                for m in range(2)
                for n in range(TOGETHER)
            ]
            members = jnp.dot(jnp.concatenate(picks, axis=0), rows, preferred_element_type=F32)
            halves = []
            for n in range(TOGETHER):
                a = members[n * LANES : (n + 1) * LANES]
                b = members[many + n * LANES : many + (n + 1) * LANES]
                re_a, im_a = a[:, :half_len], a[:, half_len:]
                re_b, im_b = b[:, :half_len], b[:, half_len:]
                tile = j * cap + group * SUB + i + n
                scale = weight_ref[pl.ds(station_ref[tile], 1), :]
                halves.append(
                    jnp.concatenate(
                        [
                            ((re_a * re_b + im_a * im_b) * scale).astype(BF16),
                            ((im_a * re_b - re_a * im_b) * scale).astype(BF16),
                        ],
                        axis=1,
                    )
                )
            cross = jnp.concatenate(halves, axis=0)
            lagged = jnp.concatenate(
                [
                    jnp.dot(piece, lag_ref[...], preferred_element_type=F32)
                    for piece in (cross[: many // 2], cross[many // 2 :])
                ],
                axis=0,
            )
            for n in range(TOGETHER):
                tile = j * cap + group * SUB + i + n
                piece = lagged[n * LANES : (n + 1) * LANES]
                slot = lax.broadcasted_iota(jnp.int32, piece.shape, 0)
                piece = jnp.where(slot < count_ref[tile], piece, 0.0)
                out_ref[j, (i + n) * LANES : (i + n + 1) * LANES, :] = piece[:, :LAGS]


def correlate(first, steps, sources, geo, stations_of, counts, places, weight, lag_tab, previous):
    peers, cap, joint = geo
    length = sources[0][0].shape[-1]
    in_specs = [
        pl.BlockSpec((2, joint, SUB, LANES), lambda i, *_: (0, 0, i + first, 0)),
        pl.BlockSpec(weight.shape, lambda i, *_: (0, 0)),
        pl.BlockSpec(lag_tab.shape, lambda i, *_: (0, 0)),
    ]
    args = [places, weight, lag_tab]
    for array, at in sources:
        if array.ndim == 3:
            spec = pl.BlockSpec((peers, SUB, length), lambda i, *_, at=at: (0, i + at, 0))
        else:
            spec = pl.BlockSpec((SUB, length), lambda i, *_, at=at: (i + at, 0))
        in_specs.append(spec)
        args.append(array)
    aliases = {}
    if previous is not None:
        in_specs.append(pl.BlockSpec(memory_space=pl.ANY))
        args.append(previous)
        aliases = {len(args) + 1: 0}
    tiles = joint * steps * SUB
    macs = tiles * LANES * length * (2 * 2 * peers * SUB + lag_tab.shape[1])
    return pl.pallas_call(
        partial(pair_kernel, geo, first, len(sources)),
        grid_spec=pltpu.PrefetchScalarGridSpec(
            num_scalar_prefetch=2,
            grid=(steps,),
            in_specs=in_specs,
            out_specs=pl.BlockSpec((joint, SUB * LANES, LAGS), lambda i, *_: (0, i + first, 0)),
        ),
        out_shape=jax.ShapeDtypeStruct((joint, cap * LANES, LAGS), F32),
        input_output_aliases=aliases,
        compiler_params=pltpu.CompilerParams(vmem_limit_bytes=SMALL),
        cost_estimate=pl.CostEstimate(
            flops=2 * macs, bytes_accessed=tiles * LANES * LAGS * 4, transcendentals=0
        ),
        name="pairs",
    )(stations_of, counts, *args)


def pair_up(value, step, owners):
    return lax.ppermute(value, "ev", [(i, i ^ step) for i in range(owners)])


def shards(windows, rotation, source_inverse, send_rows, tile_station, tile_count, pair_rows):
    ev_dev, _, stations, length = windows.shape
    owners = lax.axis_size("ev")
    cap = send_rows.shape[1]
    tiles_dev = tile_station.shape[0]
    joint = tiles_dev // cap
    peers = owners // 2
    half = lax.axis_index("ev") // peers
    halves = [list(range(peers)), list(range(peers, owners))]
    across = [(i, (i + peers) % owners) for i in range(owners)]
    to_peers = partial(
        lax.all_to_all,
        axis_name="ev",
        split_axis=0,
        concat_axis=0,
        axis_index_groups=halves,
        tiled=True,
    )
    half_arg = half.astype(jnp.int32).reshape(1)
    me_arg = (lax.axis_index("ev") % peers).astype(jnp.int32).reshape(1)

    rows, power = event_rows(
        half_arg, windows, rotation, source_inverse, send_rows, spectral_table(length)
    )
    groups = cap // SUB
    early = groups * SPLIT[0] // sum(SPLIT)
    sizes = (early, groups - early)
    swapped = lax.ppermute(rows, "ev", across)
    send, rest = own_sends(half_arg, rows, send_rows, sizes)
    stations = power.shape[0]
    share = stations // 2
    low = lax.axis_index("ev") % 2 == 0
    parts = power[:share], power[share:]
    kept, passed = (jnp.where(low, *parts), jnp.where(low, *parts[::-1]))
    part = kept + pair_up(passed, 1, owners)
    step = 2
    while step < peers:
        part += pair_up(part, step, owners)
        step *= 2
    own = to_peers(send)
    rest = pltpu.with_memory_space_constraint(rest, pltpu.HBM)
    sends = relay_sends(me_arg, swapped, rest, cap)
    part += pair_up(part, peers, owners)
    twin = pair_up(part, 1, owners)
    power = jnp.concatenate([jnp.where(low, part, twin), jnp.where(low, twin, part)], axis=0)
    weight = 1.0 / (power / (ev_dev * owners) + epsilon)
    places = place_rows(half_arg, me_arg, pair_rows.reshape(2, joint, cap, LANES), peers, early)
    lag_tab = lag_table(length, LAGS, LAGS + 1)
    geo = (peers, cap, joint)
    far = list(sends[:peers])
    for step in reversed(range(1, peers)):
        far[step] = pair_up(far[step], step, owners)
    last = to_peers(sends[peers])
    run = partial(correlate, geo=geo, stations_of=tile_station, counts=tile_count, places=places)
    run = partial(run, weight=weight, lag_tab=lag_tab)
    result = run(0, sizes[0], [(own, 0)] + [(array, 0) for array in far], previous=None)
    result = run(early, sizes[1], [(last, 0), (last, sizes[1])], previous=result)
    return result.reshape(tiles_dev * LANES, LAGS)


def solution(mesh):
    in_specs = (
        P(("grp", "ev"), None, None, None),
        P(("grp", "ev"), None, None),
        P(("grp", "ev"), None),
        P(("grp", "ev"), None),
        P(("grp", "ev")),
        P(("grp", "ev")),
        P(None, ("grp", "ev")),
    )
    out_specs = P(("grp", "ev"), None)
    return jax.shard_map(shards, mesh=mesh, in_specs=in_specs, out_specs=out_specs, check_vma=False)
```
